256 devices in a mesh: grp: 2 (over core), gx: 8 (over x_hi, y), gy: 16 (over x_lo, z).
Axes of the slice: x: 4 (x_hi: 2, x_lo: 2; x = x_hi * 2 + x_lo), y: 4, z: 8, core: 2. Of those that a mesh axis runs over, the one named last changes fastest.
Arguments:
- right_side: float32 [128, 256, 256], P('gx', 'gy', 'grp'), may hold values from -6 to 6
- coefficient: float32 [128, 256, 256], P('gx', 'gy', 'grp'), may hold values from 0.2 to 5
Outputs:
- solution_field: float32 [128, 256, 256], P('gx', 'gy', 'grp')
- residual: float32 [128, 256, 256], P('gx', 'gy', 'grp')
The draws below stay inside these ranges and needn't reach their ends.
All inputs are finite; a program needn't handle non-finite values.
Results may differ from the reference program's by a relative error of at most 0.0001.
Values sent between devices are 32-bit elements; how exact they have to be, the bound alone decides.
No kernel may reach another device: no remote copies, remote signals or barrier semaphores. Data moves between devices by JAX's collectives and lax.ppermute only.
A program may use at most 64 MiB of HBM per device.

```python
import math
import jax
import jax.numpy as jnp

FINE_DEGREE = 5
COARSE_DEGREE = 16
OUTER = 2
NX = 128
NY = 256
NZ = 256


def block_levels(rng, dims, split, smallest, top_value):
    def one(position, blocks):
        heights = jax.random.uniform(jax.random.fold_in(jax.random.fold_in(rng, 6), position), (blocks,), jnp.float32, smallest / len(split), top_value / len(split))
        return jnp.repeat(jnp.exp(heights), dims[position] // blocks).reshape((-1,) + (1,) * (len(dims) - position - 1))

    gain = one(*split[0])
    for cut in split[1:]:
        gain = gain * one(*cut)
    return gain


def noise(key, shape, width, limit, split=(), held_as=jnp.bfloat16):
    loudness = block_levels(key, shape, split, -0.22, 0.18) if split else 1.0
    result = jax.random.normal(key, shape, jnp.float32) * width * loudness
    return jnp.minimum(jnp.maximum(result, -limit), limit).astype(held_as)


def setup_inputs(seed: int = 0) -> dict:
    key_of = jax.random.split(jax.random.key(seed), 3)
    right_side = noise(key_of[0], (NX, NY, NZ), 1.0, 6.0, ((0, 8), (1, 16), (2, 2)), jnp.float32)
    coefficient = jnp.clip(jnp.exp(math.log(5.0) - 3.218876 * jax.random.uniform(key_of[1], (NX, NY, NZ), jnp.float32) ** block_levels(key_of[1], (NX, NY, NZ), ((0, 8), (1, 16), (2, 2)), -0.2, 0.2)), 0.2, 5.0)
    return dict(right_side=right_side, coefficient=coefficient)


LOW_FINE = 0.2
LOW_COARSE = 0.02
HIGH_BOUND = 2.0
DAMPING = 0.5


def face_parts(padded):
    center = padded[1:-1, 1:-1, 1:-1]
    return (0.5 * (center + padded[:-2, 1:-1, 1:-1]), 0.5 * (center + padded[2:, 1:-1, 1:-1]),
            0.5 * (center + padded[1:-1, :-2, 1:-1]), 0.5 * (center + padded[1:-1, 2:, 1:-1]),
            0.5 * (center + padded[1:-1, 1:-1, :-2]), 0.5 * (center + padded[1:-1, 1:-1, 2:]))


def diagonal_of(parts):
    return parts[0] + parts[1] + parts[2] + parts[3] + parts[4] + parts[5]


def stencil(padded, parts, scale):
    center = padded[1:-1, 1:-1, 1:-1]
    nearby = parts[0] * padded[:-2, 1:-1, 1:-1] + parts[1] * padded[2:, 1:-1, 1:-1]
    nearby = nearby + parts[2] * padded[1:-1, :-2, 1:-1] + parts[3] * padded[1:-1, 2:, 1:-1]
    nearby = nearby + parts[4] * padded[1:-1, 1:-1, :-2] + parts[5] * padded[1:-1, 1:-1, 2:]
    return scale * (diagonal_of(parts) * center - nearby)


def restrict(field):
    size_a, size_b, size_c = field.shape
    return field.reshape(size_a // 2, 2, size_b // 2, 2, size_c // 2, 2).mean(axis=(1, 3, 5))


def prolong(field):
    return jnp.repeat(jnp.repeat(jnp.repeat(field, 2, 0), 2, 1), 2, 2)


def cheb_steps(degree, low, high):
    theta = (high + low) / 2.0
    delta = (high - low) / 2.0
    sigma = theta / delta
    rho = 1.0 / sigma
    keeps = []
    pushes = []
    for step in range(degree - 1):
        rho_new = 1.0 / (2.0 * sigma - rho)
        keeps.append(rho_new * rho)
        pushes.append(2.0 * rho_new / delta)
        rho = rho_new
    return 1.0 / theta, keeps, pushes


def chebyshev(rhs, inverse_diag, apply_fn, degree, low, high):
    inv_theta, keeps, pushes = cheb_steps(degree, low, high)
    first = inverse_diag * rhs * inv_theta
    resid, update, total = rhs, first, first
    for step in range(degree - 1):
        resid = resid - apply_fn(update)
        update = keeps[step] * update + pushes[step] * (inverse_diag * resid)
        total = total + update
    return total


def reference(right_side, coefficient):
    coefs = [coefficient]
    for level in range(3):
        coefs.append(restrict(coefs[-1]))
    scales = [1.0, 0.25, 0.0625, 0.015625]
    parts_all = [face_parts(jnp.pad(item, 1)) for item in coefs]
    inverses = [1.0 / (scales[level] * diagonal_of(parts_all[level])) for level in range(4)]

    def make_apply(level):
        return lambda field: stencil(jnp.pad(field, 1), parts_all[level], scales[level])

    solution_field = jnp.zeros_like(right_side)
    residual = right_side
    for outer in range(OUTER):
        rhs_list = [residual]
        for level in range(3):
            rhs_list.append(restrict(rhs_list[-1]))
        corrections = []
        for level in range(4):
            if level < 3:
                corrections.append(chebyshev(rhs_list[level], inverses[level], make_apply(level), FINE_DEGREE, LOW_FINE, HIGH_BOUND))
            else:
                corrections.append(chebyshev(rhs_list[level], inverses[level], make_apply(level), COARSE_DEGREE, LOW_COARSE, HIGH_BOUND))
        combined = corrections[2] + prolong(corrections[3])
        combined = corrections[1] + prolong(combined)
        combined = corrections[0] + prolong(combined)
        solution_field = solution_field + DAMPING * combined
        residual = right_side - stencil(jnp.pad(solution_field, 1), parts_all[0], 1.0)
    return solution_field, residual
```

```python
import functools

import jax
import jax.numpy as jnp
from jax import lax
from jax.experimental import pallas as pl
from jax.experimental.pallas import tpu as pltpu
from jax.sharding import PartitionSpec as P

FINE_DEGREE = 5
COARSE_DEGREE = 16
LOW_FINE = 0.2
LOW_COARSE = 0.02
HIGH_BOUND = 2.0
DAMPING = 0.5

F32 = jnp.float32
INTERPRET = False
LANES_X = {1: 1, 2: 2, 3: 4}
BLOCKS = {1: 28, 2: 10, 3: 5}
ROWS = {1: 32, 2: 24, 3: 24}
SCALE = {1: 1.0, 2: 0.25, 3: 0.0625, 4: 0.015625}


def cheb_steps(degree, low, high):
    theta = (high + low) / 2.0
    delta = (high - low) / 2.0
    sigma = theta / delta
    rho = 1.0 / sigma
    keeps = []
    pushes = []
    for step in range(degree - 1):
        rho_new = 1.0 / (2.0 * sigma - rho)
        keeps.append(rho_new * rho)
        pushes.append(2.0 * rho_new / delta)
        rho = rho_new
    return (1.0 / theta, keeps, pushes)


def roll(x, shift, axis):
    size = x.shape[axis]
    return pltpu.roll(x, shift % size, axis)


def lane_iota(shape):
    return lax.broadcasted_iota(jnp.int32, shape, len(shape) - 1)


def dot(x, m):
    return jnp.dot(x, m, precision=lax.Precision.HIGHEST, preferred_element_type=F32)


def select_matrix(fn, value):
    row = lax.broadcasted_iota(jnp.int32, (128, 128), 0)
    col = lax.broadcasted_iota(jnp.int32, (128, 128), 1)
    return jnp.where(fn(row, col), value, 0.0).astype(F32)


def x_up(q, here, after):
    if q == 1:
        return after
    zz = 128 // q
    lane = lane_iota(here.shape)
    return jnp.where(lane < 128 - zz, roll(here, -zz, 2), roll(after, -zz, 2))


def x_dn(q, here, before):
    if q == 1:
        return before
    zz = 128 // q
    lane = lane_iota(here.shape)
    return jnp.where(lane >= zz, roll(here, zz, 2), roll(before, zz, 2))


def z_up(q, v):
    zz = 128 // q
    moved = roll(v, -1, 2)
    wrap = moved if q == 1 else roll(v, zz - 1, 2)
    swapped = jnp.concatenate([wrap[1:], wrap[:1]], axis=0)
    edge = lane_iota(v.shape) % zz == zz - 1
    return jnp.where(edge, swapped, moved)


def z_dn(q, v):
    zz = 128 // q
    moved = roll(v, 1, 2)
    wrap = moved if q == 1 else roll(v, -(zz - 1), 2)
    swapped = jnp.concatenate([wrap[1:], wrap[:1]], axis=0)
    edge = lane_iota(v.shape) % zz == 0
    return jnp.where(edge, swapped, moved)


def faces(level, a, fx, fy, fz, inv, diag_ref):
    q, nb, rows = LANES_X[level], BLOCKS[level], ROWS[level]
    zz = 128 // q
    shape = (2, rows, 128)

    def body(i, _):
        here = a[:, i]
        half = 0.5 * here
        after = a[:, jnp.minimum(i + 1, nb - 1)]
        fxv = half + 0.5 * x_up(q, here, after)
        fx[:, i] = fxv
        fyv = half + 0.5 * roll(here, -1, 1)
        fy[:, i] = fyv
        core = lax.broadcasted_iota(jnp.int32, shape, 0)
        lane = lane_iota(shape) % zz
        top = (core == 1) & (lane == zz - 1)
        bottom = (core == 0) & (lane == 0)
        inner = half + 0.5 * z_up(q, here)
        fzv = jnp.where(top, 0.0, inner)
        fz[:, i] = fzv
        before = fx[:, jnp.maximum(i - 1, 0)]
        total = fxv + x_dn(q, fxv, before) + fyv + roll(fyv, 1, 1)
        total = total + jnp.where(top, half, inner) + jnp.where(bottom, half, z_dn(q, fzv))
        inv[:, i] = jnp.where(here > 0.0, 1.0 / total, 0.0)
        if diag_ref is not None:
            diag_ref[:, i] = total
        return 0

    lax.fori_loop(0, nb, body, 0)


def nearby(q, i, nb, v, fx, fy, fz):
    here = v[:, i]
    before_i = jnp.maximum(i - 1, 0)
    after = v[:, jnp.minimum(i + 1, nb - 1)]
    before = v[:, before_i]
    fxv = fx[:, i]
    fyv = fy[:, i]
    fzv = fz[:, i]
    total = fxv * x_up(q, here, after) + x_dn(q, fxv * here, fx[:, before_i] * before)
    total = total + fyv * roll(here, -1, 1) + roll(fyv * here, 1, 1)
    total = total + fzv * z_up(q, here) + z_dn(q, fzv * here)
    return here, total


def smooth(level, b, fx, fy, fz, inv, e, d, x):
    q, nb = LANES_X[level], BLOCKS[level]
    first, keeps, pushes = cheb_steps(FINE_DEGREE, LOW_FINE, HIGH_BOUND)

    def start(i, _):
        ev = b[:, i] * inv[:, i] * (1.0 / SCALE[level])
        e[:, i] = ev
        d[0, :, i] = ev * first
        x[:, i] = ev * first
        return 0

    lax.fori_loop(0, nb, start, 0)
    for step in range(FINE_DEGREE - 1):
        src, dst = d.at[step % 2], d.at[1 - step % 2]
        margin = step + 1 if level == 1 else 0

        def body(i, _):
            here, near = nearby(q, i, nb, src, fx, fy, fz)
            ev = e[:, i] - here + inv[:, i] * near
            new = keeps[step] * here + pushes[step] * ev
            e[:, i] = ev
            dst[:, i] = new
            x[:, i] = x[:, i] + new
            return 0

        lax.fori_loop(margin, nb - margin, body, 0)


def x_up4(v):
    moved = roll(v, -32, 2)
    after = jnp.concatenate([moved[1:], moved[:1]], axis=0)
    return jnp.where(lane_iota(v.shape) < 96, moved, after)


def x_dn4(v):
    moved = roll(v, 32, 2)
    before = jnp.concatenate([moved[-1:], moved[:-1]], axis=0)
    return jnp.where(lane_iota(v.shape) >= 32, moved, before)


def faces4(a, fx, fy, fz, inv):
    nb, rows, _ = a.shape
    blk = lax.broadcasted_iota(jnp.int32, a.shape, 0)
    row = lax.broadcasted_iota(jnp.int32, a.shape, 1)
    lane = lane_iota(a.shape)
    half = 0.5 * a
    total = jnp.zeros_like(a)
    for up, dn, last, start, out in (
        (x_up4, x_dn4, (blk == nb - 1) & (lane >= 96), (blk == 0) & (lane < 32), fx),
        (lambda v: roll(v, -1, 1), lambda v: roll(v, 1, 1), row == rows - 1, row == 0, fy),
        (lambda v: roll(v, -1, 2), lambda v: roll(v, 1, 2), lane % 32 == 31, lane % 32 == 0, fz),
    ):
        inner = half + 0.5 * up(a)
        off = jnp.where(last, 0.0, inner)
        out[...] = off
        total = total + jnp.where(last, half, inner) + jnp.where(start, half, dn(off))
    inv[...] = 1.0 / total


def smooth4(table, b, fx, fy, fz, inv):
    first = cheb_steps(COARSE_DEGREE, LOW_COARSE, HIGH_BOUND)[0]
    e = b * inv[...] * (1.0 / SCALE[4])
    d = e * first

    def body(step, carry):
        e, d, x = carry
        gx, gy, gz = fx[...], fy[...], fz[...]
        near = gx * x_up4(d) + x_dn4(gx * d)
        near = near + gy * roll(d, -1, 1) + roll(gy * d, 1, 1)
        near = near + gz * roll(d, -1, 2) + roll(gz * d, 1, 2)
        e = e - d + inv[...] * near
        d = table[0, step] * d + table[1, step] * e
        return e, d, x + d

    return lax.fori_loop(0, COARSE_DEGREE - 1, body, (e, d, d))[2]


def build4(src, stride, offset, core, gx_n, gy_n):
    count = gx_n * gy_n * 2
    gap = stride // 2
    pairs = src[pl.ds(offset, count, stride), :] + src[pl.ds(offset + gap, count, stride), :]
    pairs = pairs.reshape(gx_n // 2, 2, gy_n * 2, 128)
    out = None
    for odd in range(2):
        mat = select_matrix(
            lambda r, c: c == odd * 64 + (r // 64) * 32 + core * 16 + (r % 32) // 2, 0.125
        )
        part = dot(pairs[:, odd].reshape(gx_n * gy_n, 128), mat)
        out = part if out is None else out + part
    return out.reshape(gx_n // 2, gy_n * 2, 128)


def window3(src, dst, field, fields, core, pos, gx_n, gy_n):
    for bx in range(5):
        for by in range(6):
            ix = pos[1] + (bx - 2)
            iy = pos[2] + (by - 2)
            ok = (ix >= 0) & (ix < gx_n) & (iy >= 0) & (iy < gy_n)
            at = jnp.clip(ix, 0, gx_n - 1) * gy_n + jnp.clip(iy, 0, gy_n - 1)
            if fields == 1:
                tile = src[at]
            else:
                tile = src[at, pl.ds(field, 4, fields), :]
            dst[core, bx, by * 4:by * 4 + 4, :] = jnp.where(ok, tile, 0.0)


def restrict_to2(read_pair, out):
    even = jnp.concatenate([read_pair(2 * k) for k in range(4)], axis=0)
    odd = jnp.concatenate([read_pair(2 * k + 1) for k in range(4)], axis=0)
    low = select_matrix(lambda r, c: c == r // 2, 0.125)
    high = select_matrix(lambda r, c: c == 64 + r // 2, 0.125)
    both = dot(even, low) + dot(odd, high)
    for k in range(4):
        out(k, both[k * 8:k * 8 + 8])


def restrict_to3(read_rows):
    total = None
    for k in range(4):
        mat = select_matrix(lambda r, c: c == k * 32 + (r % 64) // 2, 0.125)
        part = dot(read_rows(k), mat)
        total = part if total is None else total + part
    return total


def prepare_kernel(a, b, own, up, down, slot):
    for f, src in enumerate((a, b)):
        for t in range(2):
            own[pl.ds(f * 32 + t, 16, 2)] = src[:, t * 8:t * 8 + 8, :]
            up[pl.ds(f * 12 + t, 6, 2)] = src[10:16, t * 8:t * 8 + 8, :]
            down[pl.ds(f * 12 + t, 6, 2)] = src[0:6, t * 8:t * 8 + 8, :]

        def read_pair(k):
            total = None
            for x in (2 * k, 2 * k + 1):
                part = src[x, pl.ds(0, 8, 2), :] + src[x, pl.ds(1, 8, 2), :]
                total = part if total is None else total + part
            return total

        def out(k, value):
            own[64 + f * 4 + k] = value
            if k >= 1:
                up[24 + f * 3 + k - 1] = value
            if k <= 2:
                down[24 + f * 3 + k] = value

        restrict_to2(read_pair, out)
        slot[pl.ds(f, 4, 2), :] = restrict_to3(
            lambda k: own[64 + f * 4 + k, pl.ds(0, 4, 2), :] + own[64 + f * 4 + k, pl.ds(1, 4, 2), :]
        )


def sides_kernel(nf, pos, own, lower, upper, up, down):
    c = pos[0]
    for f in range(nf):
        for out, t in ((up, 1), (down, 0)):
            for i in range(6):
                out[f * 28 + i] = lower[f * 12 + 2 * i + t]
                out[f * 28 + 22 + i] = upper[f * 12 + 2 * i + t]
            for i in range(16):
                out[f * 28 + 6 + i] = own[c, f * 32 + 2 * i + t]
            base = nf * 28 + f * 10
            for i in range(3):
                out[base + i] = lower[nf * 12 + f * 3 + i]
                out[base + 7 + i] = upper[nf * 12 + f * 3 + i]
            for i in range(4):
                out[base + 3 + i] = own[c, nf * 32 + f * 4 + i]


def spread(nf, f, core, own, xm, xp, ym, yp, fine, mid):
    for i in range(28):
        fine[core, i, 0:8, :] = ym[f * 28 + i]
        fine[core, i, 24:32, :] = yp[f * 28 + i]
        for t in range(2):
            if i < 6:
                tile = xm[f * 12 + 2 * i + t]
            elif i >= 22:
                tile = xp[f * 12 + 2 * (i - 22) + t]
            else:
                tile = own[f * 32 + 2 * (i - 6) + t]
            fine[core, i, 8 + 8 * t:16 + 8 * t, :] = tile
    base = nf * 28 + f * 10
    for i in range(10):
        mid[core, i, 0:8, :] = ym[base + i]
        mid[core, i, 16:24, :] = yp[base + i]
        if i < 3:
            tile = xm[nf * 12 + f * 3 + i]
        elif i >= 7:
            tile = xp[nf * 12 + f * 3 + i - 7]
        else:
            tile = own[nf * 32 + f * 4 + i - 3]
        mid[core, i, 8:16, :] = tile


def combine(pos, gx_n, gy_n, x4, x3, x2, tmp3, tmp2):
    gx, gy = pos[1], pos[2]
    yrow = lax.broadcasted_iota(jnp.int32, (24, gy_n * 2), 0)
    ycol = lax.broadcasted_iota(jnp.int32, (24, gy_n * 2), 1)
    rows = jnp.where(ycol == (4 * gy - 8 + yrow + 1024) // 2 - 512, 1.0, 0.0).astype(F32)
    for bx in (1, 2, 3):
        ix = gx + (bx - 2)
        ok = (ix >= 0) & (ix < gx_n)
        at = jnp.clip(ix, 0, gx_n - 1)
        odd = lax.rem(at, 2)
        spread_rows = dot(rows, x4[lax.div(at, 2)])
        for c in range(2):
            mat = select_matrix(
                lambda r, k: r == odd * 64 + (k // 64) * 32 + c * 16 + (k % 32) // 2, 1.0
            )
            part = jnp.where(ok, dot(spread_rows, mat), 0.0)
            x3[c, bx] = x3[c, bx] + part
    for c in range(2):
        for bx in (1, 2, 3):
            tmp3[c, bx, pl.ds(0, 12, 2), :] = x3[c, bx, 4:16, :]
            tmp3[c, bx, pl.ds(1, 12, 2), :] = x3[c, bx, 4:16, :]
    for low in range(4):
        blocks = [i for i in range(2, 8) if (i + 5) % 4 == low]
        mat = select_matrix(lambda r, k: r == low * 32 + (k % 64) // 2, 1.0)
        for i in blocks:
            bx = (i + 5) // 4
            part = dot(tmp3[:, bx].reshape(48, 128), mat).reshape(2, 24, 128)
            x2[:, i] = x2[:, i] + part
    for low in range(2):
        mat = select_matrix(lambda r, k: r == low * 64 + k // 2, 1.0)
        part = dot(x2[:, 2:8].reshape(2 * 6 * 24, 128), mat).reshape(2, 6, 24, 128)
        for i in range(6):
            piece = part[:, i, 4:20, :]
            tmp2[:, 2 * i + low, pl.ds(0, 16, 2), :] = piece
            tmp2[:, 2 * i + low, pl.ds(1, 16, 2), :] = piece


def first_kernel(
    gx_n, gy_n, pos, table,
    own_a, xm_a, xp_a, ym_a, yp_a, own_b, xm_b, xp_b, ym_b, yp_b,
    r3_a, r3_b, r3f_a, r3f_b,
    fx1, fy1, fz1, inv1, diag1, fx2, fy2, fz2, inv2, fx3, fy3, fz3, inv3, fx4, fy4, fz4, inv4,
    x1, right, own, up, down, slot,
    a1, b1, e1, d1, a2, b2, e2, d2, c2, a3, b3, e3, d3, c3, x4, tmp3, tmp2, rest,
):
    core = pos[0]
    mine = ((core, own_a, xm_a, xp_a, ym_a, yp_a), (1 - core, own_b, xm_b, xp_b, ym_b, yp_b))
    for c, *parts in mine:
        spread(2, 0, c, *parts, a1, a2)
        spread(2, 1, c, *parts, b1, b2)
    for c, src in ((core, r3_a), (1 - core, r3_b)):
        window3(src, a3, 0, 2, c, pos, gx_n, gy_n)
        window3(src, b3, 1, 2, c, pos, gx_n, gy_n)
    a4 = build4(r3f_a, 4, 0, core, gx_n, gy_n) + build4(r3f_b, 4, 0, 1 - core, gx_n, gy_n)
    b4 = build4(r3f_a, 4, 1, core, gx_n, gy_n) + build4(r3f_b, 4, 1, 1 - core, gx_n, gy_n)
    faces4(a4, fx4, fy4, fz4, inv4)
    faces(1, a1, fx1, fy1, fz1, inv1, diag1)
    faces(2, a2, fx2, fy2, fz2, inv2, None)
    faces(3, a3, fx3, fy3, fz3, inv3, None)
    x4[...] = smooth4(table, b4, fx4, fy4, fz4, inv4)
    smooth(3, b3, fx3, fy3, fz3, inv3, e3, d3, c3)
    smooth(2, b2, fx2, fy2, fz2, inv2, e2, d2, c2)
    smooth(1, b1, fx1, fy1, fz1, inv1, e1, d1, x1)
    combine(pos, gx_n, gy_n, x4, c3, c2, tmp3, tmp2)

    def finish(i, _):
        x1[:, i] = DAMPING * (x1[:, i] + tmp2[:, i // 2 - 1])
        return 0

    lax.fori_loop(4, 24, finish, 0)

    def residual(i, _):
        here, near = nearby(1, i + 6, 28, x1, fx1, fy1, fz1)
        bv = b1[:, i + 6]
        right[:, i] = bv[:, 8:24, :]
        res = bv - (diag1[:, i + 6] * here - near)
        rest[:, i] = res[:, 8:24, :]
        return 0

    lax.fori_loop(0, 16, residual, 0)
    for c in range(2):
        for t in range(2):
            own[c, pl.ds(t, 16, 2)] = rest[c, :, t * 8:t * 8 + 8, :]

        def read_pair(k):
            total = None
            for x in (2 * k, 2 * k + 1):
                part = rest[c, x, pl.ds(0, 8, 2), :] + rest[c, x, pl.ds(1, 8, 2), :]
                total = part if total is None else total + part
            return total

        def out(k, value):
            own[c, 32 + k] = value

        restrict_to2(read_pair, out)
    for i in range(6):
        for t in range(2):
            up[2 * i + t] = own[core, 2 * (10 + i) + t]
            down[2 * i + t] = own[core, 2 * i + t]
    for i in range(3):
        up[12 + i] = own[core, 33 + i]
        down[12 + i] = own[core, 32 + i]
    slot[...] = restrict_to3(
        lambda k: own[core, 32 + k, pl.ds(0, 4, 2), :] + own[core, 32 + k, pl.ds(1, 4, 2), :]
    )


def second_kernel(
    gx_n, gy_n, pos, table,
    own, xm_a, xp_a, ym_a, yp_a, xm_b, xp_b, ym_b, yp_b, r3_a, r3_b, r3f_a, r3f_b,
    fx1, fy1, fz1, inv1, diag1, fx2, fy2, fz2, inv2, fx3, fy3, fz3, inv3, fx4, fy4, fz4, inv4,
    x1, right, out_x, out_r,
    b1, e1, d1, c1, b2, e2, d2, c2, b3, e3, d3, c3, x4, tmp3, tmp2, rest,
):
    core = pos[0]
    spread(1, 0, core, own.at[core], xm_a, xp_a, ym_a, yp_a, b1, b2)
    spread(1, 0, 1 - core, own.at[1 - core], xm_b, xp_b, ym_b, yp_b, b1, b2)
    window3(r3_a, b3, 0, 1, core, pos, gx_n, gy_n)
    window3(r3_b, b3, 0, 1, 1 - core, pos, gx_n, gy_n)
    b4 = build4(r3f_a, 2, 0, core, gx_n, gy_n) + build4(r3f_b, 2, 0, 1 - core, gx_n, gy_n)
    x4[...] = smooth4(table, b4, fx4, fy4, fz4, inv4)
    smooth(3, b3, fx3, fy3, fz3, inv3, e3, d3, c3)
    smooth(2, b2, fx2, fy2, fz2, inv2, e2, d2, c2)
    smooth(1, b1, fx1, fy1, fz1, inv1, e1, d1, c1)
    combine(pos, gx_n, gy_n, x4, c3, c2, tmp3, tmp2)

    def finish(i, _):
        c1[:, i] = x1[:, i] + DAMPING * (c1[:, i] + tmp2[:, i // 2 - 1])
        return 0

    lax.fori_loop(4, 24, finish, 0)

    def residual(i, _):
        here, near = nearby(1, i + 6, 28, c1, fx1, fy1, fz1)
        res = diag1[:, i + 6] * here - near
        rest[:, i] = right[:, i] - res[:, 8:24, :]
        return 0

    lax.fori_loop(0, 16, residual, 0)
    out_r[...] = rest[core]
    out_x[...] = c1[core, 6:22, 8:24, :]


def call(kernel, outs, scratch, *args):
    smem = pl.BlockSpec(memory_space=pltpu.SMEM)
    vmem = pl.BlockSpec(memory_space=pltpu.VMEM)
    return pl.pallas_call(
        kernel,
        out_shape=[jax.ShapeDtypeStruct(s, F32) for s in outs],
        in_specs=[smem if a.ndim < 3 and a.shape[-1] != 128 else vmem for a in args],
        out_specs=[vmem for _ in outs],
        scratch_shapes=[pltpu.VMEM(s, F32) for s in scratch],
        compiler_params=pltpu.CompilerParams(vmem_limit_bytes=56 * 1024 * 1024),
        interpret=INTERPRET,
    )(*args)


def shift(x, axis, step):
    size = lax.axis_size(axis)
    return lax.ppermute(x, axis, [(i, i + step) for i in range(size) if 0 <= i + step < size])


def swap(x):
    return lax.ppermute(x, "grp", [(0, 1), (1, 0)])


def everywhere(slot):
    gx_n, gy_n = lax.axis_size("gx"), lax.axis_size("gy")
    copies = jnp.broadcast_to(slot[None], (gx_n * gy_n,) + slot.shape)
    return lax.all_to_all(copies, ("gx", "gy"), 0, 0, tiled=True)


def on_device(right_side, coefficient):
    gx_n, gy_n = lax.axis_size("gx"), lax.axis_size("gy")
    pos = jnp.stack([lax.axis_index("grp"), lax.axis_index("gx"), lax.axis_index("gy")])
    pos = pos.astype(jnp.int32)
    _, keeps, pushes = cheb_steps(COARSE_DEGREE, LOW_COARSE, HIGH_BOUND)
    table = jnp.array([keeps, pushes], F32)

    own, up, down, slot = call(
        prepare_kernel, [(72, 8, 128), (30, 8, 128), (30, 8, 128), (8, 128)], [],
        coefficient, right_side,
    )
    own_o = swap(own)
    xm, xp = shift(up, "gx", 1), shift(down, "gx", -1)
    r3 = everywhere(slot)
    xm_o, xp_o = swap(xm), swap(xp)
    r3_o = swap(r3)
    zero = pos * 0
    up, down = call(
        functools.partial(sides_kernel, 2), [(76, 8, 128)] * 2, [], zero, own[None], xm, xp
    )
    ym, yp = shift(up, "gy", 1), shift(down, "gy", -1)
    ym_o, yp_o = swap(ym), swap(yp)

    s1, s2, s3 = (2, 28, 32, 128), (2, 10, 24, 128), (2, 5, 24, 128)
    s4 = (gx_n // 2, gy_n * 2, 128)
    coarse = (gx_n * gy_n * 8, 128)
    outs = [s1] * 5 + [s2] * 4 + [s3] * 4 + [s4] * 4
    outs += [s1, (2, 16, 16, 128), (2, 36, 8, 128), (15, 8, 128), (15, 8, 128), (4, 128)]
    *coefs, x1, right, own, up, down, slot = call(
        functools.partial(first_kernel, gx_n, gy_n), outs,
        [s1, s1, s1, (2,) + s1, s2, s2, s2, (2,) + s2, s2, s3, s3, s3, (2,) + s3, s3,
         s4, s3, (2, 12, 32, 128), (2, 16, 16, 128)],
        pos, table, own, xm, xp, ym, yp, own_o, xm_o, xp_o, ym_o, yp_o,
        r3, r3_o, r3.reshape(coarse), r3_o.reshape(coarse),
    )
    xm, xp = shift(up, "gx", 1), shift(down, "gx", -1)
    r3 = everywhere(slot)
    xm_o, xp_o = swap(xm), swap(xp)
    r3_o = swap(r3)
    up, down = call(
        functools.partial(sides_kernel, 1), [(38, 8, 128)] * 2, [], pos, own, xm, xp
    )
    ym, yp = shift(up, "gy", 1), shift(down, "gy", -1)
    ym_o, yp_o = swap(ym), swap(yp)
    coarse = (gx_n * gy_n * 4, 128)
    solution_field, residual = call(
        functools.partial(second_kernel, gx_n, gy_n), [(16, 16, 128)] * 2,
        [s1, s1, (2,) + s1, s1, s2, s2, (2,) + s2, s2, s3, s3, (2,) + s3, s3,
         s4, s3, (2, 12, 32, 128), (2, 16, 16, 128)],
        pos, table, own, xm, xp, ym, yp, xm_o, xp_o, ym_o, yp_o,
        r3, r3_o, r3.reshape(coarse), r3_o.reshape(coarse), *coefs, x1, right,
    )
    return solution_field, residual


def solution(mesh):
    placed = P("gx", "gy", "grp")
    return jax.shard_map(
        on_device, mesh=mesh, in_specs=(placed, placed), out_specs=(placed, placed),
        check_vma=False,
    )
```

```python
import functools

import jax
import jax.numpy as jnp
from jax import lax
from jax.experimental import pallas as pl
from jax.experimental.pallas import tpu as pltpu
from jax.sharding import PartitionSpec as P

FINE_DEGREE = 5
COARSE_DEGREE = 16
LOW_FINE = 0.2
LOW_COARSE = 0.02
HIGH_BOUND = 2.0
DAMPING = 0.5

F32 = jnp.float32
INTERPRET = False
LANES_X = {1: 1, 2: 2, 3: 4}
ROWS = {1: 32, 2: 24, 3: 24}
HELD = {1: (1, 27), 2: (0, 10), 3: (0, 5)}
STEPS = {
    1: ((2, 26), (3, 25), (4, 24), (5, 23)),
    2: ((1, 9), (1, 9), (2, 8), (2, 8)),
    3: ((1, 4),) * 4,
}
CHUNK = {1: 2, 2: 2, 3: 3}
PAD = {1: 0, 2: 1, 3: 1}
SCALE = {1: 1.0, 2: 0.25, 3: 0.0625, 4: 0.015625}


def cheb_steps(degree, low, high):
    theta = (high + low) / 2.0
    delta = (high - low) / 2.0
    sigma = theta / delta
    rho = 1.0 / sigma
    keeps = []
    pushes = []
    for step in range(degree - 1):
        rho_new = 1.0 / (2.0 * sigma - rho)
        keeps.append(rho_new * rho)
        pushes.append(2.0 * rho_new / delta)
        rho = rho_new
    return (1.0 / theta, keeps, pushes)


def roll(x, shift, axis):
    size = x.shape[axis]
    return pltpu.roll(x, shift % size, axis)


def lane_iota(shape):
    return lax.broadcasted_iota(jnp.int32, shape, len(shape) - 1)


def dot(x, m):
    high = x.astype(jnp.bfloat16)
    rest = x - high.astype(F32)
    mid = rest.astype(jnp.bfloat16)
    low = (rest - mid.astype(F32)).astype(jnp.bfloat16)
    m = m.astype(jnp.bfloat16)
    mul = lambda v: jnp.dot(v, m, preferred_element_type=F32)
    return mul(high) + (mul(mid) + mul(low))


def select_matrix(fn, value):
    row = lax.broadcasted_iota(jnp.int32, (128, 128), 0)
    col = lax.broadcasted_iota(jnp.int32, (128, 128), 1)
    return jnp.where(fn(row, col), value, 0.0).astype(F32)


def neighbours(q, v):
    zz = 128 // q
    mid = v[:, 1:-1]
    lane = lane_iota(mid.shape)
    if q == 1:
        x_up, x_dn = v[:, 2:], v[:, :-2]
        for_up = for_dn = mid
    else:
        ups = roll(v[:, 1:], -zz, 3)
        dns = roll(v[:, :-1], zz, 3)
        x_up = jnp.where(lane < 128 - zz, ups[:, :-1], ups[:, 1:])
        x_dn = jnp.where(lane >= zz, dns[:, 1:], dns[:, :-1])
        for_up, for_dn = dns[:, 1:], ups[:, :-1]
    other = lambda w: jnp.concatenate([w[1:], w[:1]], axis=0)
    inner = lane % zz
    z_up = roll(jnp.where(inner == 0, other(for_up), mid), -1, 3)
    z_dn = roll(jnp.where(inner == zz - 1, other(for_dn), mid), 1, 3)
    return mid, (x_up, x_dn, roll(mid, -1, 2), roll(mid, 1, 2), z_up, z_dn)


def blocks(start, stop, step, body):
    if stop - start == step:
        body(start)
        return

    def run(n, _):
        body(start + n * step)
        return 0

    lax.fori_loop(0, (stop - start) // step, run, 0)


def faces(level, a, weights, inv, diag_ref):
    q, pad = LANES_X[level], PAD[level]
    zz = 128 // q
    first, last = HELD[level]
    step = 5 if level == 3 else 2

    def body(i):
        mid, near = neighbours(q, a[:, pl.ds(i + pad - 1, step + 2)])
        core = lax.broadcasted_iota(jnp.int32, mid.shape, 0)
        lane = lane_iota(mid.shape) % zz
        top = (core == 1) & (lane == zz - 1)
        bottom = (core == 0) & (lane == 0)
        x_up, x_dn, y_up, y_dn, z_up, z_dn = near
        z_up = jnp.where(top, 0.0, z_up)
        z_dn = jnp.where(bottom, 0.0, z_dn)
        near = (x_up, x_dn, y_up, y_dn, z_up, z_dn)
        total = 3.0 * mid + 0.5 * ((x_up + x_dn) + (y_up + y_dn) + (z_up + z_dn))
        inverse = jnp.where(mid > 0.0, 1.0 / total, 0.0)
        at = pl.ds(i, step)
        inv[:, at] = inverse
        half = 0.5 * inverse
        for k in range(6):
            w = half * (mid + near[k])
            if k == 4:
                w = jnp.where(top, 0.0, w)
            if k == 5:
                w = jnp.where(bottom, 0.0, w)
            weights[k][:, at] = w
        if diag_ref is not None:
            diag_ref[:, at] = total

    blocks(first, last, step, body)


def weighted(q, i, step, v, weights):
    mid, near = neighbours(q, v[:, pl.ds(i - 1, step + 2)])
    at = pl.ds(i, step)
    terms = [weights[k][:, at] * near[k] for k in range(6)]
    return mid, (terms[0] + terms[1]) + (terms[2] + terms[3]) + (terms[4] + terms[5])


def smooth(level, b, weights, inv, e, d, other, x):
    q = LANES_X[level]
    first, keeps, pushes = cheb_steps(FINE_DEGREE, LOW_FINE, HIGH_BOUND)
    step = CHUNK[level]

    def start(i):
        at = pl.ds(i, 5 if level == 3 else 2)
        ev = b[:, at] * inv[:, at] * (1.0 / SCALE[level])
        e[:, at] = ev
        d[:, at] = ev * first
        x[:, at] = ev * first

    blocks(*HELD[level], 5 if level == 3 else 2, start)
    for n in range(FINE_DEGREE - 1):
        src, dst = (d, other) if n % 2 == 0 else (other, d)

        def body(i):
            at = pl.ds(i, step)
            mid, near = weighted(q, i, step, src, weights)
            ev = (e[:, at] - mid) + near
            new = keeps[n] * mid + pushes[n] * ev
            x[:, at] = x[:, at] + new
            if n < FINE_DEGREE - 2:
                e[:, at] = ev
                dst[:, at] = new

        blocks(*STEPS[level][n], step, body)


def x_up4(v):
    moved = roll(v, -32, 2)
    after = jnp.concatenate([moved[1:], moved[:1]], axis=0)
    return jnp.where(lane_iota(v.shape) < 96, moved, after)


def x_dn4(v):
    moved = roll(v, 32, 2)
    before = jnp.concatenate([moved[-1:], moved[:-1]], axis=0)
    return jnp.where(lane_iota(v.shape) >= 32, moved, before)


def faces4(a, fx, fy, fz, inv):
    nb, rows, _ = a.shape
    blk = lax.broadcasted_iota(jnp.int32, a.shape, 0)
    row = lax.broadcasted_iota(jnp.int32, a.shape, 1)
    lane = lane_iota(a.shape)
    half = 0.5 * a
    total = jnp.zeros_like(a)
    for up, dn, last, start, out in (
        (x_up4, x_dn4, (blk == nb - 1) & (lane >= 96), (blk == 0) & (lane < 32), fx),
        (lambda v: roll(v, -1, 1), lambda v: roll(v, 1, 1), row == rows - 1, row == 0, fy),
        (lambda v: roll(v, -1, 2), lambda v: roll(v, 1, 2), lane % 32 == 31, lane % 32 == 0, fz),
    ):
        inner = half + 0.5 * up(a)
        off = jnp.where(last, 0.0, inner)
        out[...] = off
        total = total + jnp.where(last, half, inner) + jnp.where(start, half, dn(off))
    inv[...] = 1.0 / total


def smooth4(table, b, fx, fy, fz, inv):
    first = cheb_steps(COARSE_DEGREE, LOW_COARSE, HIGH_BOUND)[0]
    e = b * inv[...] * (1.0 / SCALE[4])
    d = e * first

    def body(step, carry):
        e, d, x = carry
        gx, gy, gz = fx[...], fy[...], fz[...]
        near = gx * x_up4(d) + x_dn4(gx * d)
        near = near + gy * roll(d, -1, 1) + roll(gy * d, 1, 1)
        near = near + gz * roll(d, -1, 2) + roll(gz * d, 1, 2)
        e = e - d + inv[...] * near
        d = table[0, step] * d + table[1, step] * e
        return e, d, x + d

    return lax.fori_loop(0, COARSE_DEGREE - 1, body, (e, d, d))[2]


def build4(src, stride, offset, core, gx_n, gy_n):
    count = gx_n * gy_n * 2
    gap = stride // 2
    pairs = src[pl.ds(offset, count, stride), :] + src[pl.ds(offset + gap, count, stride), :]
    pairs = pairs.reshape(gx_n // 2, 2, gy_n * 2, 128)
    out = None
    for odd in range(2):
        mat = select_matrix(
            lambda r, c: c == odd * 64 + (r // 64) * 32 + core * 16 + (r % 32) // 2, 0.125
        )
        part = dot(pairs[:, odd].reshape(gx_n * gy_n, 128), mat)
        out = part if out is None else out + part
    return out.reshape(gx_n // 2, gy_n * 2, 128)


def window3(src, dst, field, fields, core, pos, gx_n, gy_n, pad):
    for bx in range(5):
        for by in range(6):
            ix = pos[1] + (bx - 2)
            iy = pos[2] + (by - 2)
            ok = (ix >= 0) & (ix < gx_n) & (iy >= 0) & (iy < gy_n)
            at = jnp.clip(ix, 0, gx_n - 1) * gy_n + jnp.clip(iy, 0, gy_n - 1)
            if fields == 1:
                tile = src[at]
            else:
                tile = src[at, pl.ds(field, 4, fields), :]
            dst[core, bx + pad, by * 4:by * 4 + 4, :] = jnp.where(ok, tile, 0.0)


def restrict_to2(read_pair, out):
    even = jnp.concatenate([read_pair(2 * k) for k in range(4)], axis=0)
    odd = jnp.concatenate([read_pair(2 * k + 1) for k in range(4)], axis=0)
    low = select_matrix(lambda r, c: c == r // 2, 0.125)
    high = select_matrix(lambda r, c: c == 64 + r // 2, 0.125)
    both = dot(even, low) + dot(odd, high)
    for k in range(4):
        out(k, both[k * 8:k * 8 + 8])


def restrict_to3(read_rows):
    total = None
    for k in range(4):
        mat = select_matrix(lambda r, c: c == k * 32 + (r % 64) // 2, 0.125)
        part = dot(read_rows(k), mat)
        total = part if total is None else total + part
    return total


def position():
    return tuple(lax.axis_index(name) for name in ("grp", "gx", "gy"))


def put_pair(even, first, second, at, up, down):
    first[at] = jnp.where(even, up, down)
    second[at] = jnp.where(even, down, up)


def is_even(index):
    return lax.rem(index, 2) == 0


def prepare_kernel(a, b, own, first, second, slots):
    even = is_even(position()[1])
    slot = None
    for f, src in enumerate((a, b)):
        for t in range(2):
            own[pl.ds(f * 32 + t, 16, 2)] = src[:, t * 8:t * 8 + 8, :]
            put_pair(
                even, first, second, pl.ds(f * 12 + t, 6, 2),
                src[10:16, t * 8:t * 8 + 8, :], src[0:6, t * 8:t * 8 + 8, :],
            )

        def read_pair(k):
            total = None
            for x in (2 * k, 2 * k + 1):
                part = src[x, pl.ds(0, 8, 2), :] + src[x, pl.ds(1, 8, 2), :]
                total = part if total is None else total + part
            return total

        values = []

        def out(k, value):
            own[64 + f * 4 + k] = value
            values.append(value)

        restrict_to2(read_pair, out)
        for k in range(3):
            put_pair(even, first, second, 24 + f * 3 + k, values[k + 1], values[k])
        slots[0, pl.ds(f, 4, 2), :] = restrict_to3(
            lambda k: own[64 + f * 4 + k, pl.ds(0, 4, 2), :] + own[64 + f * 4 + k, pl.ds(1, 4, 2), :]
        )
    slots[1:] = jnp.broadcast_to(slots[0:1], (slots.shape[0] - 1, 8, 128))


def sides_kernel(nf, own, one, two, first, second):
    core, gx, gy = position()
    even_x, even_y = is_even(gx), is_even(gy)
    if nf == 2:
        mine = lambda i: own[i]
    else:
        mine = lambda i: own[core, i]

    def lower(i):
        return jnp.where(even_x, two[i], one[i])

    def upper(i):
        return jnp.where(even_x, one[i], two[i])

    for f in range(nf):
        for i in range(28):
            if i < 6:
                low, high = lower(f * 12 + 2 * i), lower(f * 12 + 2 * i + 1)
            elif i >= 22:
                low, high = upper(f * 12 + 2 * (i - 22)), upper(f * 12 + 2 * (i - 22) + 1)
            else:
                low, high = mine(f * 32 + 2 * (i - 6)), mine(f * 32 + 2 * (i - 6) + 1)
            put_pair(even_y, first, second, f * 28 + i, high, low)
        for i in range(10):
            if i < 3:
                tile = lower(nf * 12 + f * 3 + i)
            elif i >= 7:
                tile = upper(nf * 12 + f * 3 + i - 7)
            else:
                tile = mine(nf * 32 + f * 4 + i - 3)
            first[nf * 28 + f * 10 + i] = tile
            second[nf * 28 + f * 10 + i] = tile


def spread(nf, f, core, even_x, even_y, own, x_one, x_two, y_one, y_two, fine, mid, pad):
    lower = lambda i: jnp.where(even_x, x_two[i], x_one[i])
    upper = lambda i: jnp.where(even_x, x_one[i], x_two[i])
    below = lambda i: jnp.where(even_y, y_two[i], y_one[i])
    above = lambda i: jnp.where(even_y, y_one[i], y_two[i])
    for i in range(28):
        fine[core, i, 0:8, :] = below(f * 28 + i)
        fine[core, i, 24:32, :] = above(f * 28 + i)
        for t in range(2):
            if i < 6:
                tile = lower(f * 12 + 2 * i + t)
            elif i >= 22:
                tile = upper(f * 12 + 2 * (i - 22) + t)
            else:
                tile = own[f * 32 + 2 * (i - 6) + t]
            fine[core, i, 8 + 8 * t:16 + 8 * t, :] = tile
    base = nf * 28 + f * 10
    for i in range(10):
        mid[core, i + pad, 0:8, :] = below(base + i)
        mid[core, i + pad, 16:24, :] = above(base + i)
        if i < 3:
            tile = lower(nf * 12 + f * 3 + i)
        elif i >= 7:
            tile = upper(nf * 12 + f * 3 + i - 7)
        else:
            tile = own[nf * 32 + f * 4 + i - 3]
        mid[core, i + pad, 8:16, :] = tile


def add_coarsest(pos, gx_n, gy_n, x4, x3, out):
    gx, gy = pos[1], pos[2]
    yrow = lax.broadcasted_iota(jnp.int32, (24, gy_n * 2), 0)
    ycol = lax.broadcasted_iota(jnp.int32, (24, gy_n * 2), 1)
    rows = jnp.where(ycol == (4 * gy - 8 + yrow + 1024) // 2 - 512, 1.0, 0.0).astype(F32)
    for bx in (1, 2, 3):
        ix = gx + (bx - 2)
        ok = (ix >= 0) & (ix < gx_n)
        at = jnp.clip(ix, 0, gx_n - 1)
        odd = lax.rem(at, 2)
        picked = select_rows(rows, x4[lax.div(at, 2)])
        for c in range(2):
            mat = select_matrix(
                lambda r, k: r == odd * 64 + (k // 64) * 32 + c * 16 + (k % 32) // 2, 1.0
            )
            out[c, bx - 1] = x3[c, bx] + jnp.where(ok, dot(picked, mat), 0.0)


def select_rows(rows, v):
    high = v.astype(jnp.bfloat16)
    rest = v - high.astype(F32)
    mid = rest.astype(jnp.bfloat16)
    low = (rest - mid.astype(F32)).astype(jnp.bfloat16)
    rows = rows.astype(jnp.bfloat16)
    mul = lambda w: jnp.dot(rows, w, preferred_element_type=F32)
    return mul(high) + (mul(mid) + mul(low))


def combine(sum3, x2, tmp3, tmp2):
    for c in range(2):
        for bx in range(3):
            tmp3[c, bx, pl.ds(0, 12, 2), :] = sum3[c, bx, 4:16, :]
            tmp3[c, bx, pl.ds(1, 12, 2), :] = sum3[c, bx, 4:16, :]
    for low in range(4):
        mat = select_matrix(lambda r, k: r == low * 32 + (k % 64) // 2, 1.0)
        for i in [i for i in range(2, 8) if (i + 5) % 4 == low]:
            bx = (i + 5) // 4 - 1
            part = dot(tmp3[:, bx].reshape(48, 128), mat).reshape(2, 24, 128)
            x2[:, i] = x2[:, i] + part
    for low in range(2):
        mat = select_matrix(lambda r, k: r == low * 64 + k // 2, 1.0)
        part = dot(x2[:, 2:8].reshape(2 * 6 * 24, 128), mat).reshape(2, 6, 24, 128)
        for i in range(6):
            piece = part[:, i, 4:20, :]
            tmp2[:, 2 * i + low, pl.ds(0, 16, 2), :] = piece
            tmp2[:, 2 * i + low, pl.ds(1, 16, 2), :] = piece


def coarse_kernel(gx_n, gy_n, build, table, r3_a, r3_b, r3f_a, r3f_b, *refs):
    pos = position()
    core = pos[0]
    *weights3, inv3, fx4, fy4, fz4, inv4 = refs[:11]
    if build:
        sum3, a3, b3, e3, d3, o3, c3, x4 = refs[11:]
        for c in range(2):
            a3[c, 0] = jnp.zeros((24, 128), F32)
            a3[c, 6] = jnp.zeros((24, 128), F32)
        for c, src in ((core, r3_a), (1 - core, r3_b)):
            window3(src, a3, 0, 2, c, pos, gx_n, gy_n, 1)
            window3(src, b3, 1, 2, c, pos, gx_n, gy_n, 0)
        a4 = build4(r3f_a, 4, 0, core, gx_n, gy_n) + build4(r3f_b, 4, 0, 1 - core, gx_n, gy_n)
        b4 = build4(r3f_a, 4, 1, core, gx_n, gy_n) + build4(r3f_b, 4, 1, 1 - core, gx_n, gy_n)
        faces4(a4, fx4, fy4, fz4, inv4)
        faces(3, a3, weights3, inv3, None)
    else:
        sum3, b3, e3, d3, o3, c3, x4 = refs[11:]
        window3(r3_a, b3, 0, 1, core, pos, gx_n, gy_n, 0)
        window3(r3_b, b3, 0, 1, 1 - core, pos, gx_n, gy_n, 0)
        b4 = build4(r3f_a, 2, 0, core, gx_n, gy_n) + build4(r3f_b, 2, 0, 1 - core, gx_n, gy_n)
    x4[...] = smooth4(table, b4, fx4, fy4, fz4, inv4)
    smooth(3, b3, weights3, inv3, e3, d3, o3, c3)
    add_coarsest(pos, gx_n, gy_n, x4, c3, sum3)


def first_kernel(*refs):
    core, gx, gy = position()
    halves = ((core, refs[:5]), (1 - core, refs[5:10]))
    sum3 = refs[10]
    weights1, inv1, diag1 = refs[11:17], refs[17], refs[18]
    weights2, inv2 = refs[19:25], refs[25]
    x1, right, own, first, second, slots = refs[26:32]
    a1, b1, e1, d1, o1, a2, b2, e2, d2, o2, c2, tmp3, tmp2, rest = refs[32:]
    even_x, even_y = is_even(gx), is_even(gy)
    for c in range(2):
        a2[c, 0] = jnp.zeros((24, 128), F32)
        a2[c, 11] = jnp.zeros((24, 128), F32)
    for c, parts in halves:
        spread(2, 0, c, even_x, even_y, *parts, a1, a2, 1)
        spread(2, 1, c, even_x, even_y, *parts, b1, b2, 0)
    faces(1, a1, weights1, inv1, diag1)
    faces(2, a2, weights2, inv2, None)
    smooth(2, b2, weights2, inv2, e2, d2, o2, c2)
    smooth(1, b1, weights1, inv1, e1, d1, o1, x1)
    combine(sum3, c2, tmp3, tmp2)

    def finish(i, _):
        x1[:, i] = DAMPING * (x1[:, i] + tmp2[:, i // 2 - 1])
        return 0

    lax.fori_loop(5, 23, finish, 0)

    def residual(i):
        mid, near = weighted(1, i, 2, x1, weights1)
        at = pl.ds(i, 2)
        bv = b1[:, at]
        right[:, pl.ds(i - 6, 2)] = bv[:, :, 8:24, :]
        res = bv - diag1[:, at] * (mid - near)
        rest[:, pl.ds(i - 6, 2)] = res[:, :, 8:24, :]

    blocks(6, 22, 2, residual)
    for c in range(2):
        for t in range(2):
            own[c, pl.ds(t, 16, 2)] = rest[c, :, t * 8:t * 8 + 8, :]

        def read_pair(k):
            total = None
            for x in (2 * k, 2 * k + 1):
                part = rest[c, x, pl.ds(0, 8, 2), :] + rest[c, x, pl.ds(1, 8, 2), :]
                total = part if total is None else total + part
            return total

        def out(k, value):
            own[c, 32 + k] = value

        restrict_to2(read_pair, out)
    for i in range(12):
        put_pair(even_x, first, second, i, own[core, 20 + i], own[core, i])
    for i in range(3):
        put_pair(even_x, first, second, 12 + i, own[core, 33 + i], own[core, 32 + i])
    slots[0] = restrict_to3(
        lambda k: own[core, 32 + k, pl.ds(0, 4, 2), :] + own[core, 32 + k, pl.ds(1, 4, 2), :]
    )
    slots[1:] = jnp.broadcast_to(slots[0:1], (slots.shape[0] - 1, 4, 128))


def second_kernel(*refs):
    core, gx, gy = position()
    own, mine, theirs, sum3 = refs[0], refs[1:5], refs[5:9], refs[9]
    weights1, inv1, diag1 = refs[10:16], refs[16], refs[17]
    weights2, inv2 = refs[18:24], refs[24]
    x1, right, out_x, out_r = refs[25:29]
    b1, e1, d1, o1, c1, b2, e2, d2, o2, c2, tmp3, tmp2, rest = refs[29:]
    even_x, even_y = is_even(gx), is_even(gy)
    for c, parts in ((core, mine), (1 - core, theirs)):
        spread(1, 0, c, even_x, even_y, own.at[c], *parts, b1, b2, 0)
    smooth(2, b2, weights2, inv2, e2, d2, o2, c2)
    smooth(1, b1, weights1, inv1, e1, d1, o1, c1)
    combine(sum3, c2, tmp3, tmp2)

    def finish(i, _):
        c1[:, i] = x1[:, i] + DAMPING * (c1[:, i] + tmp2[:, i // 2 - 1])
        return 0

    lax.fori_loop(5, 23, finish, 0)

    def residual(i):
        mid, near = weighted(1, i, 2, c1, weights1)
        res = diag1[:, pl.ds(i, 2)] * (mid - near)
        at = pl.ds(i - 6, 2)
        rest[:, at] = right[:, at] - res[:, :, 8:24, :]

    blocks(6, 22, 2, residual)
    out_r[...] = rest[core]
    out_x[...] = c1[core, 6:22, 8:24, :]


def call(name, kernel, outs, scratch, *args):
    smem = pl.BlockSpec(memory_space=pltpu.SMEM)
    vmem = pl.BlockSpec(memory_space=pltpu.VMEM)
    return pl.pallas_call(
        kernel,
        out_shape=[jax.ShapeDtypeStruct(s, F32) for s in outs],
        in_specs=[smem if a.shape[-1] != 128 else vmem for a in args],
        out_specs=[vmem for _ in outs],
        scratch_shapes=[pltpu.VMEM(s, F32) for s in scratch],
        compiler_params=pltpu.CompilerParams(vmem_limit_bytes=56 * 1024 * 1024),
        interpret=INTERPRET,
        name=name,
    )(*args)


def trade(first, second, axis):
    size = lax.axis_size(axis)
    pairs = [(i, i ^ 1) for i in range(size)]
    others = [(i, i - 1 if i % 2 == 0 else i + 1) for i in range(1, size - 1)]
    return lax.ppermute(first, axis, pairs), lax.ppermute(second, axis, others)


def swap(x):
    return lax.ppermute(x, "grp", [(0, 1), (1, 0)])


def everywhere(slots):
    return lax.all_to_all(slots, ("gx", "gy"), 0, 0, tiled=True)


def on_device(right_side, coefficient):
    gx_n, gy_n = lax.axis_size("gx"), lax.axis_size("gy")
    count = gx_n * gy_n
    _, keeps, pushes = cheb_steps(COARSE_DEGREE, LOW_COARSE, HIGH_BOUND)
    table = jnp.array([keeps, pushes], F32)
    s1, s2, s3 = (2, 28, 32, 128), (2, 10, 24, 128), (2, 5, 24, 128)
    p2, p3 = (2, 12, 24, 128), (2, 7, 24, 128)
    s4 = (gx_n // 2, gy_n * 2, 128)
    sum3 = (2, 3, 24, 128)
    tmps = [sum3, (2, 12, 32, 128), (2, 16, 16, 128)]

    own, first, second, slots = call(
        "prepare", prepare_kernel,
        [(72, 8, 128), (30, 8, 128), (30, 8, 128), (count, 8, 128)], [], coefficient, right_side,
    )
    own_o = swap(own)
    x_one, x_two = trade(first, second, "gx")
    r3 = everywhere(slots)
    x_one_o, x_two_o = swap(x_one), swap(x_two)
    r3_o = swap(r3)
    first, second = call(
        "sides_a", functools.partial(sides_kernel, 2), [(76, 8, 128)] * 2, [], own, x_one, x_two
    )
    y_one, y_two = trade(first, second, "gy")
    flat = (count * 8, 128)
    *coarse, c3 = call(
        "coarse_a", functools.partial(coarse_kernel, gx_n, gy_n, True),
        [s3] * 7 + [s4] * 4 + [sum3], [p3, s3, s3, s3, s3, s3, s4],
        table, r3, r3_o, r3.reshape(flat), r3_o.reshape(flat),
    )
    y_one_o, y_two_o = swap(y_one), swap(y_two)
    outs = [s1] * 8 + [s2] * 7
    outs += [s1, (2, 16, 16, 128), (2, 36, 8, 128), (15, 8, 128), (15, 8, 128), (count, 4, 128)]
    *coefs, x1, right, own, first, second, slots = call(
        "fine_a", first_kernel, outs,
        [s1, s1, s1, s1, s1, p2, s2, s2, s2, s2, s2] + tmps,
        own, x_one, x_two, y_one, y_two, own_o, x_one_o, x_two_o, y_one_o, y_two_o, c3,
    )
    x_one, x_two = trade(first, second, "gx")
    r3 = everywhere(slots)
    x_one_o, x_two_o = swap(x_one), swap(x_two)
    r3_o = swap(r3)
    first, second = call(
        "sides_b", functools.partial(sides_kernel, 1), [(38, 8, 128)] * 2, [], own, x_one, x_two
    )
    y_one, y_two = trade(first, second, "gy")
    flat = (count * 4, 128)
    (c3,) = call(
        "coarse_b", functools.partial(coarse_kernel, gx_n, gy_n, False),
        [sum3], [s3, s3, s3, s3, s3, s4],
        table, r3, r3_o, r3.reshape(flat), r3_o.reshape(flat), *coarse,
    )
    y_one_o, y_two_o = swap(y_one), swap(y_two)
    solution_field, residual = call(
        "fine_b", second_kernel, [(16, 16, 128)] * 2,
        [s1, s1, s1, s1, s1, s2, s2, s2, s2, s2] + tmps,
        own, x_one, x_two, y_one, y_two, x_one_o, x_two_o, y_one_o, y_two_o, c3,
        *coefs, x1, right,
    )
    return solution_field, residual


def solution(mesh):
    placed = P("gx", "gy", "grp")
    return jax.shard_map(
        on_device, mesh=mesh, in_specs=(placed, placed), out_specs=(placed, placed),
        check_vma=False,
    )
```

```python
import functools

import jax
import jax.numpy as jnp
from jax import lax
from jax.experimental import pallas as pl
from jax.experimental.pallas import tpu as pltpu
from jax.sharding import PartitionSpec as P


FINE_DEGREE = 5
COARSE_DEGREE = 16
LOW_FINE = 0.2
LOW_COARSE = 0.02
HIGH_BOUND = 2.0
DAMPING = 0.5

F32 = jnp.float32
INTERPRET = False
LANES_X = {1: 1, 2: 2, 3: 4}
HELD = {1: (1, 27), 2: (0, 10), 3: (0, 5)}
STEPS = {
    1: ((2, 26), (3, 25), (4, 24), (5, 23)),
    2: ((1, 9), (1, 9), (2, 8), (2, 8)),
    3: ((1, 4),) * 4,
}
CHUNK = {1: 2, 2: 2, 3: 3}
PAD = {1: 0, 2: 1, 3: 1}
SCALE = {1: 1.0, 2: 0.25, 3: 0.0625, 4: 0.015625}


def cheb_steps(degree, low, high):
    theta = (high + low) / 2.0
    delta = (high - low) / 2.0
    sigma = theta / delta
    rho = 1.0 / sigma
    keeps = []
    pushes = []
    for _ in range(degree - 1):
        rho_new = 1.0 / (2.0 * sigma - rho)
        keeps.append(rho_new * rho)
        pushes.append(2.0 * rho_new / delta)
        rho = rho_new
    return (1.0 / theta, keeps, pushes)


def roll(x, shift, axis):
    size = x.shape[axis]
    return pltpu.roll(x, shift % size, axis)


def lane_iota(shape):
    return lax.broadcasted_iota(jnp.int32, shape, len(shape) - 1)


def dot(x, m):
    high = x.astype(jnp.bfloat16)
    rest = x - high.astype(F32)
    mid = rest.astype(jnp.bfloat16)
    low = (rest - mid.astype(F32)).astype(jnp.bfloat16)
    m = m.astype(jnp.bfloat16)
    mul = lambda v: jnp.dot(v, m, preferred_element_type=F32)
    return mul(high) + (mul(mid) + mul(low))


def select_matrix(fn, value):
    row = lax.broadcasted_iota(jnp.int32, (128, 128), 0)
    col = lax.broadcasted_iota(jnp.int32, (128, 128), 1)
    return jnp.where(fn(row, col), value, 0.0).astype(F32)


def neighbours(q, v):
    zz = 128 // q
    mid = v[:, 1:-1]
    lane = lane_iota(mid.shape)
    if q == 1:
        x_up, x_dn = v[:, 2:], v[:, :-2]
        for_up = for_dn = mid
    else:
        ups = roll(v[:, 1:], -zz, 3)
        dns = roll(v[:, :-1], zz, 3)
        x_up = jnp.where(lane < 128 - zz, ups[:, :-1], ups[:, 1:])
        x_dn = jnp.where(lane >= zz, dns[:, 1:], dns[:, :-1])
        for_up, for_dn = dns[:, 1:], ups[:, :-1]
    other = lambda w: jnp.concatenate([w[1:], w[:1]], axis=0)
    inner = lane % zz
    z_up = roll(jnp.where(inner == 0, other(for_up), mid), -1, 3)
    z_dn = roll(jnp.where(inner == zz - 1, other(for_dn), mid), 1, 3)
    return mid, (x_up, x_dn, roll(mid, -1, 2), roll(mid, 1, 2), z_up, z_dn)


def blocks(start, stop, step, body):
    if stop - start == step:
        body(start)
        return

    def run(n, _):
        body(start + n * step)
        return 0

    lax.fori_loop(0, (stop - start) // step, run, 0)


def faces(level, a, weights, inv, diag_ref):
    q, pad = LANES_X[level], PAD[level]
    zz = 128 // q
    first, last = HELD[level]
    step = 5 if level == 3 else 2

    def body(i):
        mid, near = neighbours(q, a[:, pl.ds(i + pad - 1, step + 2)])
        core = lax.broadcasted_iota(jnp.int32, mid.shape, 0)
        lane = lane_iota(mid.shape) % zz
        top = (core == 1) & (lane == zz - 1)
        bottom = (core == 0) & (lane == 0)
        x_up, x_dn, y_up, y_dn, z_up, z_dn = near
        z_up = jnp.where(top, 0.0, z_up)
        z_dn = jnp.where(bottom, 0.0, z_dn)
        near = (x_up, x_dn, y_up, y_dn, z_up, z_dn)
        total = 3.0 * mid + 0.5 * ((x_up + x_dn) + (y_up + y_dn) + (z_up + z_dn))
        inverse = jnp.where(mid > 0.0, 1.0 / total, 0.0)
        at = pl.ds(i, step)
        inv[:, at] = inverse
        half = 0.5 * inverse
        for k in range(6):
            w = half * (mid + near[k])
            if k == 4:
                w = jnp.where(top, 0.0, w)
            if k == 5:
                w = jnp.where(bottom, 0.0, w)
            weights[k][:, at] = w
        if diag_ref is not None:
            diag_ref[:, at] = total

    blocks(first, last, step, body)


def weighted(q, i, step, v, weights):
    mid, near = neighbours(q, v[:, pl.ds(i - 1, step + 2)])
    at = pl.ds(i, step)
    terms = [weights[k][:, at] * near[k] for k in range(6)]
    return mid, (terms[0] + terms[1]) + (terms[2] + terms[3]) + (terms[4] + terms[5])


def smooth(level, b, weights, inv, e, d, other, x):
    q = LANES_X[level]
    first, keeps, pushes = cheb_steps(FINE_DEGREE, LOW_FINE, HIGH_BOUND)
    step = CHUNK[level]

    def start(i):
        at = pl.ds(i, 5 if level == 3 else 2)
        ev = b[:, at] * inv[:, at] * (1.0 / SCALE[level])
        e[:, at] = ev
        d[:, at] = ev * first
        x[:, at] = ev * first

    blocks(*HELD[level], 5 if level == 3 else 2, start)
    if level > 1:
        for i in (HELD[level][0], HELD[level][1] - 1):
            other[:, i] = jnp.zeros_like(other[:, i])
    for n in range(FINE_DEGREE - 1):
        src, dst = (d, other) if n % 2 == 0 else (other, d)

        def body(i):
            at = pl.ds(i, step)
            mid, near = weighted(q, i, step, src, weights)
            ev = (e[:, at] - mid) + near
            new = keeps[n] * mid + pushes[n] * ev
            x[:, at] = x[:, at] + new
            if n < FINE_DEGREE - 2:
                e[:, at] = ev
                dst[:, at] = new

        blocks(*STEPS[level][n], step, body)


def x_up4(v):
    moved = roll(v, -32, 2)
    after = jnp.concatenate([moved[1:], moved[:1]], axis=0)
    return jnp.where(lane_iota(v.shape) < 96, moved, after)


def x_dn4(v):
    moved = roll(v, 32, 2)
    before = jnp.concatenate([moved[-1:], moved[:-1]], axis=0)
    return jnp.where(lane_iota(v.shape) >= 32, moved, before)


def faces4(a, fx, fy, fz, inv):
    nb, rows, _ = a.shape
    blk = lax.broadcasted_iota(jnp.int32, a.shape, 0)
    row = lax.broadcasted_iota(jnp.int32, a.shape, 1)
    lane = lane_iota(a.shape)
    half = 0.5 * a
    total = jnp.zeros_like(a)
    for up, dn, last, start, out in (
        (x_up4, x_dn4, (blk == nb - 1) & (lane >= 96), (blk == 0) & (lane < 32), fx),
        (lambda v: roll(v, -1, 1), lambda v: roll(v, 1, 1), row == rows - 1, row == 0, fy),
        (lambda v: roll(v, -1, 2), lambda v: roll(v, 1, 2), lane % 32 == 31, lane % 32 == 0, fz),
    ):
        inner = half + 0.5 * up(a)
        off = jnp.where(last, 0.0, inner)
        out[...] = off
        total = total + jnp.where(last, half, inner) + jnp.where(start, half, dn(off))
    inv[...] = 1.0 / total


def smooth4(table, b, fx, fy, fz, inv):
    first = cheb_steps(COARSE_DEGREE, LOW_COARSE, HIGH_BOUND)[0]
    e = b * inv[...] * (1.0 / SCALE[4])
    d = e * first

    def body(step, carry):
        e, d, x = carry
        gx, gy, gz = fx[...], fy[...], fz[...]
        near = gx * x_up4(d) + x_dn4(gx * d)
        near = near + gy * roll(d, -1, 1) + roll(gy * d, 1, 1)
        near = near + gz * roll(d, -1, 2) + roll(gz * d, 1, 2)
        e = e - d + inv[...] * near
        d = table[0, step] * d + table[1, step] * e
        return e, d, x + d

    return lax.fori_loop(0, COARSE_DEGREE - 1, body, (e, d, d))[2]


def build4(src, stride, offset, core, gx_n, gy_n):
    count = gx_n * gy_n * 2
    gap = stride // 2
    pairs = src[pl.ds(offset, count, stride), :] + src[pl.ds(offset + gap, count, stride), :]
    pairs = pairs.reshape(gx_n // 2, 2, gy_n * 2, 128)
    out = None
    for odd in range(2):
        mat = select_matrix(
            lambda r, c: c == odd * 64 + (r // 64) * 32 + core * 16 + (r % 32) // 2, 0.125
        )
        part = dot(pairs[:, odd].reshape(gx_n * gy_n, 128), mat)
        out = part if out is None else out + part
    return out.reshape(gx_n // 2, gy_n * 2, 128)


def window3(src, dst, field, fields, core, pos, gx_n, gy_n, pad):
    for bx in range(5):
        for by in range(6):
            ix = pos[1] + (bx - 2)
            iy = pos[2] + (by - 2)
            ok = (ix >= 0) & (ix < gx_n) & (iy >= 0) & (iy < gy_n)
            at = jnp.clip(ix, 0, gx_n - 1) * gy_n + jnp.clip(iy, 0, gy_n - 1)
            if fields == 1:
                tile = src[at]
            else:
                tile = src[at, pl.ds(field, 4, fields), :]
            dst[core, bx + pad, by * 4:by * 4 + 4, :] = jnp.where(ok, tile, 0.0)


def restrict_to2(read_pair, out):
    even = jnp.concatenate([read_pair(2 * k) for k in range(4)], axis=0)
    odd = jnp.concatenate([read_pair(2 * k + 1) for k in range(4)], axis=0)
    low = select_matrix(lambda r, c: c == r // 2, 0.125)
    high = select_matrix(lambda r, c: c == 64 + r // 2, 0.125)
    both = dot(even, low) + dot(odd, high)
    for k in range(4):
        out(k, both[k * 8:k * 8 + 8])


def restrict_to3(read_rows):
    total = None
    for k in range(4):
        mat = select_matrix(lambda r, c: c == k * 32 + (r % 64) // 2, 0.125)
        part = dot(read_rows(k), mat)
        total = part if total is None else total + part
    return total


def position():
    return tuple(lax.axis_index(name) for name in ("grp", "gx", "gy"))


def put_pair(even, first, second, at, up, down):
    first[at] = jnp.where(even, up, down)
    second[at] = jnp.where(even, down, up)


def is_even(index):
    return lax.rem(index, 2) == 0


def prepare_kernel(a, b, own, first, second, slots):
    even = is_even(position()[1])
    for f, src in enumerate((a, b)):
        for t in range(2):
            own[pl.ds(f * 32 + t, 16, 2)] = src[:, t * 8:t * 8 + 8, :]
            put_pair(
                even, first, second, pl.ds(f * 12 + t, 6, 2),
                src[10:16, t * 8:t * 8 + 8, :], src[0:6, t * 8:t * 8 + 8, :],
            )

        def read_pair(k):
            total = None
            for x in (2 * k, 2 * k + 1):
                part = src[x, pl.ds(0, 8, 2), :] + src[x, pl.ds(1, 8, 2), :]
                total = part if total is None else total + part
            return total

        values = []

        def out(k, value):
            own[64 + f * 4 + k] = value
            values.append(value)

        restrict_to2(read_pair, out)
        for k in range(3):
            put_pair(even, first, second, 24 + f * 3 + k, values[k + 1], values[k])
        slots[0, pl.ds(f, 4, 2), :] = restrict_to3(
            lambda k: own[64 + f * 4 + k, pl.ds(0, 4, 2), :] + own[64 + f * 4 + k, pl.ds(1, 4, 2), :]
        )
    slots[1:] = jnp.broadcast_to(slots[0:1], (slots.shape[0] - 1, 8, 128))


def sides_kernel(nf, own, one, two, first, second):
    core, gx, gy = position()
    even_x, even_y = is_even(gx), is_even(gy)
    if nf == 2:
        mine = lambda i: own[i]
    else:
        mine = lambda i: own[core, i]

    def lower(i):
        return jnp.where(even_x, two[i], one[i])

    def upper(i):
        return jnp.where(even_x, one[i], two[i])

    for f in range(nf):
        for i in range(28):
            if i < 6:
                low, high = lower(f * 12 + 2 * i), lower(f * 12 + 2 * i + 1)
            elif i >= 22:
                low, high = upper(f * 12 + 2 * (i - 22)), upper(f * 12 + 2 * (i - 22) + 1)
            else:
                low, high = mine(f * 32 + 2 * (i - 6)), mine(f * 32 + 2 * (i - 6) + 1)
            put_pair(even_y, first, second, f * 28 + i, high, low)
        for i in range(10):
            if i < 3:
                tile = lower(nf * 12 + f * 3 + i)
            elif i >= 7:
                tile = upper(nf * 12 + f * 3 + i - 7)
            else:
                tile = mine(nf * 32 + f * 4 + i - 3)
            first[nf * 28 + f * 10 + i] = tile
            second[nf * 28 + f * 10 + i] = tile


def spread(nf, f, core, even_x, even_y, own, x_one, x_two, y_one, y_two, fine, mid, pad):
    lower = lambda i: jnp.where(even_x, x_two[i], x_one[i])
    upper = lambda i: jnp.where(even_x, x_one[i], x_two[i])
    below = lambda i: jnp.where(even_y, y_two[i], y_one[i])
    above = lambda i: jnp.where(even_y, y_one[i], y_two[i])
    for i in range(28):
        fine[core, i, 0:8, :] = below(f * 28 + i)
        fine[core, i, 24:32, :] = above(f * 28 + i)
        for t in range(2):
            if i < 6:
                tile = lower(f * 12 + 2 * i + t)
            elif i >= 22:
                tile = upper(f * 12 + 2 * (i - 22) + t)
            else:
                tile = own[f * 32 + 2 * (i - 6) + t]
            fine[core, i, 8 + 8 * t:16 + 8 * t, :] = tile
    base = nf * 28 + f * 10
    for i in range(10):
        mid[core, i + pad, 0:8, :] = below(base + i)
        mid[core, i + pad, 16:24, :] = above(base + i)
        if i < 3:
            tile = lower(nf * 12 + f * 3 + i)
        elif i >= 7:
            tile = upper(nf * 12 + f * 3 + i - 7)
        else:
            tile = own[nf * 32 + f * 4 + i - 3]
        mid[core, i + pad, 8:16, :] = tile


def add_coarsest(pos, gx_n, gy_n, x4, x3, out):
    gx, gy = pos[1], pos[2]
    yrow = lax.broadcasted_iota(jnp.int32, (24, gy_n * 2), 0)
    ycol = lax.broadcasted_iota(jnp.int32, (24, gy_n * 2), 1)
    rows = jnp.where(ycol == (4 * gy - 8 + yrow + 1024) // 2 - 512, 1.0, 0.0).astype(F32)
    for bx in (1, 2, 3):
        ix = gx + (bx - 2)
        ok = (ix >= 0) & (ix < gx_n)
        at = jnp.clip(ix, 0, gx_n - 1)
        odd = lax.rem(at, 2)
        picked = select_rows(rows, x4[lax.div(at, 2)])
        for c in range(2):
            mat = select_matrix(
                lambda r, k: r == odd * 64 + (k // 64) * 32 + c * 16 + (k % 32) // 2, 1.0
            )
            out[c, bx - 1] = x3[c, bx] + jnp.where(ok, dot(picked, mat), 0.0)


def select_rows(rows, v):
    high = v.astype(jnp.bfloat16)
    rest = v - high.astype(F32)
    mid = rest.astype(jnp.bfloat16)
    low = (rest - mid.astype(F32)).astype(jnp.bfloat16)
    rows = rows.astype(jnp.bfloat16)
    mul = lambda w: jnp.dot(rows, w, preferred_element_type=F32)
    return mul(high) + (mul(mid) + mul(low))


def combine(sum3, c2, x2, tmp3, tmp2):
    for c in range(2):
        for bx in range(3):
            tmp3[c, bx, pl.ds(0, 12, 2), :] = sum3[c, bx, 4:16, :]
            tmp3[c, bx, pl.ds(1, 12, 2), :] = sum3[c, bx, 4:16, :]
    for low in range(4):
        mat = select_matrix(lambda r, k: r == low * 32 + (k % 64) // 2, 1.0)
        for i in [i for i in range(2, 8) if (i + 5) % 4 == low]:
            bx = (i + 5) // 4 - 1
            part = dot(tmp3[:, bx].reshape(48, 128), mat).reshape(2, 24, 128)
            x2[:, i - 2] = c2[:, i] + part
    for low in range(2):
        mat = select_matrix(lambda r, k: r == low * 64 + k // 2, 1.0)
        part = dot(x2[...].reshape(2 * 6 * 24, 128), mat).reshape(2, 6, 24, 128)
        for i in range(6):
            piece = part[:, i, 4:20, :]
            tmp2[:, 2 * i + low, pl.ds(0, 16, 2), :] = piece
            tmp2[:, 2 * i + low, pl.ds(1, 16, 2), :] = piece


def coarse_kernel(gx_n, gy_n, build, table, _, r3_a, r3_b, r3f_a, r3f_b, *refs):
    pos = position()
    core = pos[0]
    *weights3, inv3, fx4, fy4, fz4, inv4 = refs[:11]
    if build:
        sum3, a3, b3, e3, d3, o3, c3, x4 = refs[11:]
        for c in range(2):
            a3[c, 0] = jnp.zeros((24, 128), F32)
            a3[c, 6] = jnp.zeros((24, 128), F32)
        for c, src in ((core, r3_a), (1 - core, r3_b)):
            window3(src, a3, 0, 2, c, pos, gx_n, gy_n, 1)
            window3(src, b3, 1, 2, c, pos, gx_n, gy_n, 0)
        a4 = build4(r3f_a, 4, 0, core, gx_n, gy_n) + build4(r3f_b, 4, 0, 1 - core, gx_n, gy_n)
        b4 = build4(r3f_a, 4, 1, core, gx_n, gy_n) + build4(r3f_b, 4, 1, 1 - core, gx_n, gy_n)
        faces4(a4, fx4, fy4, fz4, inv4)
        faces(3, a3, weights3, inv3, None)
    else:
        sum3, b3, e3, d3, o3, c3, x4 = refs[11:]
        window3(r3_a, b3, 0, 1, core, pos, gx_n, gy_n, 0)
        window3(r3_b, b3, 0, 1, 1 - core, pos, gx_n, gy_n, 0)
        b4 = build4(r3f_a, 2, 0, core, gx_n, gy_n) + build4(r3f_b, 2, 0, 1 - core, gx_n, gy_n)
    x4[...] = smooth4(table, b4, fx4, fy4, fz4, inv4)
    smooth(3, b3, weights3, inv3, e3, d3, o3, c3)
    add_coarsest(pos, gx_n, gy_n, x4, c3, sum3)


def first_kernel(*refs):
    core, gx, gy = position()
    halves = ((core, refs[:5]), (1 - core, refs[5:10]))
    weights1, inv1, diag1 = refs[10:16], refs[16], refs[17]
    weights2, inv2 = refs[18:24], refs[24]
    c1, c2, right, token = refs[25:29]
    a1, b1, e1, d1, o1, a2, b2, e2, d2, o2 = refs[29:]
    even_x, even_y = is_even(gx), is_even(gy)
    for c in range(2):
        a2[c, 0] = jnp.zeros((24, 128), F32)
        a2[c, 11] = jnp.zeros((24, 128), F32)
    for c, parts in halves:
        spread(2, 0, c, even_x, even_y, *parts, a1, a2, 1)
        spread(2, 1, c, even_x, even_y, *parts, b1, b2, 0)
    faces(1, a1, weights1, inv1, diag1)
    faces(2, a2, weights2, inv2, None)
    smooth(2, b2, weights2, inv2, e2, d2, o2, c2)
    smooth(1, b1, weights1, inv1, e1, d1, o1, c1)
    right[...] = b1[:, 6:22, 8:24, :]
    token[...] = jnp.zeros_like(token)


def join_kernel(*refs):
    core, gx, _ = position()
    even_x = is_even(gx)
    sum3, weights1, diag1, c1, c2, right = refs[0], refs[1:7], refs[7], refs[8], refs[9], refs[10]
    x1, own, first, second, slots = refs[11:16]
    s2, tmp3, tmp2, rest = refs[16:]
    combine(sum3, c2, s2, tmp3, tmp2)

    def finish(i, _):
        x1[:, i] = DAMPING * (c1[:, i] + tmp2[:, i // 2 - 1])
        return 0

    lax.fori_loop(5, 23, finish, 0)

    def residual(i):
        mid, near = weighted(1, i, 2, x1, weights1)
        res = diag1[:, pl.ds(i, 2)] * (mid - near)
        at = pl.ds(i - 6, 2)
        rest[:, at] = right[:, at] - res[:, :, 8:24, :]

    blocks(6, 22, 2, residual)
    for c in range(2):
        for t in range(2):
            own[c, pl.ds(t, 16, 2)] = rest[c, :, t * 8:t * 8 + 8, :]

        def read_pair(k):
            total = None
            for x in (2 * k, 2 * k + 1):
                part = rest[c, x, pl.ds(0, 8, 2), :] + rest[c, x, pl.ds(1, 8, 2), :]
                total = part if total is None else total + part
            return total

        def out(k, value):
            own[c, 32 + k] = value

        restrict_to2(read_pair, out)
    for i in range(12):
        put_pair(even_x, first, second, i, own[core, 20 + i], own[core, i])
    for i in range(3):
        put_pair(even_x, first, second, 12 + i, own[core, 33 + i], own[core, 32 + i])
    slots[0] = restrict_to3(
        lambda k: own[core, 32 + k, pl.ds(0, 4, 2), :] + own[core, 32 + k, pl.ds(1, 4, 2), :]
    )
    slots[1:] = jnp.broadcast_to(slots[0:1], (slots.shape[0] - 1, 4, 128))


def second_kernel(*refs):
    core, gx, gy = position()
    own, mine, theirs, sum3 = refs[0], refs[1:5], refs[5:9], refs[9]
    weights1, inv1, diag1 = refs[10:16], refs[16], refs[17]
    weights2, inv2 = refs[18:24], refs[24]
    x1, right, out_x, out_r = refs[25:29]
    b1, e1, d1, o1, c1, b2, e2, d2, o2, c2, s2, tmp3, tmp2, rest = refs[29:]
    even_x, even_y = is_even(gx), is_even(gy)
    for c, parts in ((core, mine), (1 - core, theirs)):
        spread(1, 0, c, even_x, even_y, own.at[c], *parts, b1, b2, 0)
    smooth(2, b2, weights2, inv2, e2, d2, o2, c2)
    smooth(1, b1, weights1, inv1, e1, d1, o1, c1)
    combine(sum3, c2, s2, tmp3, tmp2)

    def finish(i, _):
        c1[:, i] = x1[:, i] + DAMPING * (c1[:, i] + tmp2[:, i // 2 - 1])
        return 0

    lax.fori_loop(5, 23, finish, 0)

    def residual(i):
        mid, near = weighted(1, i, 2, c1, weights1)
        res = diag1[:, pl.ds(i, 2)] * (mid - near)
        at = pl.ds(i - 6, 2)
        rest[:, at] = right[:, at] - res[:, :, 8:24, :]

    blocks(6, 22, 2, residual)
    out_r[...] = rest[core]
    out_x[...] = c1[core, 6:22, 8:24, :]


def call(kernel, outs, scratch, *args):
    smem = pl.BlockSpec(memory_space=pltpu.SMEM)
    vmem = pl.BlockSpec(memory_space=pltpu.VMEM)
    return pl.pallas_call(
        kernel,
        out_shape=[jax.ShapeDtypeStruct(s, F32) for s in outs],
        in_specs=[smem if a.shape[-1] != 128 else vmem for a in args],
        out_specs=[vmem for _ in outs],
        scratch_shapes=[pltpu.VMEM(s, F32) for s in scratch],
        compiler_params=pltpu.CompilerParams(vmem_limit_bytes=56 * 1024 * 1024),
        interpret=INTERPRET,
    )(*args)


def trade(first, second, axis):
    size = lax.axis_size(axis)
    pairs = [(i, i ^ 1) for i in range(size)]
    others = [(i, i - 1 if i % 2 == 0 else i + 1) for i in range(1, size - 1)]
    one = lax.ppermute(first, axis, pairs)
    two = lax.ppermute(second, axis, others)
    return one, two


def swap(x):
    return lax.ppermute(x, "grp", [(0, 1), (1, 0)])


def everywhere(slots):
    return lax.all_to_all(slots, ("gx", "gy"), 0, 0, tiled=True)


def on_device(right_side, coefficient):
    gx_n, gy_n = lax.axis_size("gx"), lax.axis_size("gy")
    count = gx_n * gy_n
    _, keeps, pushes = cheb_steps(COARSE_DEGREE, LOW_COARSE, HIGH_BOUND)
    table = jnp.array([keeps, pushes], F32)
    s1, s2, s3 = (2, 28, 32, 128), (2, 10, 24, 128), (2, 5, 24, 128)
    p2, p3 = (2, 12, 24, 128), (2, 7, 24, 128)
    s4 = (gx_n // 2, gy_n * 2, 128)
    sum3 = (2, 3, 24, 128)
    tmps = [(2, 6, 24, 128), sum3, (2, 12, 32, 128), (2, 16, 16, 128)]

    own, first, second, slots = call(
        prepare_kernel,
        [(72, 8, 128), (30, 8, 128), (30, 8, 128), (count, 8, 128)], [], coefficient, right_side,
    )
    own_o = swap(own)
    x_one, x_two = trade(first, second, "gx")
    r3 = everywhere(slots)
    x_one_o, x_two_o = swap(x_one), swap(x_two)
    r3_o = swap(r3)
    first, second = call(
        functools.partial(sides_kernel, 2), [(76, 8, 128)] * 2, [], own, x_one, x_two
    )
    y_one, y_two = trade(first, second, "gy")
    y_one_o, y_two_o = swap(y_one), swap(y_two)
    *coefs, c1, c2, right, token = call(
        first_kernel, [s1] * 8 + [s2] * 7 + [s1, s2, (2, 16, 16, 128), (8, 128)],
        [s1, s1, s1, s1, s1, p2, s2, s2, s2, s2],
        own, x_one, x_two, y_one, y_two, own_o, x_one_o, x_two_o, y_one_o, y_two_o,
    )
    flat = (count * 8, 128)
    *coarse, c3 = call(
        functools.partial(coarse_kernel, gx_n, gy_n, True),
        [s3] * 7 + [s4] * 4 + [sum3], [p3, s3, s3, s3, s3, s3, s4],
        table, token, r3, r3_o, r3.reshape(flat), r3_o.reshape(flat),
    )
    x1, own, first, second, slots = call(
        join_kernel,
        [s1, (2, 36, 8, 128), (15, 8, 128), (15, 8, 128), (count, 4, 128)], tmps,
        c3, *coefs[:6], coefs[7], c1, c2, right,
    )
    x_one, x_two = trade(first, second, "gx")
    r3 = everywhere(slots)
    x_one_o, x_two_o = swap(x_one), swap(x_two)
    r3_o = swap(r3)
    first, second = call(
        functools.partial(sides_kernel, 1), [(38, 8, 128)] * 2, [], own, x_one, x_two
    )
    y_one, y_two = trade(first, second, "gy")
    flat = (count * 4, 128)
    (c3,) = call(
        functools.partial(coarse_kernel, gx_n, gy_n, False),
        [sum3], [s3, s3, s3, s3, s3, s4],
        table, token, r3, r3_o, r3.reshape(flat), r3_o.reshape(flat), *coarse,
    )
    y_one_o, y_two_o = swap(y_one), swap(y_two)
    solution_field, residual = call(
        second_kernel, [(16, 16, 128)] * 2,
        [s1, s1, s1, s1, s1, s2, s2, s2, s2, s2] + tmps,
        own, x_one, x_two, y_one, y_two, x_one_o, x_two_o, y_one_o, y_two_o, c3,
        *coefs, x1, right,
    )
    return solution_field, residual


def solution(mesh):
    placed = P("gx", "gy", "grp")

    return jax.shard_map(
        on_device, mesh=mesh, in_specs=(placed, placed), out_specs=(placed, placed),
        check_vma=False,
    )
```

```python
import functools

import jax
import jax.numpy as jnp
from jax import lax
from jax.experimental import pallas as pl
from jax.experimental.pallas import tpu as pltpu
from jax.sharding import PartitionSpec as P


FINE_DEGREE = 5
COARSE_DEGREE = 16
LOW_FINE = 0.2
LOW_COARSE = 0.02
HIGH_BOUND = 2.0
DAMPING = 0.5

F32 = jnp.float32
INTERPRET = False
LANES_X = {1: 1, 2: 2, 3: 4}
HELD = {1: (1, 27), 2: (0, 10), 3: (0, 5)}
STEPS = {
    1: ((2, 26), (3, 25), (4, 24), (5, 23)),
    2: ((1, 9), (1, 9), (2, 8), (2, 8)),
    3: ((1, 4),) * 4,
}
CHUNK = {1: 2, 2: 2, 3: 3}
PAD = {1: 0, 2: 1, 3: 1}
SCALE = {1: 1.0, 2: 0.25, 3: 0.0625, 4: 0.015625}


def cheb_steps(degree, low, high):
    theta = (high + low) / 2.0
    delta = (high - low) / 2.0
    sigma = theta / delta
    rho = 1.0 / sigma
    keeps = []
    pushes = []
    for _ in range(degree - 1):
        rho_new = 1.0 / (2.0 * sigma - rho)
        keeps.append(rho_new * rho)
        pushes.append(2.0 * rho_new / delta)
        rho = rho_new
    return (1.0 / theta, keeps, pushes)


def roll(x, shift, axis):
    size = x.shape[axis]
    return pltpu.roll(x, shift % size, axis)


def lane_iota(shape):
    return lax.broadcasted_iota(jnp.int32, shape, len(shape) - 1)


def dot(x, m):
    high = x.astype(jnp.bfloat16)
    rest = x - high.astype(F32)
    mid = rest.astype(jnp.bfloat16)
    low = (rest - mid.astype(F32)).astype(jnp.bfloat16)
    m = m.astype(jnp.bfloat16)
    mul = lambda v: jnp.dot(v, m, preferred_element_type=F32)
    return mul(high) + (mul(mid) + mul(low))


def select_matrix(fn, value):
    row = lax.broadcasted_iota(jnp.int32, (128, 128), 0)
    col = lax.broadcasted_iota(jnp.int32, (128, 128), 1)
    return jnp.where(fn(row, col), value, 0.0).astype(F32)


def neighbours(q, v):
    zz = 128 // q
    mid = v[:, 1:-1]
    lane = lane_iota(mid.shape)
    if q == 1:
        x_up, x_dn = v[:, 2:], v[:, :-2]
        for_up = for_dn = mid
    else:
        ups = roll(v[:, 1:], -zz, 3)
        dns = roll(v[:, :-1], zz, 3)
        x_up = jnp.where(lane < 128 - zz, ups[:, :-1], ups[:, 1:])
        x_dn = jnp.where(lane >= zz, dns[:, 1:], dns[:, :-1])
        for_up, for_dn = dns[:, 1:], ups[:, :-1]
    other = lambda w: jnp.concatenate([w[1:], w[:1]], axis=0)
    inner = lane % zz
    z_up = roll(jnp.where(inner == 0, other(for_up), mid), -1, 3)
    z_dn = roll(jnp.where(inner == zz - 1, other(for_dn), mid), 1, 3)
    return mid, (x_up, x_dn, roll(mid, -1, 2), roll(mid, 1, 2), z_up, z_dn)


def blocks(start, stop, step, body):
    if stop - start == step:
        body(start)
        return

    def run(n, _):
        body(start + n * step)
        return 0

    lax.fori_loop(0, (stop - start) // step, run, 0)


def faces(level, a, weights, inv, diag_ref):
    q, pad = LANES_X[level], PAD[level]
    zz = 128 // q
    first, last = HELD[level]
    step = 5 if level == 3 else 2

    def body(i):
        mid, near = neighbours(q, a[:, pl.ds(i + pad - 1, step + 2)])
        core = lax.broadcasted_iota(jnp.int32, mid.shape, 0)
        lane = lane_iota(mid.shape) % zz
        top = (core == 1) & (lane == zz - 1)
        bottom = (core == 0) & (lane == 0)
        x_up, x_dn, y_up, y_dn, z_up, z_dn = near
        z_up = jnp.where(top, 0.0, z_up)
        z_dn = jnp.where(bottom, 0.0, z_dn)
        near = (x_up, x_dn, y_up, y_dn, z_up, z_dn)
        total = 3.0 * mid + 0.5 * ((x_up + x_dn) + (y_up + y_dn) + (z_up + z_dn))
        inverse = jnp.where(mid > 0.0, 1.0 / total, 0.0)
        at = pl.ds(i, step)
        inv[:, at] = inverse
        half = 0.5 * inverse
        for k in range(6):
            w = half * (mid + near[k])
            if k == 4:
                w = jnp.where(top, 0.0, w)
            if k == 5:
                w = jnp.where(bottom, 0.0, w)
            weights[k][:, at] = w
        if diag_ref is not None:
            diag_ref[:, at] = total

    blocks(first, last, step, body)


def weighted(q, i, step, v, weights):
    mid, near = neighbours(q, v[:, pl.ds(i - 1, step + 2)])
    at = pl.ds(i, step)
    terms = [weights[k][:, at] * near[k] for k in range(6)]
    return mid, (terms[0] + terms[1]) + (terms[2] + terms[3]) + (terms[4] + terms[5])


def smooth(level, b, weights, inv, e, d, other, x):
    q = LANES_X[level]
    first, keeps, pushes = cheb_steps(FINE_DEGREE, LOW_FINE, HIGH_BOUND)
    step = CHUNK[level]

    def start(i):
        at = pl.ds(i, 5 if level == 3 else 2)
        ev = b[:, at] * inv[:, at] * (1.0 / SCALE[level])
        e[:, at] = ev
        d[:, at] = ev * first
        x[:, at] = ev * first

    blocks(*HELD[level], 5 if level == 3 else 2, start)
    if level > 1:
        for i in (HELD[level][0], HELD[level][1] - 1):
            other[:, i] = jnp.zeros_like(other[:, i])
    for n in range(FINE_DEGREE - 1):
        src, dst = (d, other) if n % 2 == 0 else (other, d)

        def body(i):
            at = pl.ds(i, step)
            mid, near = weighted(q, i, step, src, weights)
            ev = (e[:, at] - mid) + near
            new = keeps[n] * mid + pushes[n] * ev
            x[:, at] = x[:, at] + new
            if n < FINE_DEGREE - 2:
                e[:, at] = ev
                dst[:, at] = new

        blocks(*STEPS[level][n], step, body)


def x_up4(v):
    moved = roll(v, -32, 2)
    after = jnp.concatenate([moved[1:], moved[:1]], axis=0)
    return jnp.where(lane_iota(v.shape) < 96, moved, after)


def x_dn4(v):
    moved = roll(v, 32, 2)
    before = jnp.concatenate([moved[-1:], moved[:-1]], axis=0)
    return jnp.where(lane_iota(v.shape) >= 32, moved, before)


def faces4(a, fx, fy, fz, inv):
    nb, rows, _ = a.shape
    blk = lax.broadcasted_iota(jnp.int32, a.shape, 0)
    row = lax.broadcasted_iota(jnp.int32, a.shape, 1)
    lane = lane_iota(a.shape)
    half = 0.5 * a
    total = jnp.zeros_like(a)
    for up, dn, last, start, out in (
        (x_up4, x_dn4, (blk == nb - 1) & (lane >= 96), (blk == 0) & (lane < 32), fx),
        (lambda v: roll(v, -1, 1), lambda v: roll(v, 1, 1), row == rows - 1, row == 0, fy),
        (lambda v: roll(v, -1, 2), lambda v: roll(v, 1, 2), lane % 32 == 31, lane % 32 == 0, fz),
    ):
        inner = half + 0.5 * up(a)
        off = jnp.where(last, 0.0, inner)
        out[...] = off
        total = total + jnp.where(last, half, inner) + jnp.where(start, half, dn(off))
    inv[...] = 1.0 / total


def smooth4(table, b, fx, fy, fz, inv):
    first = cheb_steps(COARSE_DEGREE, LOW_COARSE, HIGH_BOUND)[0]
    e = b * inv[...] * (1.0 / SCALE[4])
    d = e * first

    def body(step, carry):
        e, d, x = carry
        gx, gy, gz = fx[...], fy[...], fz[...]
        near = gx * x_up4(d) + x_dn4(gx * d)
        near = near + gy * roll(d, -1, 1) + roll(gy * d, 1, 1)
        near = near + gz * roll(d, -1, 2) + roll(gz * d, 1, 2)
        e = e - d + inv[...] * near
        d = table[0, step] * d + table[1, step] * e
        return e, d, x + d

    return lax.fori_loop(0, COARSE_DEGREE - 1, body, (e, d, d))[2]


def build4(src, stride, offset, core, gx_n, gy_n):
    count = gx_n * gy_n * 2
    gap = stride // 2
    pairs = src[pl.ds(offset, count, stride), :] + src[pl.ds(offset + gap, count, stride), :]
    pairs = pairs.reshape(gx_n // 2, 2, gy_n * 2, 128)
    out = None
    for odd in range(2):
        mat = select_matrix(
            lambda r, c: c == odd * 64 + (r // 64) * 32 + core * 16 + (r % 32) // 2, 0.125
        )
        part = dot(pairs[:, odd].reshape(gx_n * gy_n, 128), mat)
        out = part if out is None else out + part
    return out.reshape(gx_n // 2, gy_n * 2, 128)


def window3(src, dst, field, fields, core, pos, gx_n, gy_n, pad):
    for bx in range(5):
        for by in range(6):
            ix = pos[1] + (bx - 2)
            iy = pos[2] + (by - 2)
            ok = (ix >= 0) & (ix < gx_n) & (iy >= 0) & (iy < gy_n)
            at = jnp.clip(ix, 0, gx_n - 1) * gy_n + jnp.clip(iy, 0, gy_n - 1)
            if fields == 1:
                tile = src[at]
            else:
                tile = src[at, pl.ds(field, 4, fields), :]
            dst[core, bx + pad, by * 4:by * 4 + 4, :] = jnp.where(ok, tile, 0.0)


def restrict_to2(read_pair, out):
    even = jnp.concatenate([read_pair(2 * k) for k in range(4)], axis=0)
    odd = jnp.concatenate([read_pair(2 * k + 1) for k in range(4)], axis=0)
    low = select_matrix(lambda r, c: c == r // 2, 0.125)
    high = select_matrix(lambda r, c: c == 64 + r // 2, 0.125)
    both = dot(even, low) + dot(odd, high)
    for k in range(4):
        out(k, both[k * 8:k * 8 + 8])


def restrict_to3(read_rows):
    total = None
    for k in range(4):
        mat = select_matrix(lambda r, c: c == k * 32 + (r % 64) // 2, 0.125)
        part = dot(read_rows(k), mat)
        total = part if total is None else total + part
    return total


def position():
    return tuple(lax.axis_index(name) for name in ("grp", "gx", "gy"))


def put_pair(even, first, second, at, up, down):
    first[at] = jnp.where(even, up, down)
    second[at] = jnp.where(even, down, up)


def is_even(index):
    return lax.rem(index, 2) == 0


def prepare_kernel(a, b, own, first, second, slots):
    even = is_even(position()[1])
    for f, src in enumerate((a, b)):
        for t in range(2):
            own[pl.ds(f * 32 + t, 16, 2)] = src[:, t * 8:t * 8 + 8, :]
            put_pair(
                even, first, second, pl.ds(f * 12 + t, 6, 2),
                src[10:16, t * 8:t * 8 + 8, :], src[0:6, t * 8:t * 8 + 8, :],
            )

        def read_pair(k):
            total = None
            for x in (2 * k, 2 * k + 1):
                part = src[x, pl.ds(0, 8, 2), :] + src[x, pl.ds(1, 8, 2), :]
                total = part if total is None else total + part
            return total

        values = []

        def out(k, value):
            own[64 + f * 4 + k] = value
            values.append(value)

        restrict_to2(read_pair, out)
        for k in range(3):
            put_pair(even, first, second, 24 + f * 3 + k, values[k + 1], values[k])
        slots[0, pl.ds(f, 4, 2), :] = restrict_to3(
            lambda k: own[64 + f * 4 + k, pl.ds(0, 4, 2), :] + own[64 + f * 4 + k, pl.ds(1, 4, 2), :]
        )
    slots[1:] = jnp.broadcast_to(slots[0:1], (slots.shape[0] - 1, 8, 128))


def sides_kernel(nf, own, one, two, first, second):
    core, gx, gy = position()
    even_x, even_y = is_even(gx), is_even(gy)
    if nf == 2:
        mine = lambda i: own[i]
    else:
        mine = lambda i: own[core, i]

    def lower(i):
        return jnp.where(even_x, two[i], one[i])

    def upper(i):
        return jnp.where(even_x, one[i], two[i])

    for f in range(nf):
        for i in range(28):
            if i < 6:
                low, high = lower(f * 12 + 2 * i), lower(f * 12 + 2 * i + 1)
            elif i >= 22:
                low, high = upper(f * 12 + 2 * (i - 22)), upper(f * 12 + 2 * (i - 22) + 1)
            else:
                low, high = mine(f * 32 + 2 * (i - 6)), mine(f * 32 + 2 * (i - 6) + 1)
            put_pair(even_y, first, second, f * 28 + i, high, low)
        for i in range(10):
            if i < 3:
                tile = lower(nf * 12 + f * 3 + i)
            elif i >= 7:
                tile = upper(nf * 12 + f * 3 + i - 7)
            else:
                tile = mine(nf * 32 + f * 4 + i - 3)
            first[nf * 28 + f * 10 + i] = tile
            second[nf * 28 + f * 10 + i] = tile


def spread(nf, f, core, even_x, even_y, own, x_one, x_two, y_one, y_two, fine, mid, pad):
    lower = lambda i: jnp.where(even_x, x_two[i], x_one[i])
    upper = lambda i: jnp.where(even_x, x_one[i], x_two[i])
    below = lambda i: jnp.where(even_y, y_two[i], y_one[i])
    above = lambda i: jnp.where(even_y, y_one[i], y_two[i])
    for i in range(28):
        fine[core, i, 0:8, :] = below(f * 28 + i)
        fine[core, i, 24:32, :] = above(f * 28 + i)
        for t in range(2):
            if i < 6:
                tile = lower(f * 12 + 2 * i + t)
            elif i >= 22:
                tile = upper(f * 12 + 2 * (i - 22) + t)
            else:
                tile = own[f * 32 + 2 * (i - 6) + t]
            fine[core, i, 8 + 8 * t:16 + 8 * t, :] = tile
    base = nf * 28 + f * 10
    for i in range(10):
        mid[core, i + pad, 0:8, :] = below(base + i)
        mid[core, i + pad, 16:24, :] = above(base + i)
        if i < 3:
            tile = lower(nf * 12 + f * 3 + i)
        elif i >= 7:
            tile = upper(nf * 12 + f * 3 + i - 7)
        else:
            tile = own[nf * 32 + f * 4 + i - 3]
        mid[core, i + pad, 8:16, :] = tile


def add_coarsest(pos, gx_n, gy_n, x4, x3, out):
    gx, gy = pos[1], pos[2]
    yrow = lax.broadcasted_iota(jnp.int32, (24, gy_n * 2), 0)
    ycol = lax.broadcasted_iota(jnp.int32, (24, gy_n * 2), 1)
    rows = jnp.where(ycol == (4 * gy - 8 + yrow + 1024) // 2 - 512, 1.0, 0.0).astype(F32)
    for bx in (1, 2, 3):
        ix = gx + (bx - 2)
        ok = (ix >= 0) & (ix < gx_n)
        at = jnp.clip(ix, 0, gx_n - 1)
        odd = lax.rem(at, 2)
        picked = select_rows(rows, x4[lax.div(at, 2)])
        for c in range(2):
            mat = select_matrix(
                lambda r, k: r == odd * 64 + (k // 64) * 32 + c * 16 + (k % 32) // 2, 1.0
            )
            out[c, bx - 1] = x3[c, bx] + jnp.where(ok, dot(picked, mat), 0.0)


def select_rows(rows, v):
    high = v.astype(jnp.bfloat16)
    rest = v - high.astype(F32)
    mid = rest.astype(jnp.bfloat16)
    low = (rest - mid.astype(F32)).astype(jnp.bfloat16)
    rows = rows.astype(jnp.bfloat16)
    mul = lambda w: jnp.dot(rows, w, preferred_element_type=F32)
    return mul(high) + (mul(mid) + mul(low))


def combine(sum3, c2, x2, tmp3, tmp2):
    for c in range(2):
        for bx in range(3):
            tmp3[c, bx, pl.ds(0, 12, 2), :] = sum3[c, bx, 4:16, :]
            tmp3[c, bx, pl.ds(1, 12, 2), :] = sum3[c, bx, 4:16, :]
    for low in range(4):
        mat = select_matrix(lambda r, k: r == low * 32 + (k % 64) // 2, 1.0)
        for i in [i for i in range(2, 8) if (i + 5) % 4 == low]:
            bx = (i + 5) // 4 - 1
            part = dot(tmp3[:, bx].reshape(48, 128), mat).reshape(2, 24, 128)
            x2[:, i - 2] = c2[:, i] + part
    for low in range(2):
        mat = select_matrix(lambda r, k: r == low * 64 + k // 2, 1.0)
        part = dot(x2[...].reshape(2 * 6 * 24, 128), mat).reshape(2, 6, 24, 128)
        for i in range(6):
            piece = part[:, i, 4:20, :]
            tmp2[:, 2 * i + low, pl.ds(0, 16, 2), :] = piece
            tmp2[:, 2 * i + low, pl.ds(1, 16, 2), :] = piece


def coarse(gx_n, gy_n, build, table, r3_a, r3_b, r3f_a, r3f_b, *refs):
    pos = position()
    core = pos[0]
    *weights3, inv3, fx4, fy4, fz4, inv4 = refs[:11]
    if build:
        sum3, a3, b3, e3, d3, o3, c3, x4 = refs[11:]
        for c in range(2):
            a3[c, 0] = jnp.zeros((24, 128), F32)
            a3[c, 6] = jnp.zeros((24, 128), F32)
        for c, src in ((core, r3_a), (1 - core, r3_b)):
            window3(src, a3, 0, 2, c, pos, gx_n, gy_n, 1)
            window3(src, b3, 1, 2, c, pos, gx_n, gy_n, 0)
        a4 = build4(r3f_a, 4, 0, core, gx_n, gy_n) + build4(r3f_b, 4, 0, 1 - core, gx_n, gy_n)
        b4 = build4(r3f_a, 4, 1, core, gx_n, gy_n) + build4(r3f_b, 4, 1, 1 - core, gx_n, gy_n)
        faces4(a4, fx4, fy4, fz4, inv4)
        faces(3, a3, weights3, inv3, None)
    else:
        sum3, b3, e3, d3, o3, c3, x4 = refs[11:]
        window3(r3_a, b3, 0, 1, core, pos, gx_n, gy_n, 0)
        window3(r3_b, b3, 0, 1, 1 - core, pos, gx_n, gy_n, 0)
        b4 = build4(r3f_a, 2, 0, core, gx_n, gy_n) + build4(r3f_b, 2, 0, 1 - core, gx_n, gy_n)
    x4[...] = smooth4(table, b4, fx4, fy4, fz4, inv4)
    smooth(3, b3, weights3, inv3, e3, d3, o3, c3)
    add_coarsest(pos, gx_n, gy_n, x4, c3, sum3)


def coarse_kernel(gx_n, gy_n, *refs):
    coarse(gx_n, gy_n, False, *refs)


def first_kernel(*refs):
    core, gx, gy = position()
    halves = ((core, refs[:5]), (1 - core, refs[5:10]))
    weights1, inv1, diag1 = refs[10:16], refs[16], refs[17]
    weights2, inv2 = refs[18:24], refs[24]
    b1, c2 = refs[25:27]
    a1, a2, b2, e2, d2, o2 = refs[27:]
    even_x, even_y = is_even(gx), is_even(gy)
    for c in range(2):
        a2[c, 0] = jnp.zeros((24, 128), F32)
        a2[c, 11] = jnp.zeros((24, 128), F32)
    for c, parts in halves:
        spread(2, 0, c, even_x, even_y, *parts, a1, a2, 1)
        spread(2, 1, c, even_x, even_y, *parts, b1, b2, 0)
    faces(1, a1, weights1, inv1, diag1)
    faces(2, a2, weights2, inv2, None)
    smooth(2, b2, weights2, inv2, e2, d2, o2, c2)


def smooth_kernel(*refs):
    weights1, inv1, b1, c1, e1, d1, o1 = refs[:6], *refs[6:]
    smooth(1, b1, weights1, inv1, e1, d1, o1, c1)


def join_kernel(gx_n, gy_n, *refs):
    core, gx, _ = position()
    even_x = is_even(gx)
    weights1, diag1, b1, c1, c2 = refs[5:11], *refs[11:15]
    x1, right, own, first, second, slots = refs[26:32]
    sum3, s2, tmp3, tmp2, rest = refs[32:37]
    coarse(gx_n, gy_n, True, *refs[:5], *refs[15:26], sum3, *refs[37:])
    combine(sum3, c2, s2, tmp3, tmp2)

    def finish(i, _):
        x1[:, i] = DAMPING * (c1[:, i] + tmp2[:, i // 2 - 1])
        return 0

    lax.fori_loop(5, 23, finish, 0)

    def residual(i):
        mid, near = weighted(1, i, 2, x1, weights1)
        bv = b1[:, pl.ds(i, 2)]
        res = bv - diag1[:, pl.ds(i, 2)] * (mid - near)
        at = pl.ds(i - 6, 2)
        right[:, at] = bv[:, :, 8:24, :]
        rest[:, at] = res[:, :, 8:24, :]

    blocks(6, 22, 2, residual)
    for c in range(2):
        for t in range(2):
            own[c, pl.ds(t, 16, 2)] = rest[c, :, t * 8:t * 8 + 8, :]

        def read_pair(k):
            total = None
            for x in (2 * k, 2 * k + 1):
                part = rest[c, x, pl.ds(0, 8, 2), :] + rest[c, x, pl.ds(1, 8, 2), :]
                total = part if total is None else total + part
            return total

        def out(k, value):
            own[c, 32 + k] = value

        restrict_to2(read_pair, out)
    for i in range(12):
        put_pair(even_x, first, second, i, own[core, 20 + i], own[core, i])
    for i in range(3):
        put_pair(even_x, first, second, 12 + i, own[core, 33 + i], own[core, 32 + i])
    slots[0] = restrict_to3(
        lambda k: own[core, 32 + k, pl.ds(0, 4, 2), :] + own[core, 32 + k, pl.ds(1, 4, 2), :]
    )
    slots[1:] = jnp.broadcast_to(slots[0:1], (slots.shape[0] - 1, 4, 128))


def second_kernel(*refs):
    core, gx, gy = position()
    own, mine, theirs, sum3 = refs[0], refs[1:5], refs[5:9], refs[9]
    weights1, inv1, diag1 = refs[10:16], refs[16], refs[17]
    weights2, inv2 = refs[18:24], refs[24]
    x1, right, out_x, out_r = refs[25:29]
    b1, e1, d1, o1, c1, b2, e2, d2, o2, c2, s2, tmp3, tmp2, rest = refs[29:]
    even_x, even_y = is_even(gx), is_even(gy)
    for c, parts in ((core, mine), (1 - core, theirs)):
        spread(1, 0, c, even_x, even_y, own.at[c], *parts, b1, b2, 0)
    smooth(2, b2, weights2, inv2, e2, d2, o2, c2)
    smooth(1, b1, weights1, inv1, e1, d1, o1, c1)
    combine(sum3, c2, s2, tmp3, tmp2)

    def finish(i, _):
        c1[:, i] = x1[:, i] + DAMPING * (c1[:, i] + tmp2[:, i // 2 - 1])
        return 0

    lax.fori_loop(5, 23, finish, 0)

    def residual(i):
        mid, near = weighted(1, i, 2, c1, weights1)
        res = diag1[:, pl.ds(i, 2)] * (mid - near)
        at = pl.ds(i - 6, 2)
        rest[:, at] = right[:, at] - res[:, :, 8:24, :]

    blocks(6, 22, 2, residual)
    out_r[...] = rest[core]
    out_x[...] = c1[core, 6:22, 8:24, :]


def call(kernel, outs, scratch, *args):
    smem = pl.BlockSpec(memory_space=pltpu.SMEM)
    vmem = pl.BlockSpec(memory_space=pltpu.VMEM)
    return pl.pallas_call(
        kernel,
        out_shape=[jax.ShapeDtypeStruct(s, F32) for s in outs],
        in_specs=[smem if a.shape[-1] != 128 else vmem for a in args],
        out_specs=[vmem for _ in outs],
        scratch_shapes=[pltpu.VMEM(s, F32) for s in scratch],
        compiler_params=pltpu.CompilerParams(vmem_limit_bytes=24 * 1024 * 1024),
        interpret=INTERPRET,
    )(*args)


def trade(first, second, axis):
    size = lax.axis_size(axis)
    pairs = [(i, i ^ 1) for i in range(size)]
    others = [(i, i - 1 if i % 2 == 0 else i + 1) for i in range(1, size - 1)]
    one = lax.ppermute(first, axis, pairs)
    two = lax.ppermute(second, axis, others)
    return one, two


def swap(x):
    return lax.ppermute(x, "grp", [(0, 1), (1, 0)])


def everywhere(slots):
    return lax.all_to_all(slots, ("gx", "gy"), 0, 0, tiled=True)


def on_device(right_side, coefficient):
    gx_n, gy_n = lax.axis_size("gx"), lax.axis_size("gy")
    count = gx_n * gy_n
    _, keeps, pushes = cheb_steps(COARSE_DEGREE, LOW_COARSE, HIGH_BOUND)
    table = jnp.array([keeps, pushes], F32)
    s1, s2, s3 = (2, 28, 32, 128), (2, 10, 24, 128), (2, 5, 24, 128)
    p2, p3 = (2, 12, 24, 128), (2, 7, 24, 128)
    s4 = (gx_n // 2, gy_n * 2, 128)
    sum3 = (2, 3, 24, 128)
    tmps = [(2, 6, 24, 128), sum3, (2, 12, 32, 128), (2, 16, 16, 128)]

    own, first, second, slots = call(
        prepare_kernel,
        [(72, 8, 128), (30, 8, 128), (30, 8, 128), (count, 8, 128)], [], coefficient, right_side,
    )
    own_o = swap(own)
    x_one, x_two = trade(first, second, "gx")
    r3 = everywhere(slots)
    x_one_o, x_two_o = swap(x_one), swap(x_two)
    r3_o = swap(r3)
    first, second = call(
        functools.partial(sides_kernel, 2), [(76, 8, 128)] * 2, [], own, x_one, x_two
    )
    y_one, y_two = trade(first, second, "gy")
    y_one_o, y_two_o = swap(y_one), swap(y_two)
    *coefs, b1, c2 = call(
        first_kernel, [s1] * 8 + [s2] * 7 + [s1, s2], [s1, p2, s2, s2, s2, s2],
        own, x_one, x_two, y_one, y_two, own_o, x_one_o, x_two_o, y_one_o, y_two_o,
    )
    (c1,) = call(smooth_kernel, [s1], [s1, s1, s1], *coefs[:7], b1)
    flat = (count * 8, 128)
    *coarse, x1, right, own, first, second, slots = call(
        functools.partial(join_kernel, gx_n, gy_n),
        [s3] * 7 + [s4] * 4
        + [s1, (2, 16, 16, 128), (2, 36, 8, 128), (15, 8, 128), (15, 8, 128), (count, 4, 128)],
        [sum3] + tmps + [p3, s3, s3, s3, s3, s3, s4],
        table, r3, r3_o, r3.reshape(flat), r3_o.reshape(flat), *coefs[:6], coefs[7], b1, c1, c2,
    )
    x_one, x_two = trade(first, second, "gx")
    r3 = everywhere(slots)
    x_one_o, x_two_o = swap(x_one), swap(x_two)
    r3_o = swap(r3)
    first, second = call(
        functools.partial(sides_kernel, 1), [(38, 8, 128)] * 2, [], own, x_one, x_two
    )
    y_one, y_two = trade(first, second, "gy")
    flat = (count * 4, 128)
    (c3,) = call(
        functools.partial(coarse_kernel, gx_n, gy_n),
        [sum3], [s3, s3, s3, s3, s3, s4],
        table, r3, r3_o, r3.reshape(flat), r3_o.reshape(flat), *coarse,
    )
    y_one_o, y_two_o = swap(y_one), swap(y_two)
    solution_field, residual = call(
        second_kernel, [(16, 16, 128)] * 2,
        [s1, s1, s1, s1, s1, s2, s2, s2, s2, s2] + tmps,
        own, x_one, x_two, y_one, y_two, x_one_o, x_two_o, y_one_o, y_two_o, c3,
        *coefs, x1, right,
    )
    return solution_field, residual


def solution(mesh):
    placed = P("gx", "gy", "grp")

    return jax.shard_map(
        on_device, mesh=mesh, in_specs=(placed, placed), out_specs=(placed, placed),
        check_vma=False,
    )
```

```python
import functools

import jax
import jax.numpy as jnp
from jax import lax
from jax.experimental import pallas as pl
from jax.experimental.pallas import tpu as pltpu
from jax.sharding import PartitionSpec as P


FINE_DEGREE = 5
COARSE_DEGREE = 16
LOW_FINE = 0.2
LOW_COARSE = 0.02
HIGH_BOUND = 2.0
DAMPING = 0.5

F32 = jnp.float32
INTERPRET = False
LANES_X = {1: 1, 2: 2, 3: 4}
HELD = {1: (1, 27), 2: (0, 10), 3: (0, 5)}
STEPS = {
    1: ((2, 26), (3, 25), (4, 24), (5, 23)),
    2: ((1, 9), (1, 9), (2, 8), (2, 8)),
    3: ((1, 4),) * 4,
}
CHUNK = {1: 2, 2: 2, 3: 3}
PAD = {1: 0, 2: 1, 3: 1}
SCALE = {1: 1.0, 2: 0.25, 3: 0.0625, 4: 0.015625}


def cheb_steps(degree, low, high):
    theta = (high + low) / 2.0
    delta = (high - low) / 2.0
    sigma = theta / delta
    rho = 1.0 / sigma
    keeps = []
    pushes = []
    for _ in range(degree - 1):
        rho_new = 1.0 / (2.0 * sigma - rho)
        keeps.append(rho_new * rho)
        pushes.append(2.0 * rho_new / delta)
        rho = rho_new
    return (1.0 / theta, keeps, pushes)


def roll(x, shift, axis):
    size = x.shape[axis]
    return pltpu.roll(x, shift % size, axis)


def lane_iota(shape):
    return lax.broadcasted_iota(jnp.int32, shape, len(shape) - 1)


def dot(x, m):
    high = x.astype(jnp.bfloat16)
    rest = x - high.astype(F32)
    mid = rest.astype(jnp.bfloat16)
    low = (rest - mid.astype(F32)).astype(jnp.bfloat16)
    m = m.astype(jnp.bfloat16)
    mul = lambda v: jnp.dot(v, m, preferred_element_type=F32)
    return mul(high) + (mul(mid) + mul(low))


def select_matrix(fn, value):
    row = lax.broadcasted_iota(jnp.int32, (128, 128), 0)
    col = lax.broadcasted_iota(jnp.int32, (128, 128), 1)
    return jnp.where(fn(row, col), value, 0.0).astype(F32)


def neighbours(q, v):
    zz = 128 // q
    mid = v[:, 1:-1]
    lane = lane_iota(mid.shape)
    if q == 1:
        x_up, x_dn = v[:, 2:], v[:, :-2]
        for_up = for_dn = mid
    else:
        ups = roll(v[:, 1:], -zz, 3)
        dns = roll(v[:, :-1], zz, 3)
        x_up = jnp.where(lane < 128 - zz, ups[:, :-1], ups[:, 1:])
        x_dn = jnp.where(lane >= zz, dns[:, 1:], dns[:, :-1])
        for_up, for_dn = dns[:, 1:], ups[:, :-1]
    other = lambda w: jnp.concatenate([w[1:], w[:1]], axis=0)
    inner = lane % zz
    z_up = roll(jnp.where(inner == 0, other(for_up), mid), -1, 3)
    z_dn = roll(jnp.where(inner == zz - 1, other(for_dn), mid), 1, 3)
    return mid, (x_up, x_dn, roll(mid, -1, 2), roll(mid, 1, 2), z_up, z_dn)


def blocks(start, stop, step, body):
    if stop - start == step:
        body(start)
        return

    def run(n, _):
        body(start + n * step)
        return 0

    lax.fori_loop(0, (stop - start) // step, run, 0)


def faces(level, a, weights, inv, diag_ref):
    q, pad = LANES_X[level], PAD[level]
    zz = 128 // q
    first, last = HELD[level]
    step = 5 if level == 3 else 2

    def body(i):
        mid, near = neighbours(q, a[:, pl.ds(i + pad - 1, step + 2)])
        core = lax.broadcasted_iota(jnp.int32, mid.shape, 0)
        lane = lane_iota(mid.shape) % zz
        top = (core == 1) & (lane == zz - 1)
        bottom = (core == 0) & (lane == 0)
        x_up, x_dn, y_up, y_dn, z_up, z_dn = near
        z_up = jnp.where(top, 0.0, z_up)
        z_dn = jnp.where(bottom, 0.0, z_dn)
        near = (x_up, x_dn, y_up, y_dn, z_up, z_dn)
        total = 3.0 * mid + 0.5 * ((x_up + x_dn) + (y_up + y_dn) + (z_up + z_dn))
        inverse = jnp.where(mid > 0.0, 1.0 / total, 0.0)
        at = pl.ds(i, step)
        inv[:, at] = inverse
        half = 0.5 * inverse
        for k in range(6):
            w = half * (mid + near[k])
            if k == 4:
                w = jnp.where(top, 0.0, w)
            if k == 5:
                w = jnp.where(bottom, 0.0, w)
            weights[k][:, at] = w
        if diag_ref is not None:
            diag_ref[:, at] = total

    blocks(first, last, step, body)


def weighted(q, i, step, v, weights):
    mid, near = neighbours(q, v[:, pl.ds(i - 1, step + 2)])
    at = pl.ds(i, step)
    terms = [weights[k][:, at] * near[k] for k in range(6)]
    return mid, (terms[0] + terms[1]) + (terms[2] + terms[3]) + (terms[4] + terms[5])


def smooth(level, b, weights, inv, e, d, other, x):
    q = LANES_X[level]
    first, keeps, pushes = cheb_steps(FINE_DEGREE, LOW_FINE, HIGH_BOUND)
    step = CHUNK[level]

    def start(i):
        at = pl.ds(i, 5 if level == 3 else 2)
        ev = b[:, at] * inv[:, at] * (1.0 / SCALE[level])
        e[:, at] = ev
        d[:, at] = ev * first
        x[:, at] = ev * first

    blocks(*HELD[level], 5 if level == 3 else 2, start)
    if level > 1:
        for i in (HELD[level][0], HELD[level][1] - 1):
            other[:, i] = jnp.zeros_like(other[:, i])
    for n in range(FINE_DEGREE - 1):
        src, dst = (d, other) if n % 2 == 0 else (other, d)

        def body(i):
            at = pl.ds(i, step)
            mid, near = weighted(q, i, step, src, weights)
            ev = (e[:, at] - mid) + near
            new = keeps[n] * mid + pushes[n] * ev
            x[:, at] = x[:, at] + new
            if n < FINE_DEGREE - 2:
                e[:, at] = ev
                dst[:, at] = new

        blocks(*STEPS[level][n], step, body)


def x_up4(v):
    moved = roll(v, -32, 2)
    after = jnp.concatenate([moved[1:], moved[:1]], axis=0)
    return jnp.where(lane_iota(v.shape) < 96, moved, after)


def x_dn4(v):
    moved = roll(v, 32, 2)
    before = jnp.concatenate([moved[-1:], moved[:-1]], axis=0)
    return jnp.where(lane_iota(v.shape) >= 32, moved, before)


def faces4(a, fx, fy, fz, inv):
    nb, rows, _ = a.shape
    blk = lax.broadcasted_iota(jnp.int32, a.shape, 0)
    row = lax.broadcasted_iota(jnp.int32, a.shape, 1)
    lane = lane_iota(a.shape)
    half = 0.5 * a
    total = jnp.zeros_like(a)
    for up, dn, last, start, out in (
        (x_up4, x_dn4, (blk == nb - 1) & (lane >= 96), (blk == 0) & (lane < 32), fx),
        (lambda v: roll(v, -1, 1), lambda v: roll(v, 1, 1), row == rows - 1, row == 0, fy),
        (lambda v: roll(v, -1, 2), lambda v: roll(v, 1, 2), lane % 32 == 31, lane % 32 == 0, fz),
    ):
        inner = half + 0.5 * up(a)
        off = jnp.where(last, 0.0, inner)
        out[...] = off
        total = total + jnp.where(last, half, inner) + jnp.where(start, half, dn(off))
    inv[...] = 1.0 / total


def smooth4(b, fx, fy, fz, inv):
    first, keeps, pushes = cheb_steps(COARSE_DEGREE, LOW_COARSE, HIGH_BOUND)
    e = b * inv[...] * (1.0 / SCALE[4])
    x = d = e * first
    for keep, push in zip(keeps, pushes):
        gx, gy, gz = fx[...], fy[...], fz[...]
        near = gx * x_up4(d) + x_dn4(gx * d)
        near = near + gy * roll(d, -1, 1) + roll(gy * d, 1, 1)
        near = near + gz * roll(d, -1, 2) + roll(gz * d, 1, 2)
        e = e - d + inv[...] * near
        d = keep * d + push * e
        x = x + d
    return x


def build4(src, stride, offset, core, gx_n, gy_n):
    count = gx_n * gy_n * 2
    gap = stride // 2
    pairs = src[pl.ds(offset, count, stride), :] + src[pl.ds(offset + gap, count, stride), :]
    pairs = pairs.reshape(gx_n // 2, 2, gy_n * 2, 128)
    out = None
    for odd in range(2):
        mat = select_matrix(
            lambda r, c: c == odd * 64 + (r // 64) * 32 + core * 16 + (r % 32) // 2, 0.125
        )
        part = dot(pairs[:, odd].reshape(gx_n * gy_n, 128), mat)
        out = part if out is None else out + part
    return out.reshape(gx_n // 2, gy_n * 2, 128)


def window3(src, dst, field, fields, core, pos, gx_n, gy_n, pad):
    for bx in range(5):
        for by in range(6):
            ix = pos[1] + (bx - 2)
            iy = pos[2] + (by - 2)
            ok = (ix >= 0) & (ix < gx_n) & (iy >= 0) & (iy < gy_n)
            at = jnp.clip(ix, 0, gx_n - 1) * gy_n + jnp.clip(iy, 0, gy_n - 1)
            if fields == 1:
                tile = src[at]
            else:
                tile = src[at, pl.ds(field, 4, fields), :]
            dst[core, bx + pad, by * 4:by * 4 + 4, :] = jnp.where(ok, tile, 0.0)


def restrict_to2(read_pair, out):
    even = jnp.concatenate([read_pair(2 * k) for k in range(4)], axis=0)
    odd = jnp.concatenate([read_pair(2 * k + 1) for k in range(4)], axis=0)
    low = select_matrix(lambda r, c: c == r // 2, 0.125)
    high = select_matrix(lambda r, c: c == 64 + r // 2, 0.125)
    both = dot(even, low) + dot(odd, high)
    for k in range(4):
        out(k, both[k * 8:k * 8 + 8])


def restrict_to3(read_rows):
    total = None
    for k in range(4):
        mat = select_matrix(lambda r, c: c == k * 32 + (r % 64) // 2, 0.125)
        part = dot(read_rows(k), mat)
        total = part if total is None else total + part
    return total


class Copies:
    def __init__(self, sems):
        self.sems, self.made = sems, []

    def start(self, src, dst):
        copy = pltpu.make_async_copy(src, dst, self.sems.at[len(self.made)])
        copy.start()
        self.made.append(copy)
        return copy

    def finish(self):
        for copy in self.made:
            copy.wait()


def position():
    return tuple(lax.axis_index(name) for name in ("grp", "gx", "gy"))


def put_pair(even, first, second, at, up, down):
    first[at] = jnp.where(even, up, down)
    second[at] = jnp.where(even, down, up)


def is_even(index):
    return lax.rem(index, 2) == 0


def prepare_kernel(a_hbm, b_hbm, own, own_hbm, first, second, slots, a, b, sems):
    even = is_even(position()[1])
    copies = Copies(sems)
    copies.start(a_hbm, a)
    copies.start(b_hbm, b)
    for f, src in enumerate((a, b)):
        copies.made[f].wait()
        for t in range(2):
            own[pl.ds(f * 32 + t, 16, 2)] = src[:, t * 8:t * 8 + 8, :]
            put_pair(
                even, first, second, pl.ds(f * 12 + t, 6, 2),
                src[10:16, t * 8:t * 8 + 8, :], src[0:6, t * 8:t * 8 + 8, :],
            )

        def read_pair(k):
            total = None
            for x in (2 * k, 2 * k + 1):
                part = src[x, pl.ds(0, 8, 2), :] + src[x, pl.ds(1, 8, 2), :]
                total = part if total is None else total + part
            return total

        values = []

        def out(k, value):
            own[64 + f * 4 + k] = value
            values.append(value)

        restrict_to2(read_pair, out)
        for k in range(3):
            put_pair(even, first, second, 24 + f * 3 + k, values[k + 1], values[k])
        slots[0, pl.ds(f, 4, 2), :] = restrict_to3(
            lambda k: own[64 + f * 4 + k, pl.ds(0, 4, 2), :] + own[64 + f * 4 + k, pl.ds(1, 4, 2), :]
        )
    keep = copies.start(own, own_hbm)
    slots[1:] = jnp.broadcast_to(slots[0:1], (slots.shape[0] - 1, 8, 128))
    keep.wait()


def sides_kernel(nf, own, one, two, first, second):
    core, gx, gy = position()
    even_x, even_y = is_even(gx), is_even(gy)
    if nf == 2:
        mine = lambda i: own[i]
    else:
        mine = lambda i: own[core, i]

    def lower(i):
        return jnp.where(even_x, two[i], one[i])

    def upper(i):
        return jnp.where(even_x, one[i], two[i])

    for f in range(nf):
        for i in range(28):
            if i < 6:
                low, high = lower(f * 12 + 2 * i), lower(f * 12 + 2 * i + 1)
            elif i >= 22:
                low, high = upper(f * 12 + 2 * (i - 22)), upper(f * 12 + 2 * (i - 22) + 1)
            else:
                low, high = mine(f * 32 + 2 * (i - 6)), mine(f * 32 + 2 * (i - 6) + 1)
            put_pair(even_y, first, second, f * 28 + i, high, low)
        for i in range(10):
            if i < 3:
                tile = lower(nf * 12 + f * 3 + i)
            elif i >= 7:
                tile = upper(nf * 12 + f * 3 + i - 7)
            else:
                tile = mine(nf * 32 + f * 4 + i - 3)
            first[nf * 28 + f * 10 + i] = tile
            second[nf * 28 + f * 10 + i] = tile


def spread(nf, f, core, even_x, even_y, x_one, x_two, y_one, y_two, fine, mid, pad):
    lower = lambda i: jnp.where(even_x, x_two[i], x_one[i])
    upper = lambda i: jnp.where(even_x, x_one[i], x_two[i])
    below = lambda i: jnp.where(even_y, y_two[i], y_one[i])
    above = lambda i: jnp.where(even_y, y_one[i], y_two[i])
    for i in range(28):
        fine[core, i, 0:8, :] = below(f * 28 + i)
        fine[core, i, 24:32, :] = above(f * 28 + i)
        for t in range(2):
            if i < 6:
                tile = lower(f * 12 + 2 * i + t)
            elif i >= 22:
                tile = upper(f * 12 + 2 * (i - 22) + t)
            else:
                continue
            fine[core, i, 8 + 8 * t:16 + 8 * t, :] = tile
    base = nf * 28 + f * 10
    for i in range(10):
        mid[core, i + pad, 0:8, :] = below(base + i)
        mid[core, i + pad, 16:24, :] = above(base + i)
        if i < 3:
            tile = lower(nf * 12 + f * 3 + i)
        elif i >= 7:
            tile = upper(nf * 12 + f * 3 + i - 7)
        else:
            continue
        mid[core, i + pad, 8:16, :] = tile


def spread_own(nf, f, core, own, fine, mid, pad):
    for i in range(16):
        for t in range(2):
            fine[core, i + 6, 8 + 8 * t:16 + 8 * t, :] = own[f * 32 + 2 * i + t]
    for i in range(4):
        mid[core, i + 3 + pad, 8:16, :] = own[nf * 32 + f * 4 + i]


def add_coarsest(pos, gx_n, gy_n, x4, x3, out):
    gx, gy = pos[1], pos[2]
    yrow = lax.broadcasted_iota(jnp.int32, (24, gy_n * 2), 0)
    ycol = lax.broadcasted_iota(jnp.int32, (24, gy_n * 2), 1)
    rows = jnp.where(ycol == (4 * gy - 8 + yrow + 1024) // 2 - 512, 1.0, 0.0).astype(F32)
    for bx in (1, 2, 3):
        ix = gx + (bx - 2)
        ok = (ix >= 0) & (ix < gx_n)
        at = jnp.clip(ix, 0, gx_n - 1)
        odd = lax.rem(at, 2)
        picked = select_rows(rows, x4[lax.div(at, 2)])
        for c in range(2):
            mat = select_matrix(
                lambda r, k: r == odd * 64 + (k // 64) * 32 + c * 16 + (k % 32) // 2, 1.0
            )
            out[c, bx - 1] = x3[c, bx] + jnp.where(ok, dot(picked, mat), 0.0)


def select_rows(rows, v):
    high = v.astype(jnp.bfloat16)
    rest = v - high.astype(F32)
    mid = rest.astype(jnp.bfloat16)
    low = (rest - mid.astype(F32)).astype(jnp.bfloat16)
    rows = rows.astype(jnp.bfloat16)
    mul = lambda w: jnp.dot(rows, w, preferred_element_type=F32)
    return mul(high) + (mul(mid) + mul(low))


def combine(sum3, c2, x2, tmp3, tmp2):
    for c in range(2):
        for bx in range(3):
            tmp3[c, bx, pl.ds(0, 12, 2), :] = sum3[c, bx, 4:16, :]
            tmp3[c, bx, pl.ds(1, 12, 2), :] = sum3[c, bx, 4:16, :]
    for low in range(4):
        mat = select_matrix(lambda r, k: r == low * 32 + (k % 64) // 2, 1.0)
        for i in [i for i in range(2, 8) if (i + 5) % 4 == low]:
            bx = (i + 5) // 4 - 1
            part = dot(tmp3[:, bx].reshape(48, 128), mat).reshape(2, 24, 128)
            x2[:, i - 2] = c2[:, i] + part
    for low in range(2):
        mat = select_matrix(lambda r, k: r == low * 64 + k // 2, 1.0)
        part = dot(x2[...].reshape(2 * 6 * 24, 128), mat).reshape(2, 6, 24, 128)
        for i in range(6):
            piece = part[:, i, 4:20, :]
            tmp2[:, 2 * i + low, pl.ds(0, 16, 2), :] = piece
            tmp2[:, 2 * i + low, pl.ds(1, 16, 2), :] = piece


def split3(ref):
    return [ref.at[k] for k in range(6)], ref.at[6]


def coarse_first_kernel(
    gx_n, gy_n, r3_a, r3_b, r3f_a, r3f_b, sum3, w3_hbm, w4_hbm,
    w3, w4, a3, b3, e3, d3, o3, c3, x4, sems,
):
    pos = position()
    core = pos[0]
    weights3, inv3 = split3(w3)
    fx4, fy4, fz4, inv4 = (w4.at[k] for k in range(4))
    copies = Copies(sems)
    for c in range(2):
        a3[c, 0] = jnp.zeros((24, 128), F32)
        a3[c, 6] = jnp.zeros((24, 128), F32)
    for c, src in ((core, r3_a), (1 - core, r3_b)):
        window3(src, a3, 0, 2, c, pos, gx_n, gy_n, 1)
        window3(src, b3, 1, 2, c, pos, gx_n, gy_n, 0)
    a4 = build4(r3f_a, 4, 0, core, gx_n, gy_n) + build4(r3f_b, 4, 0, 1 - core, gx_n, gy_n)
    b4 = build4(r3f_a, 4, 1, core, gx_n, gy_n) + build4(r3f_b, 4, 1, 1 - core, gx_n, gy_n)
    faces4(a4, fx4, fy4, fz4, inv4)
    copies.start(w4, w4_hbm)
    faces(3, a3, weights3, inv3, None)
    copies.start(w3, w3_hbm)
    x4[...] = smooth4(b4, fx4, fy4, fz4, inv4)
    smooth(3, b3, weights3, inv3, e3, d3, o3, c3)
    add_coarsest(pos, gx_n, gy_n, x4, c3, sum3)
    copies.finish()


def coarse_second_kernel(
    gx_n, gy_n, r3_a, r3_b, r3f_a, r3f_b, w3_hbm, w4_hbm, sum3,
    w3, w4, b3, e3, d3, o3, c3, x4, sems,
):
    pos = position()
    core = pos[0]
    copies = Copies(sems)
    copies.start(w4_hbm, w4)
    copies.start(w3_hbm, w3)
    weights3, inv3 = split3(w3)
    window3(r3_a, b3, 0, 1, core, pos, gx_n, gy_n, 0)
    window3(r3_b, b3, 0, 1, 1 - core, pos, gx_n, gy_n, 0)
    b4 = build4(r3f_a, 2, 0, core, gx_n, gy_n) + build4(r3f_b, 2, 0, 1 - core, gx_n, gy_n)
    copies.made[0].wait()
    x4[...] = smooth4(b4, *(w4.at[k] for k in range(4)))
    copies.made[1].wait()
    smooth(3, b3, weights3, inv3, e3, d3, o3, c3)
    add_coarsest(pos, gx_n, gy_n, x4, c3, sum3)


def first_kernel(
    own_a, x_one_a, x_two_a, y_one_a, y_two_a, own_b, x_one_b, x_two_b, y_one_b, y_two_b, sum3,
    w1_hbm, w2_hbm, x1_hbm, right_hbm, own_hbm, own, first, second, slots,
    w1, w2, x1, own_s, a1, b1, e1, d1, o1, a2, b2, e2, d2, o2, c2, s2, tmp3, tmp2, rest, sems,
):
    core, gx, gy = position()
    even_x, even_y = is_even(gx), is_even(gy)
    copies = Copies(sems)
    copies.start(own_a, own_s)
    halves = (
        (core, (x_one_a, x_two_a, y_one_a, y_two_a)),
        (1 - core, (x_one_b, x_two_b, y_one_b, y_two_b)),
    )
    weights1, inv1 = split3(w1)
    diag1 = w1.at[7]
    weights2, inv2 = split3(w2)
    for c in range(2):
        a2[c, 0] = jnp.zeros((24, 128), F32)
        a2[c, 11] = jnp.zeros((24, 128), F32)
    for c, parts in halves:
        spread(2, 0, c, even_x, even_y, *parts, a1, a2, 1)
        spread(2, 1, c, even_x, even_y, *parts, b1, b2, 0)
    spread_own(2, 0, 1 - core, own_b, a1, a2, 1)
    spread_own(2, 1, 1 - core, own_b, b1, b2, 0)
    copies.finish()
    spread_own(2, 0, core, own_s, a1, a2, 1)
    spread_own(2, 1, core, own_s, b1, b2, 0)
    out = Copies(sems.at[pl.ds(1, 5)])
    out.start(b1.at[:, 6:22, 8:24, :], right_hbm)
    faces(2, a2, weights2, inv2, None)
    out.start(w2, w2_hbm)
    faces(1, a1, weights1, inv1, diag1)
    out.start(w1, w1_hbm)
    smooth(2, b2, weights2, inv2, e2, d2, o2, c2)
    smooth(1, b1, weights1, inv1, e1, d1, o1, x1)
    combine(sum3, c2, s2, tmp3, tmp2)

    def finish(i, _):
        x1[:, i] = DAMPING * (x1[:, i] + tmp2[:, i // 2 - 1])
        return 0

    lax.fori_loop(5, 23, finish, 0)
    out.start(x1, x1_hbm)

    def residual(i):
        mid, near = weighted(1, i, 2, x1, weights1)
        at = pl.ds(i, 2)
        res = b1[:, at] - diag1[:, at] * (mid - near)
        rest[:, pl.ds(i - 6, 2)] = res[:, :, 8:24, :]

    blocks(6, 22, 2, residual)
    for c in range(2):
        for t in range(2):
            own[c, pl.ds(t, 16, 2)] = rest[c, :, t * 8:t * 8 + 8, :]

        def read_pair(k):
            total = None
            for x in (2 * k, 2 * k + 1):
                part = rest[c, x, pl.ds(0, 8, 2), :] + rest[c, x, pl.ds(1, 8, 2), :]
                total = part if total is None else total + part
            return total

        def put(k, value):
            own[c, 32 + k] = value

        restrict_to2(read_pair, put)
    out.start(own, own_hbm)
    for i in range(12):
        put_pair(even_x, first, second, i, own[core, 20 + i], own[core, i])
    for i in range(3):
        put_pair(even_x, first, second, 12 + i, own[core, 33 + i], own[core, 32 + i])
    slots[0] = restrict_to3(
        lambda k: own[core, 32 + k, pl.ds(0, 4, 2), :] + own[core, 32 + k, pl.ds(1, 4, 2), :]
    )
    slots[1:] = jnp.broadcast_to(slots[0:1], (slots.shape[0] - 1, 4, 128))
    out.finish()


def second_kernel(
    own_hbm, w1_hbm, w2_hbm, x1_hbm, right_hbm,
    x_one_a, x_two_a, y_one_a, y_two_a, x_one_b, x_two_b, y_one_b, y_two_b, sum3,
    out_x, out_r,
    w1, w2, x1, right, own, b1, e1, d1, o1, c1, b2, e2, d2, o2, c2, s2, tmp3, tmp2, rest, sems,
):
    core, gx, gy = position()
    even_x, even_y = is_even(gx), is_even(gy)
    copies = Copies(sems)
    for src, dst in (
        (own_hbm, own), (w2_hbm, w2), (w1_hbm, w1), (x1_hbm, x1), (right_hbm, right)
    ):
        copies.start(src, dst)
    weights1, inv1 = split3(w1)
    diag1 = w1.at[7]
    weights2, inv2 = split3(w2)
    spread(1, 0, core, even_x, even_y, x_one_a, x_two_a, y_one_a, y_two_a, b1, b2, 0)
    spread(1, 0, 1 - core, even_x, even_y, x_one_b, x_two_b, y_one_b, y_two_b, b1, b2, 0)
    copies.made[0].wait()
    for c in range(2):
        spread_own(1, 0, c, own.at[c], b1, b2, 0)
    copies.made[1].wait()
    smooth(2, b2, weights2, inv2, e2, d2, o2, c2)
    copies.made[2].wait()
    smooth(1, b1, weights1, inv1, e1, d1, o1, c1)
    copies.made[3].wait()
    copies.made[4].wait()
    combine(sum3, c2, s2, tmp3, tmp2)

    def finish(i, _):
        c1[:, i] = x1[:, i] + DAMPING * (c1[:, i] + tmp2[:, i // 2 - 1])
        return 0

    lax.fori_loop(5, 23, finish, 0)
    field = copies.start(c1.at[core, 6:22, 8:24, :], out_x)

    def residual(i):
        mid, near = weighted(1, i, 2, c1, weights1)
        res = diag1[:, pl.ds(i, 2)] * (mid - near)
        at = pl.ds(i - 6, 2)
        rest[:, at] = right[:, at] - res[:, :, 8:24, :]

    blocks(6, 22, 2, residual)
    done = copies.start(rest.at[core], out_r)
    field.wait()
    done.wait()


def call(kernel, outs, scratch, *args, hbm_in=(), hbm_out=(), sems=0, limit=8):
    vmem = pl.BlockSpec(memory_space=pltpu.VMEM)
    hbm = pl.BlockSpec(memory_space=pltpu.HBM)
    specs = [vmem for _ in args]
    args = list(args)
    for i in hbm_in:
        specs[i] = hbm
        args[i] = pltpu.with_memory_space_constraint(args[i], pltpu.HBM)
    scratch = [pltpu.VMEM(s, F32) for s in scratch]
    if sems:
        scratch.append(pltpu.SemaphoreType.DMA((sems,)))
    return pl.pallas_call(
        kernel,
        out_shape=[
            pltpu.HBM(s, F32) if i in hbm_out else jax.ShapeDtypeStruct(s, F32)
            for i, s in enumerate(outs)
        ],
        in_specs=specs,
        out_specs=[hbm if i in hbm_out else vmem for i in range(len(outs))],
        scratch_shapes=scratch,
        compiler_params=pltpu.CompilerParams(vmem_limit_bytes=limit * 1024 * 1024),
        interpret=INTERPRET,
    )(*args)


def trade(first, second, axis):
    size = lax.axis_size(axis)
    pairs = [(i, i ^ 1) for i in range(size)]
    others = [(i, i - 1 if i % 2 == 0 else i + 1) for i in range(1, size - 1)]
    one = lax.ppermute(first, axis, pairs)
    two = lax.ppermute(second, axis, others)
    return one, two


def swap(x):
    return lax.ppermute(x, "grp", [(0, 1), (1, 0)])


def everywhere(slots):
    return lax.all_to_all(slots, ("gx", "gy"), 0, 0, tiled=True)


def on_device(right_side, coefficient):
    gx_n, gy_n = lax.axis_size("gx"), lax.axis_size("gy")
    count = gx_n * gy_n
    s1, s2, s3 = (2, 28, 32, 128), (2, 10, 24, 128), (2, 5, 24, 128)
    p2, p3 = (2, 12, 24, 128), (2, 7, 24, 128)
    s4 = (gx_n // 2, gy_n * 2, 128)
    sum3 = (2, 3, 24, 128)
    tmps = [(2, 6, 24, 128), sum3, (2, 12, 32, 128), (2, 16, 16, 128)]

    own, own_kept, first, second, slots = call(
        prepare_kernel,
        [(72, 8, 128), (72, 8, 128), (30, 8, 128), (30, 8, 128), (count, 8, 128)],
        [(16, 16, 128)] * 2, coefficient, right_side, hbm_in=(0, 1), hbm_out=(1,), sems=3,
    )
    own_o = swap(own_kept)
    x_one, x_two = trade(first, second, "gx")
    r3 = everywhere(slots)
    x_one_o, x_two_o = swap(x_one), swap(x_two)
    r3_o = swap(r3)
    first, second = call(
        functools.partial(sides_kernel, 2), [(76, 8, 128)] * 2, [], own, x_one, x_two
    )
    y_one, y_two = trade(first, second, "gy")
    y_one_o, y_two_o = swap(y_one), swap(y_two)
    flat = (count * 8, 128)
    w1s, w2s, w3s, w4s = (8,) + s1, (7,) + s2, (7,) + s3, (4,) + s4
    c3, w3, w4 = call(
        functools.partial(coarse_first_kernel, gx_n, gy_n), [sum3, w3s, w4s],
        [w3s, w4s, p3, s3, s3, s3, s3, s3, s4],
        r3, r3_o, r3.reshape(flat), r3_o.reshape(flat), hbm_out=(1, 2), sems=2, limit=12,
    )
    w1, w2, x1, right, own_kept, own, first, second, slots = call(
        first_kernel,
        [w1s, w2s, s1, (2, 16, 16, 128), (2, 36, 8, 128), (2, 36, 8, 128), (15, 8, 128),
         (15, 8, 128), (count, 4, 128)],
        [w1s, w2s, s1, (72, 8, 128), s1, s1, s1, s1, s1, p2, s2, s2, s2, s2, s2] + tmps,
        own_kept, x_one, x_two, y_one, y_two, own_o, x_one_o, x_two_o, y_one_o, y_two_o, c3,
        hbm_in=(0,), hbm_out=(0, 1, 2, 3, 4), sems=6, limit=28,
    )
    x_one, x_two = trade(first, second, "gx")
    r3 = everywhere(slots)
    x_one_o, x_two_o = swap(x_one), swap(x_two)
    r3_o = swap(r3)
    first, second = call(
        functools.partial(sides_kernel, 1), [(38, 8, 128)] * 2, [], own, x_one, x_two
    )
    y_one, y_two = trade(first, second, "gy")
    y_one_o, y_two_o = swap(y_one), swap(y_two)
    flat = (count * 4, 128)
    (c3,) = call(
        functools.partial(coarse_second_kernel, gx_n, gy_n),
        [sum3], [w3s, w4s, s3, s3, s3, s3, s3, s4],
        r3, r3_o, r3.reshape(flat), r3_o.reshape(flat), w3, w4,
        hbm_in=(4, 5), sems=2, limit=12,
    )
    solution_field, residual = call(
        second_kernel, [(16, 16, 128)] * 2,
        [w1s, w2s, s1, (2, 16, 16, 128), (2, 36, 8, 128), s1, s1, s1, s1, s1, s2, s2, s2, s2, s2]
        + tmps,
        own_kept, w1, w2, x1, right,
        x_one, x_two, y_one, y_two, x_one_o, x_two_o, y_one_o, y_two_o, c3,
        hbm_in=(0, 1, 2, 3, 4), hbm_out=(0, 1), sems=7, limit=28,
    )
    return solution_field, residual


def solution(mesh):
    placed = P("gx", "gy", "grp")

    return jax.shard_map(
        on_device, mesh=mesh, in_specs=(placed, placed), out_specs=(placed, placed),
        check_vma=False,
    )
```

```python
import functools

import jax
import jax.numpy as jnp
from jax import lax
from jax.experimental import pallas as pl
from jax.experimental.pallas import tpu as pltpu
from jax.sharding import PartitionSpec as P


FINE_DEGREE = 5
COARSE_DEGREE = 16
LOW_FINE = 0.2
LOW_COARSE = 0.02
HIGH_BOUND = 2.0
DAMPING = 0.5

F32 = jnp.float32
INTERPRET = False
LANES_X = {1: 1, 2: 2, 3: 4}
HELD = {1: (1, 27), 2: (0, 10), 3: (0, 5)}
STEPS = {
    1: ((2, 26), (3, 25), (4, 24), (5, 23)),
    2: ((1, 9), (1, 9), (2, 8), (2, 8)),
    3: ((1, 4),) * 4,
}
CHUNK = {1: 2, 2: 2, 3: 3}
PAD = {1: 0, 2: 1, 3: 1}
SCALE = {1: 1.0, 2: 0.25, 3: 0.0625, 4: 0.015625}


def cheb_steps(degree, low, high):
    theta = (high + low) / 2.0
    delta = (high - low) / 2.0
    sigma = theta / delta
    rho = 1.0 / sigma
    keeps = []
    pushes = []
    for _ in range(degree - 1):
        rho_new = 1.0 / (2.0 * sigma - rho)
        keeps.append(rho_new * rho)
        pushes.append(2.0 * rho_new / delta)
        rho = rho_new
    return (1.0 / theta, keeps, pushes)


def roll(x, shift, axis):
    size = x.shape[axis]
    return pltpu.roll(x, shift % size, axis)


def lane_iota(shape):
    return lax.broadcasted_iota(jnp.int32, shape, len(shape) - 1)


def dot(x, m):
    high = x.astype(jnp.bfloat16)
    rest = x - high.astype(F32)
    mid = rest.astype(jnp.bfloat16)
    low = (rest - mid.astype(F32)).astype(jnp.bfloat16)
    m = m.astype(jnp.bfloat16)
    mul = lambda v: jnp.dot(v, m, preferred_element_type=F32)
    return mul(high) + (mul(mid) + mul(low))


def select_matrix(fn, value):
    row = lax.broadcasted_iota(jnp.int32, (128, 128), 0)
    col = lax.broadcasted_iota(jnp.int32, (128, 128), 1)
    return jnp.where(fn(row, col), value, 0.0).astype(F32)


def neighbours(q, v):
    zz = 128 // q
    mid = v[:, 1:-1]
    lane = lane_iota(mid.shape)
    if q == 1:
        x_up, x_dn = v[:, 2:], v[:, :-2]
        for_up = for_dn = mid
    else:
        ups = roll(v[:, 1:], -zz, 3)
        dns = roll(v[:, :-1], zz, 3)
        x_up = jnp.where(lane < 128 - zz, ups[:, :-1], ups[:, 1:])
        x_dn = jnp.where(lane >= zz, dns[:, 1:], dns[:, :-1])
        for_up, for_dn = dns[:, 1:], ups[:, :-1]
    other = lambda w: jnp.concatenate([w[1:], w[:1]], axis=0)
    inner = lane % zz
    z_up = roll(jnp.where(inner == 0, other(for_up), mid), -1, 3)
    z_dn = roll(jnp.where(inner == zz - 1, other(for_dn), mid), 1, 3)
    return mid, (x_up, x_dn, roll(mid, -1, 2), roll(mid, 1, 2), z_up, z_dn)


def blocks(start, stop, step, body):
    if stop - start == step:
        body(start)
        return

    def run(n, _):
        body(start + n * step)
        return 0

    lax.fori_loop(0, (stop - start) // step, run, 0)


def faces(level, a, weights, inv, diag_ref):
    q, pad = LANES_X[level], PAD[level]
    zz = 128 // q
    first, last = HELD[level]
    step = 5 if level == 3 else 2

    def body(i):
        mid, near = neighbours(q, a[:, pl.ds(i + pad - 1, step + 2)])
        core = lax.broadcasted_iota(jnp.int32, mid.shape, 0)
        lane = lane_iota(mid.shape) % zz
        top = (core == 1) & (lane == zz - 1)
        bottom = (core == 0) & (lane == 0)
        x_up, x_dn, y_up, y_dn, z_up, z_dn = near
        z_up = jnp.where(top, 0.0, z_up)
        z_dn = jnp.where(bottom, 0.0, z_dn)
        near = (x_up, x_dn, y_up, y_dn, z_up, z_dn)
        total = 3.0 * mid + 0.5 * ((x_up + x_dn) + (y_up + y_dn) + (z_up + z_dn))
        inverse = jnp.where(mid > 0.0, 1.0 / total, 0.0)
        at = pl.ds(i, step)
        inv[:, at] = inverse
        half = 0.5 * inverse
        for k in range(6):
            w = half * (mid + near[k])
            if k == 4:
                w = jnp.where(top, 0.0, w)
            if k == 5:
                w = jnp.where(bottom, 0.0, w)
            weights[k][:, at] = w
        if diag_ref is not None:
            diag_ref[:, at] = total

    blocks(first, last, step, body)


def weighted(q, i, step, v, weights):
    mid, near = neighbours(q, v[:, pl.ds(i - 1, step + 2)])
    at = pl.ds(i, step)
    terms = [weights[k][:, at] * near[k] for k in range(6)]
    return mid, (terms[0] + terms[1]) + (terms[2] + terms[3]) + (terms[4] + terms[5])


def smooth(level, b, weights, inv, e, d, other, x):
    q = LANES_X[level]
    first, keeps, pushes = cheb_steps(FINE_DEGREE, LOW_FINE, HIGH_BOUND)
    step = CHUNK[level]

    def start(i):
        at = pl.ds(i, 5 if level == 3 else 2)
        ev = b[:, at] * inv[:, at] * (1.0 / SCALE[level])
        e[:, at] = ev
        d[:, at] = ev * first
        x[:, at] = ev * first

    blocks(*HELD[level], 5 if level == 3 else 2, start)
    if level > 1:
        for i in (HELD[level][0], HELD[level][1] - 1):
            other[:, i] = jnp.zeros_like(other[:, i])
    for n in range(FINE_DEGREE - 1):
        src, dst = (d, other) if n % 2 == 0 else (other, d)

        def body(i):
            at = pl.ds(i, step)
            mid, near = weighted(q, i, step, src, weights)
            ev = (e[:, at] - mid) + near
            new = keeps[n] * mid + pushes[n] * ev
            x[:, at] = x[:, at] + new
            if n < FINE_DEGREE - 2:
                e[:, at] = ev
                dst[:, at] = new

        blocks(*STEPS[level][n], step, body)


def x_up4(v):
    moved = roll(v, -32, 2)
    after = jnp.concatenate([moved[1:], moved[:1]], axis=0)
    return jnp.where(lane_iota(v.shape) < 96, moved, after)


def x_dn4(v):
    moved = roll(v, 32, 2)
    before = jnp.concatenate([moved[-1:], moved[:-1]], axis=0)
    return jnp.where(lane_iota(v.shape) >= 32, moved, before)


def faces4(a, fx, fy, fz, inv):
    nb, rows, _ = a.shape
    blk = lax.broadcasted_iota(jnp.int32, a.shape, 0)
    row = lax.broadcasted_iota(jnp.int32, a.shape, 1)
    lane = lane_iota(a.shape)
    half = 0.5 * a
    total = jnp.zeros_like(a)
    for up, dn, last, start, out in (
        (x_up4, x_dn4, (blk == nb - 1) & (lane >= 96), (blk == 0) & (lane < 32), fx),
        (lambda v: roll(v, -1, 1), lambda v: roll(v, 1, 1), row == rows - 1, row == 0, fy),
        (lambda v: roll(v, -1, 2), lambda v: roll(v, 1, 2), lane % 32 == 31, lane % 32 == 0, fz),
    ):
        inner = half + 0.5 * up(a)
        off = jnp.where(last, 0.0, inner)
        out[...] = off
        total = total + jnp.where(last, half, inner) + jnp.where(start, half, dn(off))
    inv[...] = 1.0 / total


def smooth4(b, fx, fy, fz, inv):
    first, keeps, pushes = cheb_steps(COARSE_DEGREE, LOW_COARSE, HIGH_BOUND)
    e = b * inv[...] * (1.0 / SCALE[4])
    x = d = e * first
    for keep, push in zip(keeps, pushes):
        gx, gy, gz = fx[...], fy[...], fz[...]
        near = gx * x_up4(d) + x_dn4(gx * d)
        near = near + gy * roll(d, -1, 1) + roll(gy * d, 1, 1)
        near = near + gz * roll(d, -1, 2) + roll(gz * d, 1, 2)
        e = e - d + inv[...] * near
        d = keep * d + push * e
        x = x + d
    return x


def build4(src, stride, offset, core, gx_n, gy_n):
    count = gx_n * gy_n * 2
    gap = stride // 2
    pairs = src[pl.ds(offset, count, stride), :] + src[pl.ds(offset + gap, count, stride), :]
    pairs = pairs.reshape(gx_n // 2, 2, gy_n * 2, 128)
    out = None
    for odd in range(2):
        mat = select_matrix(
            lambda r, c: c == odd * 64 + (r // 64) * 32 + core * 16 + (r % 32) // 2, 0.125
        )
        part = dot(pairs[:, odd].reshape(gx_n * gy_n, 128), mat)
        out = part if out is None else out + part
    return out.reshape(gx_n // 2, gy_n * 2, 128)


def window3(src, dst, field, fields, core, pos, gx_n, gy_n, pad):
    for bx in range(5):
        for by in range(6):
            ix = pos[1] + (bx - 2)
            iy = pos[2] + (by - 2)
            ok = (ix >= 0) & (ix < gx_n) & (iy >= 0) & (iy < gy_n)
            at = jnp.clip(ix, 0, gx_n - 1) * gy_n + jnp.clip(iy, 0, gy_n - 1)
            if fields == 1:
                tile = src[at]
            else:
                tile = src[at, pl.ds(field, 4, fields), :]
            dst[core, bx + pad, by * 4:by * 4 + 4, :] = jnp.where(ok, tile, 0.0)


def restrict_to2(read_pair, out):
    even = jnp.concatenate([read_pair(2 * k) for k in range(4)], axis=0)
    odd = jnp.concatenate([read_pair(2 * k + 1) for k in range(4)], axis=0)
    low = select_matrix(lambda r, c: c == r // 2, 0.125)
    high = select_matrix(lambda r, c: c == 64 + r // 2, 0.125)
    both = dot(even, low) + dot(odd, high)
    for k in range(4):
        out(k, both[k * 8:k * 8 + 8])


def restrict_to3(read_rows):
    total = None
    for k in range(4):
        mat = select_matrix(lambda r, c: c == k * 32 + (r % 64) // 2, 0.125)
        part = dot(read_rows(k), mat)
        total = part if total is None else total + part
    return total


class Copies:
    def __init__(self, sems):
        self.sems, self.made = sems, []

    def start(self, src, dst):
        copy = pltpu.make_async_copy(src, dst, self.sems.at[len(self.made)])
        copy.start()
        self.made.append(copy)
        return copy

    def finish(self):
        for copy in self.made:
            copy.wait()


def position():
    return tuple(lax.axis_index(name) for name in ("grp", "gx", "gy"))


def put_pair(even, first, second, at, up, down):
    first[at] = jnp.where(even, up, down)
    second[at] = jnp.where(even, down, up)


def is_even(index):
    return lax.rem(index, 2) == 0


def prepare_kernel(a_hbm, b_hbm, own, mid_hbm, first, second, slots, a, b, sems):
    even = is_even(position()[1])
    copies = Copies(sems)
    copies.start(a_hbm, a)
    copies.start(b_hbm, b)
    for f, src in enumerate((a, b)):
        copies.made[f].wait()

        def read_pair(k):
            total = None
            for x in (2 * k, 2 * k + 1):
                part = src[x, pl.ds(0, 8, 2), :] + src[x, pl.ds(1, 8, 2), :]
                total = part if total is None else total + part
            return total

        values = []

        def out(k, value):
            own[64 + f * 4 + k] = value
            values.append(value)

        restrict_to2(read_pair, out)
        for k in range(3):
            put_pair(even, first, second, 24 + f * 3 + k, values[k + 1], values[k])
    keep = copies.start(own.at[64:72], mid_hbm)
    for f, src in enumerate((a, b)):
        for t in range(2):
            own[pl.ds(f * 32 + t, 16, 2)] = src[:, t * 8:t * 8 + 8, :]
            put_pair(
                even, first, second, pl.ds(f * 12 + t, 6, 2),
                src[10:16, t * 8:t * 8 + 8, :], src[0:6, t * 8:t * 8 + 8, :],
            )
        slots[0, pl.ds(f, 4, 2), :] = restrict_to3(
            lambda k: own[64 + f * 4 + k, pl.ds(0, 4, 2), :] + own[64 + f * 4 + k, pl.ds(1, 4, 2), :]
        )
    slots[1:] = jnp.broadcast_to(slots[0:1], (slots.shape[0] - 1, 8, 128))
    keep.wait()


def sides_kernel(nf, own, one, two, first, second):
    core, gx, gy = position()
    even_x, even_y = is_even(gx), is_even(gy)
    if nf == 2:
        mine = lambda i: own[i]
    else:
        mine = lambda i: own[core, i]

    def lower(i):
        return jnp.where(even_x, two[i], one[i])

    def upper(i):
        return jnp.where(even_x, one[i], two[i])

    for f in range(nf):
        for i in range(28):
            if i < 6:
                low, high = lower(f * 12 + 2 * i), lower(f * 12 + 2 * i + 1)
            elif i >= 22:
                low, high = upper(f * 12 + 2 * (i - 22)), upper(f * 12 + 2 * (i - 22) + 1)
            else:
                low, high = mine(f * 32 + 2 * (i - 6)), mine(f * 32 + 2 * (i - 6) + 1)
            put_pair(even_y, first, second, f * 28 + i, high, low)
        for i in range(10):
            if i < 3:
                tile = lower(nf * 12 + f * 3 + i)
            elif i >= 7:
                tile = upper(nf * 12 + f * 3 + i - 7)
            else:
                tile = mine(nf * 32 + f * 4 + i - 3)
            first[nf * 28 + f * 10 + i] = tile
            second[nf * 28 + f * 10 + i] = tile


def spread(nf, f, core, even_x, even_y, x_one, x_two, y_one, y_two, fine, mid, pad):
    lower = lambda i: jnp.where(even_x, x_two[i], x_one[i])
    upper = lambda i: jnp.where(even_x, x_one[i], x_two[i])
    below = lambda i: jnp.where(even_y, y_two[i], y_one[i])
    above = lambda i: jnp.where(even_y, y_one[i], y_two[i])
    for i in range(28):
        fine[core, i, 0:8, :] = below(f * 28 + i)
        fine[core, i, 24:32, :] = above(f * 28 + i)
        for t in range(2):
            if i < 6:
                tile = lower(f * 12 + 2 * i + t)
            elif i >= 22:
                tile = upper(f * 12 + 2 * (i - 22) + t)
            else:
                continue
            fine[core, i, 8 + 8 * t:16 + 8 * t, :] = tile
    base = nf * 28 + f * 10
    for i in range(10):
        mid[core, i + pad, 0:8, :] = below(base + i)
        mid[core, i + pad, 16:24, :] = above(base + i)
        if i < 3:
            tile = lower(nf * 12 + f * 3 + i)
        elif i >= 7:
            tile = upper(nf * 12 + f * 3 + i - 7)
        else:
            continue
        mid[core, i + pad, 8:16, :] = tile


def spread_own(nf, f, core, own, fine, mid, pad):
    for i in range(16):
        for t in range(2):
            fine[core, i + 6, 8 + 8 * t:16 + 8 * t, :] = own[f * 32 + 2 * i + t]
    for i in range(4):
        mid[core, i + 3 + pad, 8:16, :] = own[nf * 32 + f * 4 + i]


def add_coarsest(pos, gx_n, gy_n, x4, x3, out):
    gx, gy = pos[1], pos[2]
    yrow = lax.broadcasted_iota(jnp.int32, (24, gy_n * 2), 0)
    ycol = lax.broadcasted_iota(jnp.int32, (24, gy_n * 2), 1)
    rows = jnp.where(ycol == (4 * gy - 8 + yrow + 1024) // 2 - 512, 1.0, 0.0).astype(F32)
    for bx in (1, 2, 3):
        ix = gx + (bx - 2)
        ok = (ix >= 0) & (ix < gx_n)
        at = jnp.clip(ix, 0, gx_n - 1)
        odd = lax.rem(at, 2)
        picked = select_rows(rows, x4[lax.div(at, 2)])
        for c in range(2):
            mat = select_matrix(
                lambda r, k: r == odd * 64 + (k // 64) * 32 + c * 16 + (k % 32) // 2, 1.0
            )
            out[c, bx - 1] = x3[c, bx] + jnp.where(ok, dot(picked, mat), 0.0)


def select_rows(rows, v):
    high = v.astype(jnp.bfloat16)
    rest = v - high.astype(F32)
    mid = rest.astype(jnp.bfloat16)
    low = (rest - mid.astype(F32)).astype(jnp.bfloat16)
    rows = rows.astype(jnp.bfloat16)
    mul = lambda w: jnp.dot(rows, w, preferred_element_type=F32)
    return mul(high) + (mul(mid) + mul(low))


def combine(sum3, c2, x2, tmp3, tmp2):
    for c in range(2):
        for bx in range(3):
            tmp3[c, bx, pl.ds(0, 12, 2), :] = sum3[c, bx, 4:16, :]
            tmp3[c, bx, pl.ds(1, 12, 2), :] = sum3[c, bx, 4:16, :]
    for low in range(4):
        mat = select_matrix(lambda r, k: r == low * 32 + (k % 64) // 2, 1.0)
        for i in [i for i in range(2, 8) if (i + 5) % 4 == low]:
            bx = (i + 5) // 4 - 1
            part = dot(tmp3[:, bx].reshape(48, 128), mat).reshape(2, 24, 128)
            x2[:, i - 2] = c2[:, i] + part
    for low in range(2):
        mat = select_matrix(lambda r, k: r == low * 64 + k // 2, 1.0)
        part = dot(x2[...].reshape(2 * 6 * 24, 128), mat).reshape(2, 6, 24, 128)
        for i in range(6):
            piece = part[:, i, 4:20, :]
            tmp2[:, 2 * i + low, pl.ds(0, 16, 2), :] = piece
            tmp2[:, 2 * i + low, pl.ds(1, 16, 2), :] = piece


def split3(ref):
    return [ref.at[k] for k in range(6)], ref.at[6]


def coarse_first_kernel(
    gx_n, gy_n, r3_a, r3_b, r3f_a, r3f_b, sum3, w3_hbm, w4_hbm,
    w3, w4, a3, b3, e3, d3, o3, c3, x4, sems,
):
    pos = position()
    core = pos[0]
    weights3, inv3 = split3(w3)
    fx4, fy4, fz4, inv4 = (w4.at[k] for k in range(4))
    copies = Copies(sems)
    for c in range(2):
        a3[c, 0] = jnp.zeros((24, 128), F32)
        a3[c, 6] = jnp.zeros((24, 128), F32)
    for c, src in ((core, r3_a), (1 - core, r3_b)):
        window3(src, a3, 0, 2, c, pos, gx_n, gy_n, 1)
        window3(src, b3, 1, 2, c, pos, gx_n, gy_n, 0)
    a4 = build4(r3f_a, 4, 0, core, gx_n, gy_n) + build4(r3f_b, 4, 0, 1 - core, gx_n, gy_n)
    b4 = build4(r3f_a, 4, 1, core, gx_n, gy_n) + build4(r3f_b, 4, 1, 1 - core, gx_n, gy_n)
    faces4(a4, fx4, fy4, fz4, inv4)
    copies.start(w4, w4_hbm)
    faces(3, a3, weights3, inv3, None)
    copies.start(w3, w3_hbm)
    x4[...] = smooth4(b4, fx4, fy4, fz4, inv4)
    smooth(3, b3, weights3, inv3, e3, d3, o3, c3)
    add_coarsest(pos, gx_n, gy_n, x4, c3, sum3)
    copies.finish()


def coarse_second_kernel(
    gx_n, gy_n, r3_a, r3_b, r3f_a, r3f_b, w3_hbm, w4_hbm, sum3,
    w3, w4, b3, e3, d3, o3, c3, x4, sems,
):
    pos = position()
    core = pos[0]
    copies = Copies(sems)
    copies.start(w4_hbm, w4)
    copies.start(w3_hbm, w3)
    weights3, inv3 = split3(w3)
    window3(r3_a, b3, 0, 1, core, pos, gx_n, gy_n, 0)
    window3(r3_b, b3, 0, 1, 1 - core, pos, gx_n, gy_n, 0)
    b4 = build4(r3f_a, 2, 0, core, gx_n, gy_n) + build4(r3f_b, 2, 0, 1 - core, gx_n, gy_n)
    copies.made[0].wait()
    x4[...] = smooth4(b4, *(w4.at[k] for k in range(4)))
    copies.made[1].wait()
    smooth(3, b3, weights3, inv3, e3, d3, o3, c3)
    add_coarsest(pos, gx_n, gy_n, x4, c3, sum3)


def first_kernel(
    a_hbm, b_hbm, mid_hbm,
    x_one_a, x_two_a, y_one_a, y_two_a, own_b, x_one_b, x_two_b, y_one_b, y_two_b, sum3,
    w1_hbm, w2_hbm, x1_hbm, right_hbm, own_hbm, own, first, second, slots,
    w1, w2, x1, a1, b1, e1, d1, o1, a2, b2, e2, d2, o2, c2, s2, tmp3, tmp2, rest, sems,
):
    core, gx, gy = position()
    even_x, even_y = is_even(gx), is_even(gy)
    copies = Copies(sems)
    copies.start(a_hbm, a1.at[core, 6:22, 8:24, :])
    copies.start(b_hbm, b1.at[core, 6:22, 8:24, :])
    copies.start(mid_hbm.at[0:4], a2.at[core, 4:8, 8:16, :])
    copies.start(mid_hbm.at[4:8], b2.at[core, 3:7, 8:16, :])
    halves = (
        (core, (x_one_a, x_two_a, y_one_a, y_two_a)),
        (1 - core, (x_one_b, x_two_b, y_one_b, y_two_b)),
    )
    weights1, inv1 = split3(w1)
    diag1 = w1.at[7]
    weights2, inv2 = split3(w2)
    for c in range(2):
        a2[c, 0] = jnp.zeros((24, 128), F32)
        a2[c, 11] = jnp.zeros((24, 128), F32)
    for c, parts in halves:
        spread(2, 0, c, even_x, even_y, *parts, a1, a2, 1)
        spread(2, 1, c, even_x, even_y, *parts, b1, b2, 0)
    spread_own(2, 0, 1 - core, own_b, a1, a2, 1)
    spread_own(2, 1, 1 - core, own_b, b1, b2, 0)
    copies.finish()
    out = Copies(sems.at[pl.ds(4, 5)])
    out.start(b1.at[:, 6:22, 8:24, :], right_hbm)
    faces(2, a2, weights2, inv2, None)
    out.start(w2, w2_hbm)
    faces(1, a1, weights1, inv1, diag1)
    out.start(w1, w1_hbm)
    smooth(2, b2, weights2, inv2, e2, d2, o2, c2)
    smooth(1, b1, weights1, inv1, e1, d1, o1, x1)
    combine(sum3, c2, s2, tmp3, tmp2)

    def finish(i, _):
        x1[:, i] = DAMPING * (x1[:, i] + tmp2[:, i // 2 - 1])
        return 0

    lax.fori_loop(5, 23, finish, 0)
    out.start(x1, x1_hbm)

    def residual(i):
        mid, near = weighted(1, i, 2, x1, weights1)
        at = pl.ds(i, 2)
        res = b1[:, at] - diag1[:, at] * (mid - near)
        rest[:, pl.ds(i - 6, 2)] = res[:, :, 8:24, :]

    blocks(6, 22, 2, residual)
    for c in range(2):
        for t in range(2):
            own[c, pl.ds(t, 16, 2)] = rest[c, :, t * 8:t * 8 + 8, :]

        def read_pair(k):
            total = None
            for x in (2 * k, 2 * k + 1):
                part = rest[c, x, pl.ds(0, 8, 2), :] + rest[c, x, pl.ds(1, 8, 2), :]
                total = part if total is None else total + part
            return total

        def put(k, value):
            own[c, 32 + k] = value

        restrict_to2(read_pair, put)
    out.start(own, own_hbm)
    for i in range(12):
        put_pair(even_x, first, second, i, own[core, 20 + i], own[core, i])
    for i in range(3):
        put_pair(even_x, first, second, 12 + i, own[core, 33 + i], own[core, 32 + i])
    slots[0] = restrict_to3(
        lambda k: own[core, 32 + k, pl.ds(0, 4, 2), :] + own[core, 32 + k, pl.ds(1, 4, 2), :]
    )
    slots[1:] = jnp.broadcast_to(slots[0:1], (slots.shape[0] - 1, 4, 128))
    out.finish()


def second_kernel(
    own_hbm, w1_hbm, w2_hbm, x1_hbm, right_hbm,
    x_one_a, x_two_a, y_one_a, y_two_a, x_one_b, x_two_b, y_one_b, y_two_b, sum3,
    out_x, out_r,
    w1, w2, x1, right, own, b1, e1, d1, o1, c1, b2, e2, d2, o2, c2, s2, tmp3, tmp2, rest, sems,
):
    core, gx, gy = position()
    even_x, even_y = is_even(gx), is_even(gy)
    copies = Copies(sems)
    for src, dst in (
        (own_hbm, own), (w2_hbm, w2), (w1_hbm, w1), (x1_hbm, x1), (right_hbm, right)
    ):
        copies.start(src, dst)
    weights1, inv1 = split3(w1)
    diag1 = w1.at[7]
    weights2, inv2 = split3(w2)
    spread(1, 0, core, even_x, even_y, x_one_a, x_two_a, y_one_a, y_two_a, b1, b2, 0)
    spread(1, 0, 1 - core, even_x, even_y, x_one_b, x_two_b, y_one_b, y_two_b, b1, b2, 0)
    copies.made[0].wait()
    for c in range(2):
        spread_own(1, 0, c, own.at[c], b1, b2, 0)
    copies.made[1].wait()
    smooth(2, b2, weights2, inv2, e2, d2, o2, c2)
    copies.made[2].wait()
    smooth(1, b1, weights1, inv1, e1, d1, o1, c1)
    copies.made[3].wait()
    copies.made[4].wait()
    combine(sum3, c2, s2, tmp3, tmp2)

    def finish(i, _):
        c1[:, i] = x1[:, i] + DAMPING * (c1[:, i] + tmp2[:, i // 2 - 1])
        return 0

    lax.fori_loop(5, 23, finish, 0)
    field = copies.start(c1.at[core, 6:22, 8:24, :], out_x)

    def residual(i):
        mid, near = weighted(1, i, 2, c1, weights1)
        res = diag1[:, pl.ds(i, 2)] * (mid - near)
        at = pl.ds(i - 6, 2)
        rest[:, at] = right[:, at] - res[:, :, 8:24, :]

    blocks(6, 22, 2, residual)
    done = copies.start(rest.at[core], out_r)
    field.wait()
    done.wait()


def call(kernel, outs, scratch, *args, hbm_in=(), hbm_out=(), sems=0, limit=8):
    vmem = pl.BlockSpec(memory_space=pltpu.VMEM)
    hbm = pl.BlockSpec(memory_space=pltpu.HBM)
    specs = [vmem for _ in args]
    args = list(args)
    for i in hbm_in:
        specs[i] = hbm
        args[i] = pltpu.with_memory_space_constraint(args[i], pltpu.HBM)
    scratch = [pltpu.VMEM(s, F32) for s in scratch]
    if sems:
        scratch.append(pltpu.SemaphoreType.DMA((sems,)))
    return pl.pallas_call(
        kernel,
        out_shape=[
            pltpu.HBM(s, F32) if i in hbm_out else jax.ShapeDtypeStruct(s, F32)
            for i, s in enumerate(outs)
        ],
        in_specs=specs,
        out_specs=[hbm if i in hbm_out else vmem for i in range(len(outs))],
        scratch_shapes=scratch,
        compiler_params=pltpu.CompilerParams(vmem_limit_bytes=limit * 1024 * 1024),
        interpret=INTERPRET,
    )(*args)


def trade(first, second, axis):
    size = lax.axis_size(axis)
    pairs = [(i, i ^ 1) for i in range(size)]
    others = [(i, i - 1 if i % 2 == 0 else i + 1) for i in range(1, size - 1)]
    one = lax.ppermute(first, axis, pairs)
    two = lax.ppermute(second, axis, others)
    return one, two


def swap(x):
    return lax.ppermute(x, "grp", [(0, 1), (1, 0)])


def everywhere(slots):
    return lax.all_to_all(slots, ("gx", "gy"), 0, 0, tiled=True)


def on_device(right_side, coefficient):
    gx_n, gy_n = lax.axis_size("gx"), lax.axis_size("gy")
    count = gx_n * gy_n
    s1, s2, s3 = (2, 28, 32, 128), (2, 10, 24, 128), (2, 5, 24, 128)
    p2, p3 = (2, 12, 24, 128), (2, 7, 24, 128)
    s4 = (gx_n // 2, gy_n * 2, 128)
    sum3 = (2, 3, 24, 128)
    tmps = [(2, 6, 24, 128), sum3, (2, 12, 32, 128), (2, 16, 16, 128)]

    own, middle, first, second, slots = call(
        prepare_kernel,
        [(72, 8, 128), (8, 8, 128), (30, 8, 128), (30, 8, 128), (count, 8, 128)],
        [(16, 16, 128)] * 2, coefficient, right_side, hbm_in=(0, 1), hbm_out=(1,), sems=3,
    )
    own_o = swap(own)
    x_one, x_two = trade(first, second, "gx")
    r3 = everywhere(slots)
    x_one_o, x_two_o = swap(x_one), swap(x_two)
    r3_o = swap(r3)
    first, second = call(
        functools.partial(sides_kernel, 2), [(76, 8, 128)] * 2, [], own, x_one, x_two
    )
    y_one, y_two = trade(first, second, "gy")
    y_one_o, y_two_o = swap(y_one), swap(y_two)
    flat = (count * 8, 128)
    w1s, w2s, w3s, w4s = (8,) + s1, (7,) + s2, (7,) + s3, (4,) + s4
    c3, w3, w4 = call(
        functools.partial(coarse_first_kernel, gx_n, gy_n), [sum3, w3s, w4s],
        [w3s, w4s, p3, s3, s3, s3, s3, s3, s4],
        r3, r3_o, r3.reshape(flat), r3_o.reshape(flat), hbm_out=(1, 2), sems=2, limit=12,
    )
    w1, w2, x1, right, own_kept, own, first, second, slots = call(
        first_kernel,
        [w1s, w2s, s1, (2, 16, 16, 128), (2, 36, 8, 128), (2, 36, 8, 128), (15, 8, 128),
         (15, 8, 128), (count, 4, 128)],
        [w1s, w2s, s1, s1, s1, s1, s1, s1, p2, s2, s2, s2, s2, s2] + tmps,
        coefficient, right_side, middle,
        x_one, x_two, y_one, y_two, own_o, x_one_o, x_two_o, y_one_o, y_two_o, c3,
        hbm_in=(0, 1, 2), hbm_out=(0, 1, 2, 3, 4), sems=9, limit=28,
    )
    x_one, x_two = trade(first, second, "gx")
    r3 = everywhere(slots)
    x_one_o, x_two_o = swap(x_one), swap(x_two)
    r3_o = swap(r3)
    first, second = call(
        functools.partial(sides_kernel, 1), [(38, 8, 128)] * 2, [], own, x_one, x_two
    )
    y_one, y_two = trade(first, second, "gy")
    y_one_o, y_two_o = swap(y_one), swap(y_two)
    flat = (count * 4, 128)
    (c3,) = call(
        functools.partial(coarse_second_kernel, gx_n, gy_n),
        [sum3], [w3s, w4s, s3, s3, s3, s3, s3, s4],
        r3, r3_o, r3.reshape(flat), r3_o.reshape(flat), w3, w4,
        hbm_in=(4, 5), sems=2, limit=12,
    )
    solution_field, residual = call(
        second_kernel, [(16, 16, 128)] * 2,
        [w1s, w2s, s1, (2, 16, 16, 128), (2, 36, 8, 128), s1, s1, s1, s1, s1, s2, s2, s2, s2, s2]
        + tmps,
        own_kept, w1, w2, x1, right,
        x_one, x_two, y_one, y_two, x_one_o, x_two_o, y_one_o, y_two_o, c3,
        hbm_in=(0, 1, 2, 3, 4), hbm_out=(0, 1), sems=7, limit=28,
    )
    return solution_field, residual


def solution(mesh):
    placed = P("gx", "gy", "grp")

    return jax.shard_map(
        on_device, mesh=mesh, in_specs=(placed, placed), out_specs=(placed, placed),
        check_vma=False,
    )
```

```python
import functools

import jax
import jax.numpy as jnp
from jax import lax
from jax.experimental import pallas as pl
from jax.experimental.pallas import tpu as pltpu
from jax.sharding import PartitionSpec as P


FINE_DEGREE = 5
COARSE_DEGREE = 16
LOW_FINE = 0.2
LOW_COARSE = 0.02
HIGH_BOUND = 2.0
DAMPING = 0.5

F32 = jnp.float32
INTERPRET = False
LANES_X = {1: 1, 2: 2, 3: 4}
HELD = {1: (1, 27), 2: (0, 10), 3: (0, 5)}
STEPS = {
    1: ((2, 26), (3, 25), (4, 24), (5, 23)),
    2: ((1, 9), (1, 9), (2, 8), (2, 8)),
    3: ((1, 4),) * 4,
}
CHUNK = {1: 2, 2: 2, 3: 3}
PAD = {1: 0, 2: 1, 3: 1}
SCALE = {1: 1.0, 2: 0.25, 3: 0.0625, 4: 0.015625}


def cheb_steps(degree, low, high):
    theta = (high + low) / 2.0
    delta = (high - low) / 2.0
    sigma = theta / delta
    rho = 1.0 / sigma
    keeps = []
    pushes = []
    for _ in range(degree - 1):
        rho_new = 1.0 / (2.0 * sigma - rho)
        keeps.append(rho_new * rho)
        pushes.append(2.0 * rho_new / delta)
        rho = rho_new
    return (1.0 / theta, keeps, pushes)


def roll(x, shift, axis):
    size = x.shape[axis]
    return pltpu.roll(x, shift % size, axis)


def lane_iota(shape):
    return lax.broadcasted_iota(jnp.int32, shape, len(shape) - 1)


def dot(x, m):
    high = x.astype(jnp.bfloat16)
    rest = x - high.astype(F32)
    mid = rest.astype(jnp.bfloat16)
    low = (rest - mid.astype(F32)).astype(jnp.bfloat16)
    m = m.astype(jnp.bfloat16)
    mul = lambda v: jnp.dot(v, m, preferred_element_type=F32)
    return mul(high) + (mul(mid) + mul(low))


def select_matrix(fn, value):
    row = lax.broadcasted_iota(jnp.int32, (128, 128), 0)
    col = lax.broadcasted_iota(jnp.int32, (128, 128), 1)
    return jnp.where(fn(row, col), value, 0.0).astype(F32)


def neighbours(q, v):
    zz = 128 // q
    mid = v[:, 1:-1]
    lane = lane_iota(mid.shape)
    if q == 1:
        x_up, x_dn = v[:, 2:], v[:, :-2]
        for_up = for_dn = mid
    else:
        ups = roll(v[:, 1:], -zz, 3)
        dns = roll(v[:, :-1], zz, 3)
        x_up = jnp.where(lane < 128 - zz, ups[:, :-1], ups[:, 1:])
        x_dn = jnp.where(lane >= zz, dns[:, 1:], dns[:, :-1])
        for_up, for_dn = dns[:, 1:], ups[:, :-1]
    other = lambda w: jnp.concatenate([w[1:], w[:1]], axis=0)
    inner = lane % zz
    z_up = roll(jnp.where(inner == 0, other(for_up), mid), -1, 3)
    z_dn = roll(jnp.where(inner == zz - 1, other(for_dn), mid), 1, 3)
    return mid, (x_up, x_dn, roll(mid, -1, 2), roll(mid, 1, 2), z_up, z_dn)


def blocks(start, stop, step, body):
    if stop - start == step:
        body(start)
        return

    def run(n, _):
        body(start + n * step)
        return 0

    lax.fori_loop(0, (stop - start) // step, run, 0)


def faces(level, a, weights, inv, diag_ref):
    q, pad = LANES_X[level], PAD[level]
    zz = 128 // q
    first, last = HELD[level]
    step = 5 if level == 3 else 2

    def body(i):
        mid, near = neighbours(q, a[:, pl.ds(i + pad - 1, step + 2)])
        core = lax.broadcasted_iota(jnp.int32, mid.shape, 0)
        lane = lane_iota(mid.shape) % zz
        top = (core == 1) & (lane == zz - 1)
        bottom = (core == 0) & (lane == 0)
        x_up, x_dn, y_up, y_dn, z_up, z_dn = near
        z_up = jnp.where(top, 0.0, z_up)
        z_dn = jnp.where(bottom, 0.0, z_dn)
        near = (x_up, x_dn, y_up, y_dn, z_up, z_dn)
        total = 3.0 * mid + 0.5 * ((x_up + x_dn) + (y_up + y_dn) + (z_up + z_dn))
        inverse = jnp.where(mid > 0.0, 1.0 / total, 0.0)
        at = pl.ds(i, step)
        inv[:, at] = inverse
        half = 0.5 * inverse
        for k in range(6):
            w = half * (mid + near[k])
            if k == 4:
                w = jnp.where(top, 0.0, w)
            if k == 5:
                w = jnp.where(bottom, 0.0, w)
            weights[k][:, at] = w
        if diag_ref is not None:
            diag_ref[:, at] = total

    blocks(first, last, step, body)


def weighted(q, i, step, v, weights):
    mid, near = neighbours(q, v[:, pl.ds(i - 1, step + 2)])
    at = pl.ds(i, step)
    terms = [weights[k][:, at] * near[k] for k in range(6)]
    return mid, (terms[0] + terms[1]) + (terms[2] + terms[3]) + (terms[4] + terms[5])


def smooth(level, b, weights, inv, e, d, other, x):
    q = LANES_X[level]
    first, keeps, pushes = cheb_steps(FINE_DEGREE, LOW_FINE, HIGH_BOUND)
    step = CHUNK[level]

    def start(i):
        at = pl.ds(i, 5 if level == 3 else 2)
        ev = b[:, at] * inv[:, at] * (1.0 / SCALE[level])
        e[:, at] = ev
        d[:, at] = ev * first
        x[:, at] = ev * first

    blocks(*HELD[level], 5 if level == 3 else 2, start)
    if level > 1:
        for i in (HELD[level][0], HELD[level][1] - 1):
            other[:, i] = jnp.zeros_like(other[:, i])
    for n in range(FINE_DEGREE - 1):
        src, dst = (d, other) if n % 2 == 0 else (other, d)

        def body(i):
            at = pl.ds(i, step)
            mid, near = weighted(q, i, step, src, weights)
            ev = (e[:, at] - mid) + near
            new = keeps[n] * mid + pushes[n] * ev
            x[:, at] = x[:, at] + new
            if n < FINE_DEGREE - 2:
                e[:, at] = ev
                dst[:, at] = new

        blocks(*STEPS[level][n], step, body)


def x_up4(v):
    moved = roll(v, -32, 2)
    after = jnp.concatenate([moved[1:], moved[:1]], axis=0)
    return jnp.where(lane_iota(v.shape) < 96, moved, after)


def x_dn4(v):
    moved = roll(v, 32, 2)
    before = jnp.concatenate([moved[-1:], moved[:-1]], axis=0)
    return jnp.where(lane_iota(v.shape) >= 32, moved, before)


def faces4(a, fx, fy, fz, inv):
    nb, rows, _ = a.shape
    blk = lax.broadcasted_iota(jnp.int32, a.shape, 0)
    row = lax.broadcasted_iota(jnp.int32, a.shape, 1)
    lane = lane_iota(a.shape)
    half = 0.5 * a
    total = jnp.zeros_like(a)
    for up, dn, last, start, out in (
        (x_up4, x_dn4, (blk == nb - 1) & (lane >= 96), (blk == 0) & (lane < 32), fx),
        (lambda v: roll(v, -1, 1), lambda v: roll(v, 1, 1), row == rows - 1, row == 0, fy),
        (lambda v: roll(v, -1, 2), lambda v: roll(v, 1, 2), lane % 32 == 31, lane % 32 == 0, fz),
    ):
        inner = half + 0.5 * up(a)
        off = jnp.where(last, 0.0, inner)
        out[...] = off
        total = total + jnp.where(last, half, inner) + jnp.where(start, half, dn(off))
    inv[...] = 1.0 / total


def smooth4(b, fx, fy, fz, inv):
    first, keeps, pushes = cheb_steps(COARSE_DEGREE, LOW_COARSE, HIGH_BOUND)
    e = b * inv[...] * (1.0 / SCALE[4])
    x = d = e * first
    for keep, push in zip(keeps, pushes):
        gx, gy, gz = fx[...], fy[...], fz[...]
        near = gx * x_up4(d) + x_dn4(gx * d)
        near = near + gy * roll(d, -1, 1) + roll(gy * d, 1, 1)
        near = near + gz * roll(d, -1, 2) + roll(gz * d, 1, 2)
        e = e - d + inv[...] * near
        d = keep * d + push * e
        x = x + d
    return x


def build4(src, stride, offset, core, gx_n, gy_n):
    count = gx_n * gy_n * 2
    gap = stride // 2
    pairs = src[pl.ds(offset, count, stride), :] + src[pl.ds(offset + gap, count, stride), :]
    pairs = pairs.reshape(gx_n // 2, 2, gy_n * 2, 128)
    out = None
    for odd in range(2):
        mat = select_matrix(
            lambda r, c: c == odd * 64 + (r // 64) * 32 + core * 16 + (r % 32) // 2, 0.125
        )
        part = dot(pairs[:, odd].reshape(gx_n * gy_n, 128), mat)
        out = part if out is None else out + part
    return out.reshape(gx_n // 2, gy_n * 2, 128)


def window3(src, dst, field, fields, core, pos, gx_n, gy_n, pad):
    for bx in range(5):
        for by in range(6):
            ix = pos[1] + (bx - 2)
            iy = pos[2] + (by - 2)
            ok = (ix >= 0) & (ix < gx_n) & (iy >= 0) & (iy < gy_n)
            at = jnp.clip(ix, 0, gx_n - 1) * gy_n + jnp.clip(iy, 0, gy_n - 1)
            if fields == 1:
                tile = src[at]
            else:
                tile = src[at, pl.ds(field, 4, fields), :]
            dst[core, bx + pad, by * 4:by * 4 + 4, :] = jnp.where(ok, tile, 0.0)


def restrict_to2(read_pair, out):
    even = jnp.concatenate([read_pair(2 * k) for k in range(4)], axis=0)
    odd = jnp.concatenate([read_pair(2 * k + 1) for k in range(4)], axis=0)
    low = select_matrix(lambda r, c: c == r // 2, 0.125)
    high = select_matrix(lambda r, c: c == 64 + r // 2, 0.125)
    both = dot(even, low) + dot(odd, high)
    for k in range(4):
        out(k, both[k * 8:k * 8 + 8])


def restrict_to3(read_rows):
    total = None
    for k in range(4):
        mat = select_matrix(lambda r, c: c == k * 32 + (r % 64) // 2, 0.125)
        part = dot(read_rows(k), mat)
        total = part if total is None else total + part
    return total


class Copies:
    def __init__(self, sems):
        self.sems, self.made = sems, []

    def start(self, src, dst):
        copy = pltpu.make_async_copy(src, dst, self.sems.at[len(self.made)])
        copy.start()
        self.made.append(copy)
        return copy

    def finish(self):
        for copy in self.made:
            copy.wait()


def position():
    return tuple(lax.axis_index(name) for name in ("grp", "gx", "gy"))


def put_pair(even, first, second, at, up, down):
    first[at] = jnp.where(even, up, down)
    second[at] = jnp.where(even, down, up)


def is_even(index):
    return lax.rem(index, 2) == 0


def prepare_kernel(a_hbm, b_hbm, own, mid_hbm, first, second, slots, a, b, sems):
    even = is_even(position()[1])
    copies = Copies(sems)
    copies.start(a_hbm, a)
    copies.start(b_hbm, b)
    for f, src in enumerate((a, b)):
        copies.made[f].wait()

        def read_pair(k):
            total = None
            for x in (2 * k, 2 * k + 1):
                part = src[x, pl.ds(0, 8, 2), :] + src[x, pl.ds(1, 8, 2), :]
                total = part if total is None else total + part
            return total

        values = []

        def out(k, value):
            own[64 + f * 4 + k] = value
            values.append(value)

        restrict_to2(read_pair, out)
        for k in range(3):
            put_pair(even, first, second, 24 + f * 3 + k, values[k + 1], values[k])
    keep = copies.start(own.at[64:72], mid_hbm)
    for f, src in enumerate((a, b)):
        for t in range(2):
            own[pl.ds(f * 32 + t, 16, 2)] = src[:, t * 8:t * 8 + 8, :]
            put_pair(
                even, first, second, pl.ds(f * 12 + t, 6, 2),
                src[10:16, t * 8:t * 8 + 8, :], src[0:6, t * 8:t * 8 + 8, :],
            )
        slots[0, pl.ds(f, 4, 2), :] = restrict_to3(
            lambda k: own[64 + f * 4 + k, pl.ds(0, 4, 2), :] + own[64 + f * 4 + k, pl.ds(1, 4, 2), :]
        )
    slots[1:] = jnp.broadcast_to(slots[0:1], (slots.shape[0] - 1, 8, 128))
    keep.wait()


def sides_kernel(nf, own, one, two, first, second):
    core, gx, gy = position()
    even_x, even_y = is_even(gx), is_even(gy)
    if nf == 2:
        mine = lambda i: own[i]
    else:
        mine = lambda i: own[core, i]

    def lower(i):
        return jnp.where(even_x, two[i], one[i])

    def upper(i):
        return jnp.where(even_x, one[i], two[i])

    for f in range(nf):
        for i in range(28):
            if i < 6:
                low, high = lower(f * 12 + 2 * i), lower(f * 12 + 2 * i + 1)
            elif i >= 22:
                low, high = upper(f * 12 + 2 * (i - 22)), upper(f * 12 + 2 * (i - 22) + 1)
            else:
                low, high = mine(f * 32 + 2 * (i - 6)), mine(f * 32 + 2 * (i - 6) + 1)
            put_pair(even_y, first, second, f * 28 + i, high, low)
        for i in range(10):
            if i < 3:
                tile = lower(nf * 12 + f * 3 + i)
            elif i >= 7:
                tile = upper(nf * 12 + f * 3 + i - 7)
            else:
                tile = mine(nf * 32 + f * 4 + i - 3)
            first[nf * 28 + f * 10 + i] = tile
            second[nf * 28 + f * 10 + i] = tile


def spread(nf, f, core, even_x, even_y, x_one, x_two, y_one, y_two, fine, mid, pad):
    lower = lambda i: jnp.where(even_x, x_two[i], x_one[i])
    upper = lambda i: jnp.where(even_x, x_one[i], x_two[i])
    below = lambda i: jnp.where(even_y, y_two[i], y_one[i])
    above = lambda i: jnp.where(even_y, y_one[i], y_two[i])
    for i in range(28):
        fine[core, i, 0:8, :] = below(f * 28 + i)
        fine[core, i, 24:32, :] = above(f * 28 + i)
        for t in range(2):
            if i < 6:
                tile = lower(f * 12 + 2 * i + t)
            elif i >= 22:
                tile = upper(f * 12 + 2 * (i - 22) + t)
            else:
                continue
            fine[core, i, 8 + 8 * t:16 + 8 * t, :] = tile
    base = nf * 28 + f * 10
    for i in range(10):
        mid[core, i + pad, 0:8, :] = below(base + i)
        mid[core, i + pad, 16:24, :] = above(base + i)
        if i < 3:
            tile = lower(nf * 12 + f * 3 + i)
        elif i >= 7:
            tile = upper(nf * 12 + f * 3 + i - 7)
        else:
            continue
        mid[core, i + pad, 8:16, :] = tile


def spread_own(nf, f, core, own, fine, mid, pad):
    for i in range(16):
        for t in range(2):
            fine[core, i + 6, 8 + 8 * t:16 + 8 * t, :] = own[f * 32 + 2 * i + t]
    for i in range(4):
        mid[core, i + 3 + pad, 8:16, :] = own[nf * 32 + f * 4 + i]


def add_coarsest(pos, gx_n, gy_n, x4, x3, out):
    gx, gy = pos[1], pos[2]
    yrow = lax.broadcasted_iota(jnp.int32, (24, gy_n * 2), 0)
    ycol = lax.broadcasted_iota(jnp.int32, (24, gy_n * 2), 1)
    rows = jnp.where(ycol == (4 * gy - 8 + yrow + 1024) // 2 - 512, 1.0, 0.0).astype(F32)
    for bx in (1, 2, 3):
        ix = gx + (bx - 2)
        ok = (ix >= 0) & (ix < gx_n)
        at = jnp.clip(ix, 0, gx_n - 1)
        odd = lax.rem(at, 2)
        picked = select_rows(rows, x4[lax.div(at, 2)])
        for c in range(2):
            mat = select_matrix(
                lambda r, k: r == odd * 64 + (k // 64) * 32 + c * 16 + (k % 32) // 2, 1.0
            )
            out[c, bx - 1] = x3[c, bx] + jnp.where(ok, dot(picked, mat), 0.0)


def select_rows(rows, v):
    high = v.astype(jnp.bfloat16)
    rest = v - high.astype(F32)
    mid = rest.astype(jnp.bfloat16)
    low = (rest - mid.astype(F32)).astype(jnp.bfloat16)
    rows = rows.astype(jnp.bfloat16)
    mul = lambda w: jnp.dot(rows, w, preferred_element_type=F32)
    return mul(high) + (mul(mid) + mul(low))


def combine(sum3, c2, x2, tmp3, tmp2):
    for c in range(2):
        for bx in range(3):
            tmp3[c, bx, pl.ds(0, 12, 2), :] = sum3[c, bx, 4:16, :]
            tmp3[c, bx, pl.ds(1, 12, 2), :] = sum3[c, bx, 4:16, :]
    for low in range(4):
        mat = select_matrix(lambda r, k: r == low * 32 + (k % 64) // 2, 1.0)
        for i in [i for i in range(2, 8) if (i + 5) % 4 == low]:
            bx = (i + 5) // 4 - 1
            part = dot(tmp3[:, bx].reshape(48, 128), mat).reshape(2, 24, 128)
            x2[:, i - 2] = c2[:, i] + part
    for low in range(2):
        mat = select_matrix(lambda r, k: r == low * 64 + k // 2, 1.0)
        part = dot(x2[...].reshape(2 * 6 * 24, 128), mat).reshape(2, 6, 24, 128)
        for i in range(6):
            piece = part[:, i, 4:20, :]
            tmp2[:, 2 * i + low, pl.ds(0, 16, 2), :] = piece
            tmp2[:, 2 * i + low, pl.ds(1, 16, 2), :] = piece


def split3(ref):
    return [ref.at[k] for k in range(6)], ref.at[6]


def coarse_first_kernel(
    gx_n, gy_n, r3_a, r3_b, r3f_a, r3f_b, sum3, w3_hbm, w4_hbm,
    w3, w4, a3, b3, e3, d3, o3, c3, x4, sems,
):
    pos = position()
    core = pos[0]
    weights3, inv3 = split3(w3)
    fx4, fy4, fz4, inv4 = (w4.at[k] for k in range(4))
    copies = Copies(sems)
    for c in range(2):
        a3[c, 0] = jnp.zeros((24, 128), F32)
        a3[c, 6] = jnp.zeros((24, 128), F32)
    for c, src in ((core, r3_a), (1 - core, r3_b)):
        window3(src, a3, 0, 2, c, pos, gx_n, gy_n, 1)
        window3(src, b3, 1, 2, c, pos, gx_n, gy_n, 0)
    a4 = build4(r3f_a, 4, 0, core, gx_n, gy_n) + build4(r3f_b, 4, 0, 1 - core, gx_n, gy_n)
    b4 = build4(r3f_a, 4, 1, core, gx_n, gy_n) + build4(r3f_b, 4, 1, 1 - core, gx_n, gy_n)
    faces4(a4, fx4, fy4, fz4, inv4)
    copies.start(w4, w4_hbm)
    faces(3, a3, weights3, inv3, None)
    copies.start(w3, w3_hbm)
    x4[...] = smooth4(b4, fx4, fy4, fz4, inv4)
    smooth(3, b3, weights3, inv3, e3, d3, o3, c3)
    add_coarsest(pos, gx_n, gy_n, x4, c3, sum3)
    copies.finish()


def coarse_second_kernel(
    gx_n, gy_n, r3_a, r3_b, r3f_a, r3f_b, w3_hbm, w4_hbm, sum3,
    w3, w4, b3, e3, d3, o3, c3, x4, sems,
):
    pos = position()
    core = pos[0]
    copies = Copies(sems)
    copies.start(w4_hbm, w4)
    copies.start(w3_hbm, w3)
    weights3, inv3 = split3(w3)
    window3(r3_a, b3, 0, 1, core, pos, gx_n, gy_n, 0)
    window3(r3_b, b3, 0, 1, 1 - core, pos, gx_n, gy_n, 0)
    b4 = build4(r3f_a, 2, 0, core, gx_n, gy_n) + build4(r3f_b, 2, 0, 1 - core, gx_n, gy_n)
    copies.made[0].wait()
    x4[...] = smooth4(b4, *(w4.at[k] for k in range(4)))
    copies.made[1].wait()
    smooth(3, b3, weights3, inv3, e3, d3, o3, c3)
    add_coarsest(pos, gx_n, gy_n, x4, c3, sum3)


def first_kernel(
    a_hbm, b_hbm, mid_hbm,
    x_one_a, x_two_a, y_one_a, y_two_a, own_b, x_one_b, x_two_b, y_one_b, y_two_b,
    w1_hbm, w2_hbm, c1_hbm, c2_hbm, right_hbm,
    w1, w2, c1, a1, b1, e1, d1, o1, a2, b2, e2, d2, o2, c2, sems,
):
    core, gx, gy = position()
    even_x, even_y = is_even(gx), is_even(gy)
    copies = Copies(sems)
    copies.start(a_hbm, a1.at[core, 6:22, 8:24, :])
    copies.start(b_hbm, b1.at[core, 6:22, 8:24, :])
    copies.start(mid_hbm.at[0:4], a2.at[core, 4:8, 8:16, :])
    copies.start(mid_hbm.at[4:8], b2.at[core, 3:7, 8:16, :])
    halves = (
        (core, (x_one_a, x_two_a, y_one_a, y_two_a)),
        (1 - core, (x_one_b, x_two_b, y_one_b, y_two_b)),
    )
    weights1, inv1 = split3(w1)
    diag1 = w1.at[7]
    weights2, inv2 = split3(w2)
    for c in range(2):
        a2[c, 0] = jnp.zeros((24, 128), F32)
        a2[c, 11] = jnp.zeros((24, 128), F32)
    for c, parts in halves:
        spread(2, 0, c, even_x, even_y, *parts, a1, a2, 1)
        spread(2, 1, c, even_x, even_y, *parts, b1, b2, 0)
    spread_own(2, 0, 1 - core, own_b, a1, a2, 1)
    spread_own(2, 1, 1 - core, own_b, b1, b2, 0)
    copies.finish()
    out = Copies(sems.at[pl.ds(4, 5)])
    out.start(b1.at[:, 6:22, 8:24, :], right_hbm)
    faces(2, a2, weights2, inv2, None)
    out.start(w2, w2_hbm)
    faces(1, a1, weights1, inv1, diag1)
    out.start(w1, w1_hbm)
    smooth(2, b2, weights2, inv2, e2, d2, o2, c2)
    out.start(c2, c2_hbm)
    smooth(1, b1, weights1, inv1, e1, d1, o1, c1)
    out.start(c1, c1_hbm)
    out.finish()


def join_first_kernel(
    gx_n, gy_n, r3_a, r3_b, r3f_a, r3f_b, w1_hbm, right_hbm, c1_hbm, c2_hbm,
    w3_hbm, w4_hbm, x1_hbm, own_hbm, own, first, second, slots,
    sum3, w3, w4, a3, b3, e3, d3, o3, c3, x4, w1, right, x1, c2, s2, tmp3, tmp2, rest, sems,
):
    core, gx, _ = position()
    even_x = is_even(gx)
    weights1, diag1 = split3(w1)[0], w1.at[7]
    copies = Copies(sems.at[pl.ds(2, 4)])
    copies.start(c2_hbm, c2)
    copies.start(c1_hbm, x1)
    copies.start(w1_hbm.at[:, :, 6:22], w1.at[:, :, 6:22])
    copies.start(right_hbm, right)
    coarse_first_kernel(
        gx_n, gy_n, r3_a, r3_b, r3f_a, r3f_b, sum3, w3_hbm, w4_hbm,
        w3, w4, a3, b3, e3, d3, o3, c3, x4, sems.at[pl.ds(0, 2)],
    )
    copies.made[0].wait()
    combine(sum3, c2, s2, tmp3, tmp2)
    copies.made[1].wait()

    def finish(i, _):
        x1[:, i] = DAMPING * (x1[:, i] + tmp2[:, i // 2 - 1])
        return 0

    lax.fori_loop(5, 23, finish, 0)
    out = Copies(sems.at[pl.ds(6, 2)])
    out.start(x1, x1_hbm)
    copies.made[2].wait()
    copies.made[3].wait()

    def residual(i):
        mid, near = weighted(1, i, 2, x1, weights1)
        res = diag1[:, pl.ds(i, 2)] * (mid - near)
        at = pl.ds(i - 6, 2)
        rest[:, at] = right[:, at] - res[:, :, 8:24, :]

    blocks(6, 22, 2, residual)
    for c in range(2):
        for t in range(2):
            own[c, pl.ds(t, 16, 2)] = rest[c, :, t * 8:t * 8 + 8, :]

        def read_pair(k):
            total = None
            for x in (2 * k, 2 * k + 1):
                part = rest[c, x, pl.ds(0, 8, 2), :] + rest[c, x, pl.ds(1, 8, 2), :]
                total = part if total is None else total + part
            return total

        def put(k, value):
            own[c, 32 + k] = value

        restrict_to2(read_pair, put)
    out.start(own, own_hbm)
    for i in range(12):
        put_pair(even_x, first, second, i, own[core, 20 + i], own[core, i])
    for i in range(3):
        put_pair(even_x, first, second, 12 + i, own[core, 33 + i], own[core, 32 + i])
    slots[0] = restrict_to3(
        lambda k: own[core, 32 + k, pl.ds(0, 4, 2), :] + own[core, 32 + k, pl.ds(1, 4, 2), :]
    )
    slots[1:] = jnp.broadcast_to(slots[0:1], (slots.shape[0] - 1, 4, 128))
    out.finish()


def second_kernel(
    own_hbm, w1_hbm, w2_hbm,
    x_one_a, x_two_a, y_one_a, y_two_a, x_one_b, x_two_b, y_one_b, y_two_b, c1_hbm, c2_hbm,
    w1, w2, own, b1, e1, d1, o1, c1, b2, e2, d2, o2, c2, sems,
):
    core, gx, gy = position()
    even_x, even_y = is_even(gx), is_even(gy)
    copies = Copies(sems)
    for src, dst in ((own_hbm, own), (w2_hbm, w2), (w1_hbm.at[0:7], w1)):
        copies.start(src, dst)
    weights1, inv1 = split3(w1)
    weights2, inv2 = split3(w2)
    spread(1, 0, core, even_x, even_y, x_one_a, x_two_a, y_one_a, y_two_a, b1, b2, 0)
    spread(1, 0, 1 - core, even_x, even_y, x_one_b, x_two_b, y_one_b, y_two_b, b1, b2, 0)
    copies.made[0].wait()
    for c in range(2):
        spread_own(1, 0, c, own.at[c], b1, b2, 0)
    copies.made[1].wait()
    smooth(2, b2, weights2, inv2, e2, d2, o2, c2)
    middle = copies.start(c2, c2_hbm)
    copies.made[2].wait()
    smooth(1, b1, weights1, inv1, e1, d1, o1, c1)
    last = copies.start(c1, c1_hbm)
    middle.wait()
    last.wait()


def join_second_kernel(
    gx_n, gy_n, r3_a, r3_b, r3f_a, r3f_b, w3_hbm, w4_hbm, w1_hbm, x1_hbm, right_hbm,
    c1_hbm, c2_hbm, out_x, out_r,
    sum3, w3, w4, b3, e3, d3, o3, c3, x4, w1, x1, right, c1, c2, s2, tmp3, tmp2, rest, sems,
):
    core = position()[0]
    weights1, diag1 = split3(w1)[0], w1.at[7]
    copies = Copies(sems.at[pl.ds(2, 7)])
    own = pl.ds(6, 16)
    for src, dst in (
        (c2_hbm, c2), (c1_hbm, c1), (x1_hbm, x1), (w1_hbm.at[:, :, own], w1.at[:, :, own]),
        (right_hbm, right),
    ):
        copies.start(src, dst)
    coarse_second_kernel(
        gx_n, gy_n, r3_a, r3_b, r3f_a, r3f_b, w3_hbm, w4_hbm, sum3,
        w3, w4, b3, e3, d3, o3, c3, x4, sems.at[pl.ds(0, 2)],
    )
    copies.made[0].wait()
    combine(sum3, c2, s2, tmp3, tmp2)
    copies.made[1].wait()
    copies.made[2].wait()

    def finish(i, _):
        c1[:, i] = x1[:, i] + DAMPING * (c1[:, i] + tmp2[:, i // 2 - 1])
        return 0

    lax.fori_loop(5, 23, finish, 0)
    field = copies.start(c1.at[core, 6:22, 8:24, :], out_x)
    copies.made[3].wait()
    copies.made[4].wait()

    def residual(i):
        mid, near = weighted(1, i, 2, c1, weights1)
        res = diag1[:, pl.ds(i, 2)] * (mid - near)
        at = pl.ds(i - 6, 2)
        rest[:, at] = right[:, at] - res[:, :, 8:24, :]

    blocks(6, 22, 2, residual)
    done = copies.start(rest.at[core], out_r)
    field.wait()
    done.wait()


def call(kernel, outs, scratch, *args, hbm_in=(), hbm_out=(), sems=0, limit=8):
    vmem = pl.BlockSpec(memory_space=pltpu.VMEM)
    hbm = pl.BlockSpec(memory_space=pltpu.HBM)
    specs = [vmem for _ in args]
    args = list(args)
    for i in hbm_in:
        specs[i] = hbm
        args[i] = pltpu.with_memory_space_constraint(args[i], pltpu.HBM)
    scratch = [pltpu.VMEM(s, F32) for s in scratch]
    if sems:
        scratch.append(pltpu.SemaphoreType.DMA((sems,)))
    return pl.pallas_call(
        kernel,
        out_shape=[
            pltpu.HBM(s, F32) if i in hbm_out else jax.ShapeDtypeStruct(s, F32)
            for i, s in enumerate(outs)
        ],
        in_specs=specs,
        out_specs=[hbm if i in hbm_out else vmem for i in range(len(outs))],
        scratch_shapes=scratch,
        compiler_params=pltpu.CompilerParams(vmem_limit_bytes=limit * 1024 * 1024),
        interpret=INTERPRET,
    )(*args)


def trade(first, second, axis):
    size = lax.axis_size(axis)
    pairs = [(i, i ^ 1) for i in range(size)]
    others = [(i, i - 1 if i % 2 == 0 else i + 1) for i in range(1, size - 1)]
    one = lax.ppermute(first, axis, pairs)
    two = lax.ppermute(second, axis, others)
    return one, two


def swap(x):
    return lax.ppermute(x, "grp", [(0, 1), (1, 0)])


def everywhere(slots):
    return lax.all_to_all(slots, ("gx", "gy"), 0, 0, tiled=True)


def on_device(right_side, coefficient):
    gx_n, gy_n = lax.axis_size("gx"), lax.axis_size("gy")
    count = gx_n * gy_n
    s1, s2, s3 = (2, 28, 32, 128), (2, 10, 24, 128), (2, 5, 24, 128)
    p2, p3 = (2, 12, 24, 128), (2, 7, 24, 128)
    s4 = (gx_n // 2, gy_n * 2, 128)
    sum3 = (2, 3, 24, 128)
    tmps = [(2, 6, 24, 128), sum3, (2, 12, 32, 128), (2, 16, 16, 128)]

    own, middle, first, second, slots = call(
        prepare_kernel,
        [(72, 8, 128), (8, 8, 128), (30, 8, 128), (30, 8, 128), (count, 8, 128)],
        [(16, 16, 128)] * 2, coefficient, right_side, hbm_in=(0, 1), hbm_out=(1,), sems=3,
    )
    own_o = swap(own)
    x_one, x_two = trade(first, second, "gx")
    r3 = everywhere(slots)
    x_one_o, x_two_o = swap(x_one), swap(x_two)
    r3_o = swap(r3)
    first, second = call(
        functools.partial(sides_kernel, 2), [(76, 8, 128)] * 2, [], own, x_one, x_two
    )
    y_one, y_two = trade(first, second, "gy")
    y_one_o, y_two_o = swap(y_one), swap(y_two)
    w1s, w2s, w3s, w4s = (8,) + s1, (7,) + s2, (7,) + s3, (4,) + s4
    block = (2, 16, 16, 128)
    w1, w2, c1, c2, right = call(
        first_kernel, [w1s, w2s, s1, s2, block],
        [w1s, w2s, s1, s1, s1, s1, s1, s1, p2, s2, s2, s2, s2, s2],
        coefficient, right_side, middle,
        x_one, x_two, y_one, y_two, own_o, x_one_o, x_two_o, y_one_o, y_two_o,
        hbm_in=(0, 1, 2), hbm_out=(0, 1, 2, 3, 4), sems=9, limit=28,
    )
    flat = (count * 8, 128)
    w3, w4, x1, own_kept, own, first, second, slots = call(
        functools.partial(join_first_kernel, gx_n, gy_n),
        [w3s, w4s, s1, (2, 36, 8, 128), (2, 36, 8, 128), (15, 8, 128), (15, 8, 128),
         (count, 4, 128)],
        [sum3, w3s, w4s, p3, s3, s3, s3, s3, s3, s4, w1s, block, s1, s2] + tmps,
        r3, r3_o, r3.reshape(flat), r3_o.reshape(flat), w1, right, c1, c2,
        hbm_in=(4, 5, 6, 7), hbm_out=(0, 1, 2, 3), sems=8, limit=28,
    )
    x_one, x_two = trade(first, second, "gx")
    r3 = everywhere(slots)
    x_one_o, x_two_o = swap(x_one), swap(x_two)
    r3_o = swap(r3)
    first, second = call(
        functools.partial(sides_kernel, 1), [(38, 8, 128)] * 2, [], own, x_one, x_two
    )
    y_one, y_two = trade(first, second, "gy")
    y_one_o, y_two_o = swap(y_one), swap(y_two)
    flat = (count * 4, 128)
    c1, c2 = call(
        second_kernel, [s1, s2],
        [(7,) + s1, w2s, (2, 36, 8, 128), s1, s1, s1, s1, s1, s2, s2, s2, s2, s2],
        own_kept, w1, w2, x_one, x_two, y_one, y_two, x_one_o, x_two_o, y_one_o, y_two_o,
        hbm_in=(0, 1, 2), hbm_out=(0, 1), sems=5, limit=28,
    )
    solution_field, residual = call(
        functools.partial(join_second_kernel, gx_n, gy_n), [(16, 16, 128)] * 2,
        [sum3, w3s, w4s, s3, s3, s3, s3, s3, s4, w1s, s1, block, s1, s2] + tmps,
        r3, r3_o, r3.reshape(flat), r3_o.reshape(flat), w3, w4, w1, x1, right, c1, c2,
        hbm_in=(4, 5, 6, 7, 8, 9, 10), hbm_out=(0, 1), sems=9, limit=28,
    )
    return solution_field, residual


def solution(mesh):
    placed = P("gx", "gy", "grp")

    return jax.shard_map(
        on_device, mesh=mesh, in_specs=(placed, placed), out_specs=(placed, placed),
        check_vma=False,
    )
```

```python
import functools

import jax
import jax.numpy as jnp
from jax import lax
from jax.experimental import pallas as pl
from jax.experimental.pallas import tpu as pltpu
from jax.sharding import PartitionSpec as P


FINE_DEGREE = 5
COARSE_DEGREE = 16
LOW_FINE = 0.2
LOW_COARSE = 0.02
HIGH_BOUND = 2.0
DAMPING = 0.5

F32 = jnp.float32
INTERPRET = False
LANES_X = {1: 1, 2: 2, 3: 4}
HELD = {1: (1, 27), 2: (0, 10), 3: (0, 5)}
STEPS = {
    1: ((2, 26), (3, 25), (4, 24), (5, 23)),
    2: ((1, 9), (1, 9), (2, 8), (2, 8)),
    3: ((1, 4),) * 4,
}
CHUNK = {1: 2, 2: 2, 3: 3}
PAD = {1: 0, 2: 1, 3: 1}
SCALE = {1: 1.0, 2: 0.25, 3: 0.0625, 4: 0.015625}


def cheb_steps(degree, low, high):
    theta = (high + low) / 2.0
    delta = (high - low) / 2.0
    sigma = theta / delta
    rho = 1.0 / sigma
    keeps = []
    pushes = []
    for _ in range(degree - 1):
        rho_new = 1.0 / (2.0 * sigma - rho)
        keeps.append(rho_new * rho)
        pushes.append(2.0 * rho_new / delta)
        rho = rho_new
    return (1.0 / theta, keeps, pushes)


def roll(x, shift, axis):
    size = x.shape[axis]
    return pltpu.roll(x, shift % size, axis)


def lane_iota(shape):
    return lax.broadcasted_iota(jnp.int32, shape, len(shape) - 1)


def dot(x, m):
    high = x.astype(jnp.bfloat16)
    rest = x - high.astype(F32)
    mid = rest.astype(jnp.bfloat16)
    low = (rest - mid.astype(F32)).astype(jnp.bfloat16)
    m = m.astype(jnp.bfloat16)
    mul = lambda v: jnp.dot(v, m, preferred_element_type=F32)
    return mul(high) + (mul(mid) + mul(low))


def select_matrix(fn, value):
    row = lax.broadcasted_iota(jnp.int32, (128, 128), 0)
    col = lax.broadcasted_iota(jnp.int32, (128, 128), 1)
    return jnp.where(fn(row, col), value, 0.0).astype(F32)


def neighbours(q, v):
    zz = 128 // q
    mid = v[:, 1:-1]
    lane = lane_iota(mid.shape)
    if q == 1:
        x_up, x_dn = v[:, 2:], v[:, :-2]
        for_up = for_dn = mid
    else:
        ups = roll(v[:, 1:], -zz, 3)
        dns = roll(v[:, :-1], zz, 3)
        x_up = jnp.where(lane < 128 - zz, ups[:, :-1], ups[:, 1:])
        x_dn = jnp.where(lane >= zz, dns[:, 1:], dns[:, :-1])
        for_up, for_dn = dns[:, 1:], ups[:, :-1]
    other = lambda w: jnp.concatenate([w[1:], w[:1]], axis=0)
    inner = lane % zz
    z_up = roll(jnp.where(inner == 0, other(for_up), mid), -1, 3)
    z_dn = roll(jnp.where(inner == zz - 1, other(for_dn), mid), 1, 3)
    return mid, (x_up, x_dn, roll(mid, -1, 2), roll(mid, 1, 2), z_up, z_dn)


def blocks(start, stop, step, body):
    if stop - start == step:
        body(start)
        return

    def run(n, _):
        body(start + n * step)
        return 0

    lax.fori_loop(0, (stop - start) // step, run, 0)


def faces(level, a, weights, inv, diag_ref):
    q, pad = LANES_X[level], PAD[level]
    zz = 128 // q
    first, last = HELD[level]
    step = 5 if level == 3 else 2

    def body(i):
        mid, near = neighbours(q, a[:, pl.ds(i + pad - 1, step + 2)])
        core = lax.broadcasted_iota(jnp.int32, mid.shape, 0)
        lane = lane_iota(mid.shape) % zz
        top = (core == 1) & (lane == zz - 1)
        bottom = (core == 0) & (lane == 0)
        x_up, x_dn, y_up, y_dn, z_up, z_dn = near
        z_up = jnp.where(top, 0.0, z_up)
        z_dn = jnp.where(bottom, 0.0, z_dn)
        near = (x_up, x_dn, y_up, y_dn, z_up, z_dn)
        total = 3.0 * mid + 0.5 * ((x_up + x_dn) + (y_up + y_dn) + (z_up + z_dn))
        inverse = jnp.where(mid > 0.0, 1.0 / total, 0.0)
        at = pl.ds(i, step)
        inv[:, at] = inverse
        half = 0.5 * inverse
        for k in range(6):
            w = half * (mid + near[k])
            if k == 4:
                w = jnp.where(top, 0.0, w)
            if k == 5:
                w = jnp.where(bottom, 0.0, w)
            weights[k][:, at] = w
        if diag_ref is not None:
            diag_ref[:, at] = total

    blocks(first, last, step, body)


def weighted(q, i, step, v, weights):
    mid, near = neighbours(q, v[:, pl.ds(i - 1, step + 2)])
    at = pl.ds(i, step)
    terms = [weights[k][:, at] * near[k] for k in range(6)]
    return mid, (terms[0] + terms[1]) + (terms[2] + terms[3]) + (terms[4] + terms[5])


def smooth(level, b, weights, inv, e, d, other, x):
    q = LANES_X[level]
    first, keeps, pushes = cheb_steps(FINE_DEGREE, LOW_FINE, HIGH_BOUND)
    step = CHUNK[level]

    def start(i):
        at = pl.ds(i, 5 if level == 3 else 2)
        ev = b[:, at] * inv[:, at] * (1.0 / SCALE[level])
        e[:, at] = ev
        d[:, at] = ev * first
        x[:, at] = ev * first

    blocks(*HELD[level], 5 if level == 3 else 2, start)
    if level > 1:
        for i in (HELD[level][0], HELD[level][1] - 1):
            other[:, i] = jnp.zeros_like(other[:, i])
    for n in range(FINE_DEGREE - 1):
        src, dst = (d, other) if n % 2 == 0 else (other, d)

        def body(i):
            at = pl.ds(i, step)
            mid, near = weighted(q, i, step, src, weights)
            ev = (e[:, at] - mid) + near
            new = keeps[n] * mid + pushes[n] * ev
            x[:, at] = x[:, at] + new
            if n < FINE_DEGREE - 2:
                e[:, at] = ev
                dst[:, at] = new

        blocks(*STEPS[level][n], step, body)


def x_up4(v):
    moved = roll(v, -32, 2)
    after = jnp.concatenate([moved[1:], moved[:1]], axis=0)
    return jnp.where(lane_iota(v.shape) < 96, moved, after)


def x_dn4(v):
    moved = roll(v, 32, 2)
    before = jnp.concatenate([moved[-1:], moved[:-1]], axis=0)
    return jnp.where(lane_iota(v.shape) >= 32, moved, before)


def faces4(a, fx, fy, fz, inv):
    nb, rows, _ = a.shape
    blk = lax.broadcasted_iota(jnp.int32, a.shape, 0)
    row = lax.broadcasted_iota(jnp.int32, a.shape, 1)
    lane = lane_iota(a.shape)
    half = 0.5 * a
    total = jnp.zeros_like(a)
    for up, dn, last, start, out in (
        (x_up4, x_dn4, (blk == nb - 1) & (lane >= 96), (blk == 0) & (lane < 32), fx),
        (lambda v: roll(v, -1, 1), lambda v: roll(v, 1, 1), row == rows - 1, row == 0, fy),
        (lambda v: roll(v, -1, 2), lambda v: roll(v, 1, 2), lane % 32 == 31, lane % 32 == 0, fz),
    ):
        inner = half + 0.5 * up(a)
        off = jnp.where(last, 0.0, inner)
        out[...] = off
        total = total + jnp.where(last, half, inner) + jnp.where(start, half, dn(off))
    inv[...] = 1.0 / total


def smooth4(b, fx, fy, fz, inv):
    first, keeps, pushes = cheb_steps(COARSE_DEGREE, LOW_COARSE, HIGH_BOUND)
    e = b * inv[...] * (1.0 / SCALE[4])
    x = d = e * first
    for keep, push in zip(keeps, pushes):
        gx, gy, gz = fx[...], fy[...], fz[...]
        near = gx * x_up4(d) + x_dn4(gx * d)
        near = near + gy * roll(d, -1, 1) + roll(gy * d, 1, 1)
        near = near + gz * roll(d, -1, 2) + roll(gz * d, 1, 2)
        e = e - d + inv[...] * near
        d = keep * d + push * e
        x = x + d
    return x


def build4(src, stride, offset, core, gx_n, gy_n):
    count = gx_n * gy_n * 2
    gap = stride // 2
    pairs = src[pl.ds(offset, count, stride), :] + src[pl.ds(offset + gap, count, stride), :]
    pairs = pairs.reshape(gx_n // 2, 2, gy_n * 2, 128)
    out = None
    for odd in range(2):
        mat = select_matrix(
            lambda r, c: c == odd * 64 + (r // 64) * 32 + core * 16 + (r % 32) // 2, 0.125
        )
        part = dot(pairs[:, odd].reshape(gx_n * gy_n, 128), mat)
        out = part if out is None else out + part
    return out.reshape(gx_n // 2, gy_n * 2, 128)


def window3(src, dst, field, fields, core, pos, gx_n, gy_n, pad):
    for bx in range(5):
        for by in range(6):
            ix = pos[1] + (bx - 2)
            iy = pos[2] + (by - 2)
            ok = (ix >= 0) & (ix < gx_n) & (iy >= 0) & (iy < gy_n)
            at = jnp.clip(ix, 0, gx_n - 1) * gy_n + jnp.clip(iy, 0, gy_n - 1)
            if fields == 1:
                tile = src[at]
            else:
                tile = src[at, pl.ds(field, 4, fields), :]
            dst[core, bx + pad, by * 4:by * 4 + 4, :] = jnp.where(ok, tile, 0.0)


def restrict_to2(read_pair, out):
    even = jnp.concatenate([read_pair(2 * k) for k in range(4)], axis=0)
    odd = jnp.concatenate([read_pair(2 * k + 1) for k in range(4)], axis=0)
    low = select_matrix(lambda r, c: c == r // 2, 0.125)
    high = select_matrix(lambda r, c: c == 64 + r // 2, 0.125)
    both = dot(even, low) + dot(odd, high)
    for k in range(4):
        out(k, both[k * 8:k * 8 + 8])


def restrict_to3(read_rows):
    total = None
    for k in range(4):
        mat = select_matrix(lambda r, c: c == k * 32 + (r % 64) // 2, 0.125)
        part = dot(read_rows(k), mat)
        total = part if total is None else total + part
    return total


class Copies:
    def __init__(self, sems):
        self.sems, self.made = sems, []

    def start(self, src, dst):
        copy = pltpu.make_async_copy(src, dst, self.sems.at[len(self.made)])
        copy.start()
        self.made.append(copy)
        return copy

    def finish(self):
        for copy in self.made:
            copy.wait()


def position():
    return tuple(lax.axis_index(name) for name in ("grp", "gx", "gy"))


def put_pair(even, first, second, at, up, down):
    first[at] = jnp.where(even, up, down)
    second[at] = jnp.where(even, down, up)


def is_even(index):
    return lax.rem(index, 2) == 0


def prepare_kernel(a_hbm, b_hbm, own, mid_hbm, first, second, slots, a, b, sems):
    even = is_even(position()[1])
    copies = Copies(sems)
    copies.start(a_hbm, a)
    copies.start(b_hbm, b)
    for f, src in enumerate((a, b)):
        copies.made[f].wait()

        def read_pair(k):
            total = None
            for x in (2 * k, 2 * k + 1):
                part = src[x, pl.ds(0, 8, 2), :] + src[x, pl.ds(1, 8, 2), :]
                total = part if total is None else total + part
            return total

        values = []

        def out(k, value):
            own[64 + f * 4 + k] = value
            values.append(value)

        restrict_to2(read_pair, out)
        for k in range(3):
            put_pair(even, first, second, 24 + f * 3 + k, values[k + 1], values[k])
    keep = copies.start(own.at[64:72], mid_hbm)
    for f, src in enumerate((a, b)):
        for t in range(2):
            own[pl.ds(f * 32 + t, 16, 2)] = src[:, t * 8:t * 8 + 8, :]
            put_pair(
                even, first, second, pl.ds(f * 12 + t, 6, 2),
                src[10:16, t * 8:t * 8 + 8, :], src[0:6, t * 8:t * 8 + 8, :],
            )
        slots[0, pl.ds(f, 4, 2), :] = restrict_to3(
            lambda k: own[64 + f * 4 + k, pl.ds(0, 4, 2), :] + own[64 + f * 4 + k, pl.ds(1, 4, 2), :]
        )
    slots[1:] = jnp.broadcast_to(slots[0:1], (slots.shape[0] - 1, 8, 128))
    keep.wait()


def sides_kernel(nf, own, one, two, first, second):
    core, gx, gy = position()
    even_x, even_y = is_even(gx), is_even(gy)
    if nf == 2:
        mine = lambda i: own[i]
    else:
        mine = lambda i: own[core, i]

    def lower(i):
        return jnp.where(even_x, two[i], one[i])

    def upper(i):
        return jnp.where(even_x, one[i], two[i])

    for f in range(nf):
        for i in range(28):
            if i < 6:
                low, high = lower(f * 12 + 2 * i), lower(f * 12 + 2 * i + 1)
            elif i >= 22:
                low, high = upper(f * 12 + 2 * (i - 22)), upper(f * 12 + 2 * (i - 22) + 1)
            else:
                low, high = mine(f * 32 + 2 * (i - 6)), mine(f * 32 + 2 * (i - 6) + 1)
            put_pair(even_y, first, second, f * 28 + i, high, low)
        for i in range(10):
            if i < 3:
                tile = lower(nf * 12 + f * 3 + i)
            elif i >= 7:
                tile = upper(nf * 12 + f * 3 + i - 7)
            else:
                tile = mine(nf * 32 + f * 4 + i - 3)
            first[nf * 28 + f * 10 + i] = tile
            second[nf * 28 + f * 10 + i] = tile


def spread(nf, f, core, even_x, even_y, x_one, x_two, y_one, y_two, fine, mid, pad):
    lower = lambda i: jnp.where(even_x, x_two[i], x_one[i])
    upper = lambda i: jnp.where(even_x, x_one[i], x_two[i])
    below = lambda i: jnp.where(even_y, y_two[i], y_one[i])
    above = lambda i: jnp.where(even_y, y_one[i], y_two[i])
    for i in range(28):
        fine[core, i, 0:8, :] = below(f * 28 + i)
        fine[core, i, 24:32, :] = above(f * 28 + i)
        for t in range(2):
            if i < 6:
                tile = lower(f * 12 + 2 * i + t)
            elif i >= 22:
                tile = upper(f * 12 + 2 * (i - 22) + t)
            else:
                continue
            fine[core, i, 8 + 8 * t:16 + 8 * t, :] = tile
    base = nf * 28 + f * 10
    for i in range(10):
        mid[core, i + pad, 0:8, :] = below(base + i)
        mid[core, i + pad, 16:24, :] = above(base + i)
        if i < 3:
            tile = lower(nf * 12 + f * 3 + i)
        elif i >= 7:
            tile = upper(nf * 12 + f * 3 + i - 7)
        else:
            continue
        mid[core, i + pad, 8:16, :] = tile


def spread_own(nf, f, core, own, fine, mid, pad):
    for i in range(16):
        for t in range(2):
            fine[core, i + 6, 8 + 8 * t:16 + 8 * t, :] = own[f * 32 + 2 * i + t]
    for i in range(4):
        mid[core, i + 3 + pad, 8:16, :] = own[nf * 32 + f * 4 + i]


def add_coarsest(pos, gx_n, gy_n, x4, x3, out):
    gx, gy = pos[1], pos[2]
    yrow = lax.broadcasted_iota(jnp.int32, (24, gy_n * 2), 0)
    ycol = lax.broadcasted_iota(jnp.int32, (24, gy_n * 2), 1)
    rows = jnp.where(ycol == (4 * gy - 8 + yrow + 1024) // 2 - 512, 1.0, 0.0).astype(F32)
    for bx in (1, 2, 3):
        ix = gx + (bx - 2)
        ok = (ix >= 0) & (ix < gx_n)
        at = jnp.clip(ix, 0, gx_n - 1)
        odd = lax.rem(at, 2)
        picked = select_rows(rows, x4[lax.div(at, 2)])
        for c in range(2):
            mat = select_matrix(
                lambda r, k: r == odd * 64 + (k // 64) * 32 + c * 16 + (k % 32) // 2, 1.0
            )
            out[c, bx - 1] = x3[c, bx] + jnp.where(ok, dot(picked, mat), 0.0)


def select_rows(rows, v):
    high = v.astype(jnp.bfloat16)
    rest = v - high.astype(F32)
    mid = rest.astype(jnp.bfloat16)
    low = (rest - mid.astype(F32)).astype(jnp.bfloat16)
    rows = rows.astype(jnp.bfloat16)
    mul = lambda w: jnp.dot(rows, w, preferred_element_type=F32)
    return mul(high) + (mul(mid) + mul(low))


def combine(sum3, c2, x2, tmp3, tmp2):
    for c in range(2):
        for bx in range(3):
            tmp3[c, bx, pl.ds(0, 12, 2), :] = sum3[c, bx, 4:16, :]
            tmp3[c, bx, pl.ds(1, 12, 2), :] = sum3[c, bx, 4:16, :]
    for low in range(4):
        mat = select_matrix(lambda r, k: r == low * 32 + (k % 64) // 2, 1.0)
        for i in [i for i in range(2, 8) if (i + 5) % 4 == low]:
            bx = (i + 5) // 4 - 1
            part = dot(tmp3[:, bx].reshape(48, 128), mat).reshape(2, 24, 128)
            x2[:, i - 2] = c2[:, i] + part
    for low in range(2):
        mat = select_matrix(lambda r, k: r == low * 64 + k // 2, 1.0)
        part = dot(x2[...].reshape(2 * 6 * 24, 128), mat).reshape(2, 6, 24, 128)
        for i in range(6):
            piece = part[:, i, 4:20, :]
            tmp2[:, 2 * i + low, pl.ds(0, 16, 2), :] = piece
            tmp2[:, 2 * i + low, pl.ds(1, 16, 2), :] = piece


def split3(ref):
    return [ref.at[k] for k in range(6)], ref.at[6]


def coarse_first_kernel(
    gx_n, gy_n, r3_a, r3_b, r3f_a, r3f_b, sum3, w3_hbm, w4_hbm,
    w3, w4, a3, b3, e3, d3, o3, c3, x4, sems,
):
    pos = position()
    core = pos[0]
    weights3, inv3 = split3(w3)
    fx4, fy4, fz4, inv4 = (w4.at[k] for k in range(4))
    copies = Copies(sems)
    for c in range(2):
        a3[c, 0] = jnp.zeros((24, 128), F32)
        a3[c, 6] = jnp.zeros((24, 128), F32)
    for c, src in ((core, r3_a), (1 - core, r3_b)):
        window3(src, a3, 0, 2, c, pos, gx_n, gy_n, 1)
        window3(src, b3, 1, 2, c, pos, gx_n, gy_n, 0)
    a4 = build4(r3f_a, 4, 0, core, gx_n, gy_n) + build4(r3f_b, 4, 0, 1 - core, gx_n, gy_n)
    b4 = build4(r3f_a, 4, 1, core, gx_n, gy_n) + build4(r3f_b, 4, 1, 1 - core, gx_n, gy_n)
    faces4(a4, fx4, fy4, fz4, inv4)
    copies.start(w4, w4_hbm)
    faces(3, a3, weights3, inv3, None)
    copies.start(w3, w3_hbm)
    x4[...] = smooth4(b4, fx4, fy4, fz4, inv4)
    smooth(3, b3, weights3, inv3, e3, d3, o3, c3)
    add_coarsest(pos, gx_n, gy_n, x4, c3, sum3)
    copies.finish()


def coarse_second_kernel(
    gx_n, gy_n, r3_a, r3_b, r3f_a, r3f_b, w3_hbm, w4_hbm, sum3,
    w3, w4, b3, e3, d3, o3, c3, x4, sems,
):
    pos = position()
    core = pos[0]
    copies = Copies(sems)
    copies.start(w4_hbm, w4)
    copies.start(w3_hbm, w3)
    weights3, inv3 = split3(w3)
    window3(r3_a, b3, 0, 1, core, pos, gx_n, gy_n, 0)
    window3(r3_b, b3, 0, 1, 1 - core, pos, gx_n, gy_n, 0)
    b4 = build4(r3f_a, 2, 0, core, gx_n, gy_n) + build4(r3f_b, 2, 0, 1 - core, gx_n, gy_n)
    copies.made[0].wait()
    x4[...] = smooth4(b4, *(w4.at[k] for k in range(4)))
    copies.made[1].wait()
    smooth(3, b3, weights3, inv3, e3, d3, o3, c3)
    add_coarsest(pos, gx_n, gy_n, x4, c3, sum3)


def first_kernel(
    a_hbm, b_hbm, mid_hbm,
    x_one_a, x_two_a, y_one_a, y_two_a, own_b, x_one_b, x_two_b, y_one_b, y_two_b,
    w1_hbm, w2_hbm, c1_hbm, c2_hbm, right_hbm,
    w1, w2, c1, a1, b1, e1, d1, o1, a2, b2, e2, d2, o2, c2, sems,
):
    core, gx, gy = position()
    even_x, even_y = is_even(gx), is_even(gy)
    copies = Copies(sems)
    copies.start(a_hbm, a1.at[core, 6:22, 8:24, :])
    copies.start(b_hbm, b1.at[core, 6:22, 8:24, :])
    copies.start(mid_hbm.at[0:4], a2.at[core, 4:8, 8:16, :])
    copies.start(mid_hbm.at[4:8], b2.at[core, 3:7, 8:16, :])
    halves = (
        (core, (x_one_a, x_two_a, y_one_a, y_two_a)),
        (1 - core, (x_one_b, x_two_b, y_one_b, y_two_b)),
    )
    weights1, inv1 = split3(w1)
    diag1 = w1.at[7]
    weights2, inv2 = split3(w2)
    for c in range(2):
        a2[c, 0] = jnp.zeros((24, 128), F32)
        a2[c, 11] = jnp.zeros((24, 128), F32)
    for c, parts in halves:
        spread(2, 0, c, even_x, even_y, *parts, a1, a2, 1)
        spread(2, 1, c, even_x, even_y, *parts, b1, b2, 0)
    spread_own(2, 0, 1 - core, own_b, a1, a2, 1)
    spread_own(2, 1, 1 - core, own_b, b1, b2, 0)
    copies.finish()
    out = Copies(sems.at[pl.ds(4, 5)])
    out.start(b1.at[:, 6:22, 8:24, :], right_hbm)
    faces(2, a2, weights2, inv2, None)
    out.start(w2, w2_hbm)
    faces(1, a1, weights1, inv1, diag1)
    out.start(w1, w1_hbm)
    smooth(2, b2, weights2, inv2, e2, d2, o2, c2)
    out.start(c2, c2_hbm)
    smooth(1, b1, weights1, inv1, e1, d1, o1, c1)
    out.start(c1.at[:, 5:23], c1_hbm.at[:, 5:23])
    out.finish()


def join_first_kernel(
    gx_n, gy_n, r3_a, r3_b, r3f_a, r3f_b, w1_hbm, right_hbm, c1_hbm, c2_hbm,
    w3_hbm, w4_hbm, x1_hbm, own_hbm, own, first, second, slots,
    sum3, w3, w4, a3, b3, e3, d3, o3, c3, x4, w1, right, x1, c2, s2, tmp3, tmp2, rest, sems,
):
    core, gx, _ = position()
    even_x = is_even(gx)
    weights1, diag1 = split3(w1)[0], w1.at[7]
    copies = Copies(sems.at[pl.ds(2, 4)])
    copies.start(c2_hbm, c2)
    copies.start(c1_hbm.at[:, 5:23], x1.at[:, 5:23])
    copies.start(w1_hbm.at[:, :, 6:22], w1.at[:, :, 6:22])
    copies.start(right_hbm, right)
    coarse_first_kernel(
        gx_n, gy_n, r3_a, r3_b, r3f_a, r3f_b, sum3, w3_hbm, w4_hbm,
        w3, w4, a3, b3, e3, d3, o3, c3, x4, sems.at[pl.ds(0, 2)],
    )
    copies.made[0].wait()
    combine(sum3, c2, s2, tmp3, tmp2)
    copies.made[1].wait()

    def finish(i, _):
        x1[:, i] = DAMPING * (x1[:, i] + tmp2[:, i // 2 - 1])
        return 0

    lax.fori_loop(5, 23, finish, 0)
    out = Copies(sems.at[pl.ds(6, 2)])
    out.start(x1, x1_hbm)
    copies.made[2].wait()
    copies.made[3].wait()

    def residual(i):
        mid, near = weighted(1, i, 2, x1, weights1)
        res = diag1[:, pl.ds(i, 2)] * (mid - near)
        at = pl.ds(i - 6, 2)
        rest[:, at] = right[:, at] - res[:, :, 8:24, :]

    blocks(6, 22, 2, residual)
    for c in range(2):
        for t in range(2):
            own[c, pl.ds(t, 16, 2)] = rest[c, :, t * 8:t * 8 + 8, :]

        def read_pair(k):
            total = None
            for x in (2 * k, 2 * k + 1):
                part = rest[c, x, pl.ds(0, 8, 2), :] + rest[c, x, pl.ds(1, 8, 2), :]
                total = part if total is None else total + part
            return total

        def put(k, value):
            own[c, 32 + k] = value

        restrict_to2(read_pair, put)
    out.start(own, own_hbm)
    for i in range(12):
        put_pair(even_x, first, second, i, own[core, 20 + i], own[core, i])
    for i in range(3):
        put_pair(even_x, first, second, 12 + i, own[core, 33 + i], own[core, 32 + i])
    slots[0] = restrict_to3(
        lambda k: own[core, 32 + k, pl.ds(0, 4, 2), :] + own[core, 32 + k, pl.ds(1, 4, 2), :]
    )
    slots[1:] = jnp.broadcast_to(slots[0:1], (slots.shape[0] - 1, 4, 128))
    out.finish()


def second_kernel(
    own_hbm, w1_hbm, w2_hbm, x1_hbm, right_hbm,
    x_one_a, x_two_a, y_one_a, y_two_a, x_one_b, x_two_b, y_one_b, y_two_b, sum3,
    out_x, out_r,
    w1, w2, x1, right, own, b1, e1, d1, o1, c1, b2, e2, d2, o2, c2, s2, tmp3, tmp2, rest, sems,
):
    core, gx, gy = position()
    even_x, even_y = is_even(gx), is_even(gy)
    copies = Copies(sems)
    for src, dst in (
        (own_hbm, own), (w2_hbm, w2), (w1_hbm, w1), (x1_hbm, x1), (right_hbm, right)
    ):
        copies.start(src, dst)
    weights1, inv1 = split3(w1)
    diag1 = w1.at[7]
    weights2, inv2 = split3(w2)
    spread(1, 0, core, even_x, even_y, x_one_a, x_two_a, y_one_a, y_two_a, b1, b2, 0)
    spread(1, 0, 1 - core, even_x, even_y, x_one_b, x_two_b, y_one_b, y_two_b, b1, b2, 0)
    copies.made[0].wait()
    for c in range(2):
        spread_own(1, 0, c, own.at[c], b1, b2, 0)
    copies.made[1].wait()
    smooth(2, b2, weights2, inv2, e2, d2, o2, c2)
    copies.made[2].wait()
    smooth(1, b1, weights1, inv1, e1, d1, o1, c1)
    copies.made[3].wait()
    copies.made[4].wait()
    combine(sum3, c2, s2, tmp3, tmp2)

    def finish(i, _):
        c1[:, i] = x1[:, i] + DAMPING * (c1[:, i] + tmp2[:, i // 2 - 1])
        return 0

    lax.fori_loop(5, 23, finish, 0)
    field = copies.start(c1.at[core, 6:22, 8:24, :], out_x)

    def residual(i):
        mid, near = weighted(1, i, 2, c1, weights1)
        res = diag1[:, pl.ds(i, 2)] * (mid - near)
        at = pl.ds(i - 6, 2)
        rest[:, at] = right[:, at] - res[:, :, 8:24, :]

    blocks(6, 22, 2, residual)
    done = copies.start(rest.at[core], out_r)
    field.wait()
    done.wait()


def call(kernel, outs, scratch, *args, hbm_in=(), hbm_out=(), sems=0, limit=8):
    vmem = pl.BlockSpec(memory_space=pltpu.VMEM)
    hbm = pl.BlockSpec(memory_space=pltpu.HBM)
    specs = [vmem for _ in args]
    args = list(args)
    for i in hbm_in:
        specs[i] = hbm
        args[i] = pltpu.with_memory_space_constraint(args[i], pltpu.HBM)
    scratch = [pltpu.VMEM(s, F32) for s in scratch]
    if sems:
        scratch.append(pltpu.SemaphoreType.DMA((sems,)))
    return pl.pallas_call(
        kernel,
        out_shape=[
            pltpu.HBM(s, F32) if i in hbm_out else jax.ShapeDtypeStruct(s, F32)
            for i, s in enumerate(outs)
        ],
        in_specs=specs,
        out_specs=[hbm if i in hbm_out else vmem for i in range(len(outs))],
        scratch_shapes=scratch,
        compiler_params=pltpu.CompilerParams(vmem_limit_bytes=limit * 1024 * 1024),
        interpret=INTERPRET,
    )(*args)


def trade(first, second, axis):
    size = lax.axis_size(axis)
    pairs = [(i, i ^ 1) for i in range(size)]
    others = [(i, i - 1 if i % 2 == 0 else i + 1) for i in range(1, size - 1)]
    one = lax.ppermute(first, axis, pairs)
    two = lax.ppermute(second, axis, others)
    return one, two


def swap(x):
    return lax.ppermute(x, "grp", [(0, 1), (1, 0)])


def everywhere(slots):
    return lax.all_to_all(slots, ("gx", "gy"), 0, 0, tiled=True)


def on_device(right_side, coefficient):
    gx_n, gy_n = lax.axis_size("gx"), lax.axis_size("gy")
    count = gx_n * gy_n
    s1, s2, s3 = (2, 28, 32, 128), (2, 10, 24, 128), (2, 5, 24, 128)
    p2, p3 = (2, 12, 24, 128), (2, 7, 24, 128)
    s4 = (gx_n // 2, gy_n * 2, 128)
    sum3 = (2, 3, 24, 128)
    tmps = [(2, 6, 24, 128), sum3, (2, 12, 32, 128), (2, 16, 16, 128)]

    own, middle, first, second, slots = call(
        prepare_kernel,
        [(72, 8, 128), (8, 8, 128), (30, 8, 128), (30, 8, 128), (count, 8, 128)],
        [(16, 16, 128)] * 2, coefficient, right_side, hbm_in=(0, 1), hbm_out=(1,), sems=3,
    )
    own_o = swap(own)
    x_one, x_two = trade(first, second, "gx")
    r3 = everywhere(slots)
    x_one_o, x_two_o = swap(x_one), swap(x_two)
    r3_o = swap(r3)
    first, second = call(
        functools.partial(sides_kernel, 2), [(76, 8, 128)] * 2, [], own, x_one, x_two
    )
    y_one, y_two = trade(first, second, "gy")
    y_one_o, y_two_o = swap(y_one), swap(y_two)
    w1s, w2s, w3s, w4s = (8,) + s1, (7,) + s2, (7,) + s3, (4,) + s4
    block = (2, 16, 16, 128)
    w1, w2, c1, c2, right = call(
        first_kernel, [w1s, w2s, s1, s2, block],
        [w1s, w2s, s1, s1, s1, s1, s1, s1, p2, s2, s2, s2, s2, s2],
        coefficient, right_side, middle,
        x_one, x_two, y_one, y_two, own_o, x_one_o, x_two_o, y_one_o, y_two_o,
        hbm_in=(0, 1, 2), hbm_out=(0, 1, 2, 3, 4), sems=9, limit=28,
    )
    flat = (count * 8, 128)
    w3, w4, x1, own_kept, own, first, second, slots = call(
        functools.partial(join_first_kernel, gx_n, gy_n),
        [w3s, w4s, s1, (2, 36, 8, 128), (2, 36, 8, 128), (15, 8, 128), (15, 8, 128),
         (count, 4, 128)],
        [sum3, w3s, w4s, p3, s3, s3, s3, s3, s3, s4, w1s, block, s1, s2] + tmps,
        r3, r3_o, r3.reshape(flat), r3_o.reshape(flat), w1, right, c1, c2,
        hbm_in=(4, 5, 6, 7), hbm_out=(0, 1, 2, 3), sems=8, limit=28,
    )
    x_one, x_two = trade(first, second, "gx")
    r3 = everywhere(slots)
    x_one_o, x_two_o = swap(x_one), swap(x_two)
    r3_o = swap(r3)
    first, second = call(
        functools.partial(sides_kernel, 1), [(38, 8, 128)] * 2, [], own, x_one, x_two
    )
    y_one, y_two = trade(first, second, "gy")
    y_one_o, y_two_o = swap(y_one), swap(y_two)
    flat = (count * 4, 128)
    (c3,) = call(
        functools.partial(coarse_second_kernel, gx_n, gy_n),
        [sum3], [w3s, w4s, s3, s3, s3, s3, s3, s4],
        r3, r3_o, r3.reshape(flat), r3_o.reshape(flat), w3, w4,
        hbm_in=(4, 5), sems=2, limit=12,
    )
    solution_field, residual = call(
        second_kernel, [(16, 16, 128)] * 2,
        [w1s, w2s, s1, (2, 16, 16, 128), (2, 36, 8, 128), s1, s1, s1, s1, s1, s2, s2, s2, s2, s2]
        + tmps,
        own_kept, w1, w2, x1, right,
        x_one, x_two, y_one, y_two, x_one_o, x_two_o, y_one_o, y_two_o, c3,
        hbm_in=(0, 1, 2, 3, 4), hbm_out=(0, 1), sems=7, limit=28,
    )
    return solution_field, residual


def solution(mesh):
    placed = P("gx", "gy", "grp")

    return jax.shard_map(
        on_device, mesh=mesh, in_specs=(placed, placed), out_specs=(placed, placed),
        check_vma=False,
    )
```

```python
import functools

import jax
import jax.numpy as jnp
from jax import lax
from jax.experimental import pallas as pl
from jax.experimental.pallas import tpu as pltpu
from jax.sharding import PartitionSpec as P


FINE_DEGREE = 5
COARSE_DEGREE = 16
LOW_FINE = 0.2
LOW_COARSE = 0.02
HIGH_BOUND = 2.0
DAMPING = 0.5

F32 = jnp.float32
INTERPRET = False
LANES_X = {1: 1, 2: 2, 3: 4}
HELD = {1: (1, 27), 2: (0, 10), 3: (0, 5)}
STEPS = {
    1: ((2, 26), (3, 25), (4, 24), (5, 23)),
    2: ((1, 9), (1, 9), (2, 8), (2, 8)),
    3: ((1, 4),) * 4,
}
CHUNK = {1: 2, 2: 2, 3: 3}
PAD = {1: 0, 2: 1, 3: 1}
UNROLL = 6
SCALE = {1: 1.0, 2: 0.25, 3: 0.0625, 4: 0.015625}


def cheb_steps(degree, low, high):
    theta = (high + low) / 2.0
    delta = (high - low) / 2.0
    sigma = theta / delta
    rho = 1.0 / sigma
    keeps = []
    pushes = []
    for _ in range(degree - 1):
        rho_new = 1.0 / (2.0 * sigma - rho)
        keeps.append(rho_new * rho)
        pushes.append(2.0 * rho_new / delta)
        rho = rho_new
    return (1.0 / theta, keeps, pushes)


def roll(x, shift, axis):
    size = x.shape[axis]
    return pltpu.roll(x, shift % size, axis)


def lane_iota(shape):
    return lax.broadcasted_iota(jnp.int32, shape, len(shape) - 1)


def dot(x, m):
    high = x.astype(jnp.bfloat16)
    rest = x - high.astype(F32)
    mid = rest.astype(jnp.bfloat16)
    low = (rest - mid.astype(F32)).astype(jnp.bfloat16)
    m = m.astype(jnp.bfloat16)
    mul = lambda v: jnp.dot(v, m, preferred_element_type=F32)
    return mul(high) + (mul(mid) + mul(low))


def select_matrix(fn, value):
    row = lax.broadcasted_iota(jnp.int32, (128, 128), 0)
    col = lax.broadcasted_iota(jnp.int32, (128, 128), 1)
    return jnp.where(fn(row, col), value, 0.0).astype(F32)


def neighbours(q, v):
    zz = 128 // q
    mid = v[:, 1:-1]
    lane = lane_iota(mid.shape)
    if q == 1:
        x_up, x_dn = v[:, 2:], v[:, :-2]
        for_up = for_dn = mid
    else:
        ups = roll(v[:, 1:], -zz, 3)
        dns = roll(v[:, :-1], zz, 3)
        x_up = jnp.where(lane < 128 - zz, ups[:, :-1], ups[:, 1:])
        x_dn = jnp.where(lane >= zz, dns[:, 1:], dns[:, :-1])
        for_up, for_dn = dns[:, 1:], ups[:, :-1]
    other = lambda w: jnp.concatenate([w[1:], w[:1]], axis=0)
    inner = lane % zz
    z_up = roll(jnp.where(inner == 0, other(for_up), mid), -1, 3)
    z_dn = roll(jnp.where(inner == zz - 1, other(for_dn), mid), 1, 3)
    return mid, (x_up, x_dn, roll(mid, -1, 2), roll(mid, 1, 2), z_up, z_dn)


def blocks(start, stop, step, body):
    count = (stop - start) // step
    turns = count // UNROLL if count > UNROLL else 0

    def run(n, _):
        for k in range(UNROLL):
            body(start + (n * UNROLL + k) * step)
        return 0

    if turns:
        lax.fori_loop(0, turns, run, 0)
    for k in range(turns * UNROLL, count):
        body(start + k * step)


def faces(level, a, weights, inv, diag_ref):
    q, pad = LANES_X[level], PAD[level]
    zz = 128 // q
    first, last = HELD[level]
    step = 5 if level == 3 else 2

    def body(i):
        mid, near = neighbours(q, a[:, pl.ds(i + pad - 1, step + 2)])
        core = lax.broadcasted_iota(jnp.int32, mid.shape, 0)
        lane = lane_iota(mid.shape) % zz
        top = (core == 1) & (lane == zz - 1)
        bottom = (core == 0) & (lane == 0)
        x_up, x_dn, y_up, y_dn, z_up, z_dn = near
        z_up = jnp.where(top, 0.0, z_up)
        z_dn = jnp.where(bottom, 0.0, z_dn)
        near = (x_up, x_dn, y_up, y_dn, z_up, z_dn)
        total = 3.0 * mid + 0.5 * ((x_up + x_dn) + (y_up + y_dn) + (z_up + z_dn))
        inverse = jnp.where(mid > 0.0, 1.0 / total, 0.0)
        at = pl.ds(i, step)
        inv[:, at] = inverse
        half = 0.5 * inverse
        for k in range(6):
            w = half * (mid + near[k])
            if k == 4:
                w = jnp.where(top, 0.0, w)
            if k == 5:
                w = jnp.where(bottom, 0.0, w)
            weights[k][:, at] = w
        if diag_ref is not None:
            diag_ref[:, at] = total

    blocks(first, last, step, body)


def weighted(q, i, step, v, weights):
    mid, near = neighbours(q, v[:, pl.ds(i - 1, step + 2)])
    at = pl.ds(i, step)
    terms = [weights[k][:, at] * near[k] for k in range(6)]
    return mid, (terms[0] + terms[1]) + (terms[2] + terms[3]) + (terms[4] + terms[5])


def smooth(level, b, weights, inv, e, d, other, x):
    q = LANES_X[level]
    first, keeps, pushes = cheb_steps(FINE_DEGREE, LOW_FINE, HIGH_BOUND)
    step = CHUNK[level]

    def start(i):
        at = pl.ds(i, 5 if level == 3 else 2)
        ev = b[:, at] * inv[:, at] * (1.0 / SCALE[level])
        e[:, at] = ev
        d[:, at] = ev * first
        x[:, at] = ev * first

    blocks(*HELD[level], 5 if level == 3 else 2, start)
    if level > 1:
        for i in (HELD[level][0], HELD[level][1] - 1):
            other[:, i] = jnp.zeros_like(other[:, i])
    for n in range(FINE_DEGREE - 1):
        src, dst = (d, other) if n % 2 == 0 else (other, d)

        def body(i):
            at = pl.ds(i, step)
            mid, near = weighted(q, i, step, src, weights)
            ev = (e[:, at] - mid) + near
            new = keeps[n] * mid + pushes[n] * ev
            x[:, at] = x[:, at] + new
            if n < FINE_DEGREE - 2:
                e[:, at] = ev
                dst[:, at] = new

        blocks(*STEPS[level][n], step, body)


def x_up4(v):
    moved = roll(v, -32, 2)
    after = jnp.concatenate([moved[1:], moved[:1]], axis=0)
    return jnp.where(lane_iota(v.shape) < 96, moved, after)


def x_dn4(v):
    moved = roll(v, 32, 2)
    before = jnp.concatenate([moved[-1:], moved[:-1]], axis=0)
    return jnp.where(lane_iota(v.shape) >= 32, moved, before)


def faces4(a, fx, fy, fz, inv):
    nb, rows, _ = a.shape
    blk = lax.broadcasted_iota(jnp.int32, a.shape, 0)
    row = lax.broadcasted_iota(jnp.int32, a.shape, 1)
    lane = lane_iota(a.shape)
    half = 0.5 * a
    total = jnp.zeros_like(a)
    for up, dn, last, start, out in (
        (x_up4, x_dn4, (blk == nb - 1) & (lane >= 96), (blk == 0) & (lane < 32), fx),
        (lambda v: roll(v, -1, 1), lambda v: roll(v, 1, 1), row == rows - 1, row == 0, fy),
        (lambda v: roll(v, -1, 2), lambda v: roll(v, 1, 2), lane % 32 == 31, lane % 32 == 0, fz),
    ):
        inner = half + 0.5 * up(a)
        off = jnp.where(last, 0.0, inner)
        out[...] = off
        total = total + jnp.where(last, half, inner) + jnp.where(start, half, dn(off))
    inv[...] = 1.0 / total


def smooth4(b, fx, fy, fz, inv):
    first, keeps, pushes = cheb_steps(COARSE_DEGREE, LOW_COARSE, HIGH_BOUND)
    e = b * inv[...] * (1.0 / SCALE[4])
    x = d = e * first
    for keep, push in zip(keeps, pushes):
        gx, gy, gz = fx[...], fy[...], fz[...]
        near = gx * x_up4(d) + x_dn4(gx * d)
        near = near + gy * roll(d, -1, 1) + roll(gy * d, 1, 1)
        near = near + gz * roll(d, -1, 2) + roll(gz * d, 1, 2)
        e = e - d + inv[...] * near
        d = keep * d + push * e
        x = x + d
    return x


def build4(src, stride, offset, core, gx_n, gy_n):
    count = gx_n * gy_n * 2
    gap = stride // 2
    pairs = src[pl.ds(offset, count, stride), :] + src[pl.ds(offset + gap, count, stride), :]
    pairs = pairs.reshape(gx_n // 2, 2, gy_n * 2, 128)
    out = None
    for odd in range(2):
        mat = select_matrix(
            lambda r, c: c == odd * 64 + (r // 64) * 32 + core * 16 + (r % 32) // 2, 0.125
        )
        part = dot(pairs[:, odd].reshape(gx_n * gy_n, 128), mat)
        out = part if out is None else out + part
    return out.reshape(gx_n // 2, gy_n * 2, 128)


def window3(src, dst, field, fields, core, pos, gx_n, gy_n, pad):
    for bx in range(5):
        for by in range(6):
            ix = pos[1] + (bx - 2)
            iy = pos[2] + (by - 2)
            ok = (ix >= 0) & (ix < gx_n) & (iy >= 0) & (iy < gy_n)
            at = jnp.clip(ix, 0, gx_n - 1) * gy_n + jnp.clip(iy, 0, gy_n - 1)
            if fields == 1:
                tile = src[at]
            else:
                tile = src[at, pl.ds(field, 4, fields), :]
            dst[core, bx + pad, by * 4:by * 4 + 4, :] = jnp.where(ok, tile, 0.0)


def restrict_to2(read_pair, out):
    even = jnp.concatenate([read_pair(2 * k) for k in range(4)], axis=0)
    odd = jnp.concatenate([read_pair(2 * k + 1) for k in range(4)], axis=0)
    low = select_matrix(lambda r, c: c == r // 2, 0.125)
    high = select_matrix(lambda r, c: c == 64 + r // 2, 0.125)
    both = dot(even, low) + dot(odd, high)
    for k in range(4):
        out(k, both[k * 8:k * 8 + 8])


def restrict_to3(read_rows):
    total = None
    for k in range(4):
        mat = select_matrix(lambda r, c: c == k * 32 + (r % 64) // 2, 0.125)
        part = dot(read_rows(k), mat)
        total = part if total is None else total + part
    return total


class Copies:
    def __init__(self, sems):
        self.sems, self.made = sems, []

    def start(self, src, dst):
        copy = pltpu.make_async_copy(src, dst, self.sems.at[len(self.made)])
        copy.start()
        self.made.append(copy)
        return copy

    def finish(self):
        for copy in self.made:
            copy.wait()


def position():
    return tuple(lax.axis_index(name) for name in ("grp", "gx", "gy"))


def put_pair(even, first, second, at, up, down):
    first[at] = jnp.where(even, up, down)
    second[at] = jnp.where(even, down, up)


def is_even(index):
    return lax.rem(index, 2) == 0


def prepare_kernel(a_hbm, b_hbm, own, mid_hbm, first, second, slots, a, b, sems):
    even = is_even(position()[1])
    copies = Copies(sems)
    copies.start(a_hbm, a)
    copies.start(b_hbm, b)
    for f, src in enumerate((a, b)):
        copies.made[f].wait()

        def read_pair(k):
            total = None
            for x in (2 * k, 2 * k + 1):
                part = src[x, pl.ds(0, 8, 2), :] + src[x, pl.ds(1, 8, 2), :]
                total = part if total is None else total + part
            return total

        values = []

        def out(k, value):
            own[64 + f * 4 + k] = value
            values.append(value)

        restrict_to2(read_pair, out)
        for k in range(3):
            put_pair(even, first, second, 24 + f * 3 + k, values[k + 1], values[k])
    keep = copies.start(own.at[64:72], mid_hbm)
    for f, src in enumerate((a, b)):
        for t in range(2):
            own[pl.ds(f * 32 + t, 16, 2)] = src[:, t * 8:t * 8 + 8, :]
            put_pair(
                even, first, second, pl.ds(f * 12 + t, 6, 2),
                src[10:16, t * 8:t * 8 + 8, :], src[0:6, t * 8:t * 8 + 8, :],
            )
        slots[0, pl.ds(f, 4, 2), :] = restrict_to3(
            lambda k: own[64 + f * 4 + k, pl.ds(0, 4, 2), :] + own[64 + f * 4 + k, pl.ds(1, 4, 2), :]
        )
    slots[1:] = jnp.broadcast_to(slots[0:1], (slots.shape[0] - 1, 8, 128))
    keep.wait()


def sides_kernel(nf, own, one, two, first, second):
    core, gx, gy = position()
    even_x, even_y = is_even(gx), is_even(gy)
    if nf == 2:
        mine = lambda i: own[i]
    else:
        mine = lambda i: own[core, i]

    def lower(i):
        return jnp.where(even_x, two[i], one[i])

    def upper(i):
        return jnp.where(even_x, one[i], two[i])

    for f in range(nf):
        for i in range(28):
            if i < 6:
                low, high = lower(f * 12 + 2 * i), lower(f * 12 + 2 * i + 1)
            elif i >= 22:
                low, high = upper(f * 12 + 2 * (i - 22)), upper(f * 12 + 2 * (i - 22) + 1)
            else:
                low, high = mine(f * 32 + 2 * (i - 6)), mine(f * 32 + 2 * (i - 6) + 1)
            put_pair(even_y, first, second, f * 28 + i, high, low)
        for i in range(10):
            if i < 3:
                tile = lower(nf * 12 + f * 3 + i)
            elif i >= 7:
                tile = upper(nf * 12 + f * 3 + i - 7)
            else:
                tile = mine(nf * 32 + f * 4 + i - 3)
            first[nf * 28 + f * 10 + i] = tile
            second[nf * 28 + f * 10 + i] = tile


def spread(nf, f, core, even_x, even_y, x_one, x_two, y_one, y_two, fine, mid, pad):
    lower = lambda i: jnp.where(even_x, x_two[i], x_one[i])
    upper = lambda i: jnp.where(even_x, x_one[i], x_two[i])
    below = lambda i: jnp.where(even_y, y_two[i], y_one[i])
    above = lambda i: jnp.where(even_y, y_one[i], y_two[i])
    for i in range(28):
        fine[core, i, 0:8, :] = below(f * 28 + i)
        fine[core, i, 24:32, :] = above(f * 28 + i)
        for t in range(2):
            if i < 6:
                tile = lower(f * 12 + 2 * i + t)
            elif i >= 22:
                tile = upper(f * 12 + 2 * (i - 22) + t)
            else:
                continue
            fine[core, i, 8 + 8 * t:16 + 8 * t, :] = tile
    base = nf * 28 + f * 10
    for i in range(10):
        mid[core, i + pad, 0:8, :] = below(base + i)
        mid[core, i + pad, 16:24, :] = above(base + i)
        if i < 3:
            tile = lower(nf * 12 + f * 3 + i)
        elif i >= 7:
            tile = upper(nf * 12 + f * 3 + i - 7)
        else:
            continue
        mid[core, i + pad, 8:16, :] = tile


def spread_own(nf, f, core, own, fine, mid, pad):
    for i in range(16):
        for t in range(2):
            fine[core, i + 6, 8 + 8 * t:16 + 8 * t, :] = own[f * 32 + 2 * i + t]
    for i in range(4):
        mid[core, i + 3 + pad, 8:16, :] = own[nf * 32 + f * 4 + i]


def add_coarsest(pos, gx_n, gy_n, x4, x3, out):
    gx, gy = pos[1], pos[2]
    yrow = lax.broadcasted_iota(jnp.int32, (24, gy_n * 2), 0)
    ycol = lax.broadcasted_iota(jnp.int32, (24, gy_n * 2), 1)
    rows = jnp.where(ycol == (4 * gy - 8 + yrow + 1024) // 2 - 512, 1.0, 0.0).astype(F32)
    for bx in (1, 2, 3):
        ix = gx + (bx - 2)
        ok = (ix >= 0) & (ix < gx_n)
        at = jnp.clip(ix, 0, gx_n - 1)
        odd = lax.rem(at, 2)
        picked = select_rows(rows, x4[lax.div(at, 2)])
        for c in range(2):
            mat = select_matrix(
                lambda r, k: r == odd * 64 + (k // 64) * 32 + c * 16 + (k % 32) // 2, 1.0
            )
            out[c, bx - 1] = x3[c, bx] + jnp.where(ok, dot(picked, mat), 0.0)


def select_rows(rows, v):
    high = v.astype(jnp.bfloat16)
    rest = v - high.astype(F32)
    mid = rest.astype(jnp.bfloat16)
    low = (rest - mid.astype(F32)).astype(jnp.bfloat16)
    rows = rows.astype(jnp.bfloat16)
    mul = lambda w: jnp.dot(rows, w, preferred_element_type=F32)
    return mul(high) + (mul(mid) + mul(low))


def combine(sum3, c2, x2, tmp3, tmp2):
    for c in range(2):
        for bx in range(3):
            tmp3[c, bx, pl.ds(0, 12, 2), :] = sum3[c, bx, 4:16, :]
            tmp3[c, bx, pl.ds(1, 12, 2), :] = sum3[c, bx, 4:16, :]
    for low in range(4):
        mat = select_matrix(lambda r, k: r == low * 32 + (k % 64) // 2, 1.0)
        for i in [i for i in range(2, 8) if (i + 5) % 4 == low]:
            bx = (i + 5) // 4 - 1
            part = dot(tmp3[:, bx].reshape(48, 128), mat).reshape(2, 24, 128)
            x2[:, i - 2] = c2[:, i] + part
    for low in range(2):
        mat = select_matrix(lambda r, k: r == low * 64 + k // 2, 1.0)
        part = dot(x2[...].reshape(2 * 6 * 24, 128), mat).reshape(2, 6, 24, 128)
        for i in range(6):
            piece = part[:, i, 4:20, :]
            tmp2[:, 2 * i + low, pl.ds(0, 16, 2), :] = piece
            tmp2[:, 2 * i + low, pl.ds(1, 16, 2), :] = piece


def split3(ref):
    return [ref.at[k] for k in range(6)], ref.at[6]


def coarse_first_kernel(
    gx_n, gy_n, r3_a, r3_b, r3f_a, r3f_b, sum3, w3_hbm, w4_hbm,
    w3, w4, a3, b3, e3, d3, o3, c3, x4, sems,
):
    pos = position()
    core = pos[0]
    weights3, inv3 = split3(w3)
    fx4, fy4, fz4, inv4 = (w4.at[k] for k in range(4))
    copies = Copies(sems)
    for c in range(2):
        a3[c, 0] = jnp.zeros((24, 128), F32)
        a3[c, 6] = jnp.zeros((24, 128), F32)
    for c, src in ((core, r3_a), (1 - core, r3_b)):
        window3(src, a3, 0, 2, c, pos, gx_n, gy_n, 1)
        window3(src, b3, 1, 2, c, pos, gx_n, gy_n, 0)
    a4 = build4(r3f_a, 4, 0, core, gx_n, gy_n) + build4(r3f_b, 4, 0, 1 - core, gx_n, gy_n)
    b4 = build4(r3f_a, 4, 1, core, gx_n, gy_n) + build4(r3f_b, 4, 1, 1 - core, gx_n, gy_n)
    faces4(a4, fx4, fy4, fz4, inv4)
    copies.start(w4, w4_hbm)
    faces(3, a3, weights3, inv3, None)
    copies.start(w3, w3_hbm)
    x4[...] = smooth4(b4, fx4, fy4, fz4, inv4)
    smooth(3, b3, weights3, inv3, e3, d3, o3, c3)
    add_coarsest(pos, gx_n, gy_n, x4, c3, sum3)
    copies.finish()


def coarse_second_kernel(
    gx_n, gy_n, r3_a, r3_b, r3f_a, r3f_b, w3_hbm, w4_hbm, sum3,
    w3, w4, b3, e3, d3, o3, c3, x4, sems,
):
    pos = position()
    core = pos[0]
    copies = Copies(sems)
    copies.start(w4_hbm, w4)
    copies.start(w3_hbm, w3)
    weights3, inv3 = split3(w3)
    window3(r3_a, b3, 0, 1, core, pos, gx_n, gy_n, 0)
    window3(r3_b, b3, 0, 1, 1 - core, pos, gx_n, gy_n, 0)
    b4 = build4(r3f_a, 2, 0, core, gx_n, gy_n) + build4(r3f_b, 2, 0, 1 - core, gx_n, gy_n)
    copies.made[0].wait()
    x4[...] = smooth4(b4, *(w4.at[k] for k in range(4)))
    copies.made[1].wait()
    smooth(3, b3, weights3, inv3, e3, d3, o3, c3)
    add_coarsest(pos, gx_n, gy_n, x4, c3, sum3)


def first_kernel(
    a_hbm, b_hbm, mid_hbm,
    x_one_a, x_two_a, y_one_a, y_two_a, own_b, x_one_b, x_two_b, y_one_b, y_two_b,
    w1_hbm, w2_hbm, c1_hbm, c2_hbm, right_hbm,
    w1, w2, c1, a1, b1, e1, d1, o1, a2, b2, e2, d2, o2, c2, sems,
):
    core, gx, gy = position()
    even_x, even_y = is_even(gx), is_even(gy)
    copies = Copies(sems)
    copies.start(a_hbm, a1.at[core, 6:22, 8:24, :])
    copies.start(b_hbm, b1.at[core, 6:22, 8:24, :])
    copies.start(mid_hbm.at[0:4], a2.at[core, 4:8, 8:16, :])
    copies.start(mid_hbm.at[4:8], b2.at[core, 3:7, 8:16, :])
    halves = (
        (core, (x_one_a, x_two_a, y_one_a, y_two_a)),
        (1 - core, (x_one_b, x_two_b, y_one_b, y_two_b)),
    )
    weights1, inv1 = split3(w1)
    diag1 = w1.at[7]
    weights2, inv2 = split3(w2)
    for c in range(2):
        a2[c, 0] = jnp.zeros((24, 128), F32)
        a2[c, 11] = jnp.zeros((24, 128), F32)
    for c, parts in halves:
        spread(2, 0, c, even_x, even_y, *parts, a1, a2, 1)
        spread(2, 1, c, even_x, even_y, *parts, b1, b2, 0)
    spread_own(2, 0, 1 - core, own_b, a1, a2, 1)
    spread_own(2, 1, 1 - core, own_b, b1, b2, 0)
    copies.finish()
    out = Copies(sems.at[pl.ds(4, 5)])
    out.start(b1.at[:, 6:22, 8:24, :], right_hbm)
    faces(2, a2, weights2, inv2, None)
    out.start(w2, w2_hbm)
    faces(1, a1, weights1, inv1, diag1)
    out.start(w1, w1_hbm)
    smooth(2, b2, weights2, inv2, e2, d2, o2, c2)
    out.start(c2, c2_hbm)
    smooth(1, b1, weights1, inv1, e1, d1, o1, c1)
    out.start(c1.at[:, 5:23], c1_hbm.at[:, 5:23])
    out.finish()


def join_first_kernel(
    gx_n, gy_n, r3_a, r3_b, r3f_a, r3f_b, w1_hbm, right_hbm, c1_hbm, c2_hbm,
    w3_hbm, w4_hbm, x1_hbm, own_hbm, own, first, second, slots,
    sum3, w3, w4, a3, b3, e3, d3, o3, c3, x4, w1, right, x1, c2, s2, tmp3, tmp2, rest, sems,
):
    core, gx, _ = position()
    even_x = is_even(gx)
    weights1, diag1 = split3(w1)[0], w1.at[7]
    copies = Copies(sems.at[pl.ds(2, 4)])
    copies.start(c2_hbm, c2)
    copies.start(c1_hbm.at[:, 5:23], x1.at[:, 5:23])
    copies.start(w1_hbm.at[:, :, 6:22], w1.at[:, :, 6:22])
    copies.start(right_hbm, right)
    coarse_first_kernel(
        gx_n, gy_n, r3_a, r3_b, r3f_a, r3f_b, sum3, w3_hbm, w4_hbm,
        w3, w4, a3, b3, e3, d3, o3, c3, x4, sems.at[pl.ds(0, 2)],
    )
    copies.made[0].wait()
    combine(sum3, c2, s2, tmp3, tmp2)
    copies.made[1].wait()

    def finish(i):
        x1[:, i] = DAMPING * (x1[:, i] + tmp2[:, i // 2 - 1])

    blocks(5, 23, 1, finish)
    out = Copies(sems.at[pl.ds(6, 2)])
    out.start(x1, x1_hbm)
    copies.made[2].wait()
    copies.made[3].wait()

    def residual(i):
        mid, near = weighted(1, i, 2, x1, weights1)
        res = diag1[:, pl.ds(i, 2)] * (mid - near)
        at = pl.ds(i - 6, 2)
        rest[:, at] = right[:, at] - res[:, :, 8:24, :]

    blocks(6, 22, 2, residual)
    for c in range(2):
        for t in range(2):
            own[c, pl.ds(t, 16, 2)] = rest[c, :, t * 8:t * 8 + 8, :]

        def read_pair(k):
            total = None
            for x in (2 * k, 2 * k + 1):
                part = rest[c, x, pl.ds(0, 8, 2), :] + rest[c, x, pl.ds(1, 8, 2), :]
                total = part if total is None else total + part
            return total

        def put(k, value):
            own[c, 32 + k] = value

        restrict_to2(read_pair, put)
    out.start(own, own_hbm)
    for i in range(12):
        put_pair(even_x, first, second, i, own[core, 20 + i], own[core, i])
    for i in range(3):
        put_pair(even_x, first, second, 12 + i, own[core, 33 + i], own[core, 32 + i])
    slots[0] = restrict_to3(
        lambda k: own[core, 32 + k, pl.ds(0, 4, 2), :] + own[core, 32 + k, pl.ds(1, 4, 2), :]
    )
    slots[1:] = jnp.broadcast_to(slots[0:1], (slots.shape[0] - 1, 4, 128))
    out.finish()


def second_kernel(
    own_hbm, w1_hbm, w2_hbm, x1_hbm, right_hbm,
    x_one_a, x_two_a, y_one_a, y_two_a, x_one_b, x_two_b, y_one_b, y_two_b, sum3,
    out_x, out_r,
    w1, w2, x1, right, own, b1, e1, d1, o1, c1, b2, e2, d2, o2, c2, s2, tmp3, tmp2, rest, sems,
):
    core, gx, gy = position()
    even_x, even_y = is_even(gx), is_even(gy)
    copies = Copies(sems)
    for src, dst in (
        (own_hbm, own), (w2_hbm, w2), (w1_hbm, w1), (x1_hbm, x1), (right_hbm, right)
    ):
        copies.start(src, dst)
    weights1, inv1 = split3(w1)
    diag1 = w1.at[7]
    weights2, inv2 = split3(w2)
    spread(1, 0, core, even_x, even_y, x_one_a, x_two_a, y_one_a, y_two_a, b1, b2, 0)
    spread(1, 0, 1 - core, even_x, even_y, x_one_b, x_two_b, y_one_b, y_two_b, b1, b2, 0)
    copies.made[0].wait()
    for c in range(2):
        spread_own(1, 0, c, own.at[c], b1, b2, 0)
    copies.made[1].wait()
    smooth(2, b2, weights2, inv2, e2, d2, o2, c2)
    copies.made[2].wait()
    smooth(1, b1, weights1, inv1, e1, d1, o1, c1)
    copies.made[3].wait()
    copies.made[4].wait()
    combine(sum3, c2, s2, tmp3, tmp2)

    def finish(i):
        c1[:, i] = x1[:, i] + DAMPING * (c1[:, i] + tmp2[:, i // 2 - 1])

    blocks(5, 23, 1, finish)
    field = copies.start(c1.at[core, 6:22, 8:24, :], out_x)

    def residual(i):
        mid, near = weighted(1, i, 2, c1, weights1)
        res = diag1[:, pl.ds(i, 2)] * (mid - near)
        at = pl.ds(i - 6, 2)
        rest[:, at] = right[:, at] - res[:, :, 8:24, :]

    blocks(6, 22, 2, residual)
    done = copies.start(rest.at[core], out_r)
    field.wait()
    done.wait()


def call(kernel, outs, scratch, *args, hbm_in=(), hbm_out=(), sems=0, limit=8):
    vmem = pl.BlockSpec(memory_space=pltpu.VMEM)
    hbm = pl.BlockSpec(memory_space=pltpu.HBM)
    specs = [vmem for _ in args]
    args = list(args)
    for i in hbm_in:
        specs[i] = hbm
        args[i] = pltpu.with_memory_space_constraint(args[i], pltpu.HBM)
    scratch = [pltpu.VMEM(s, F32) for s in scratch]
    if sems:
        scratch.append(pltpu.SemaphoreType.DMA((sems,)))
    return pl.pallas_call(
        kernel,
        out_shape=[
            pltpu.HBM(s, F32) if i in hbm_out else jax.ShapeDtypeStruct(s, F32)
            for i, s in enumerate(outs)
        ],
        in_specs=specs,
        out_specs=[hbm if i in hbm_out else vmem for i in range(len(outs))],
        scratch_shapes=scratch,
        compiler_params=pltpu.CompilerParams(vmem_limit_bytes=limit * 1024 * 1024),
        interpret=INTERPRET,
    )(*args)


def trade(first, second, axis):
    size = lax.axis_size(axis)
    pairs = [(i, i ^ 1) for i in range(size)]
    others = [(i, i - 1 if i % 2 == 0 else i + 1) for i in range(1, size - 1)]
    one = lax.ppermute(first, axis, pairs)
    two = lax.ppermute(second, axis, others)
    return one, two


def swap(x):
    return lax.ppermute(x, "grp", [(0, 1), (1, 0)])


def everywhere(slots):
    return lax.all_to_all(slots, ("gx", "gy"), 0, 0, tiled=True)


def on_device(right_side, coefficient):
    gx_n, gy_n = lax.axis_size("gx"), lax.axis_size("gy")
    count = gx_n * gy_n
    s1, s2, s3 = (2, 28, 32, 128), (2, 10, 24, 128), (2, 5, 24, 128)
    p2, p3 = (2, 12, 24, 128), (2, 7, 24, 128)
    s4 = (gx_n // 2, gy_n * 2, 128)
    sum3 = (2, 3, 24, 128)
    tmps = [(2, 6, 24, 128), sum3, (2, 12, 32, 128), (2, 16, 16, 128)]

    own, middle, first, second, slots = call(
        prepare_kernel,
        [(72, 8, 128), (8, 8, 128), (30, 8, 128), (30, 8, 128), (count, 8, 128)],
        [(16, 16, 128)] * 2, coefficient, right_side, hbm_in=(0, 1), hbm_out=(1,), sems=3,
    )
    own_o = swap(own)
    x_one, x_two = trade(first, second, "gx")
    r3 = everywhere(slots)
    x_one_o, x_two_o = swap(x_one), swap(x_two)
    r3_o = swap(r3)
    first, second = call(
        functools.partial(sides_kernel, 2), [(76, 8, 128)] * 2, [], own, x_one, x_two
    )
    y_one, y_two = trade(first, second, "gy")
    y_one_o, y_two_o = swap(y_one), swap(y_two)
    w1s, w2s, w3s, w4s = (8,) + s1, (7,) + s2, (7,) + s3, (4,) + s4
    block = (2, 16, 16, 128)
    w1, w2, c1, c2, right = call(
        first_kernel, [w1s, w2s, s1, s2, block],
        [w1s, w2s, s1, s1, s1, s1, s1, s1, p2, s2, s2, s2, s2, s2],
        coefficient, right_side, middle,
        x_one, x_two, y_one, y_two, own_o, x_one_o, x_two_o, y_one_o, y_two_o,
        hbm_in=(0, 1, 2), hbm_out=(0, 1, 2, 3, 4), sems=9, limit=28,
    )
    flat = (count * 8, 128)
    w3, w4, x1, own_kept, own, first, second, slots = call(
        functools.partial(join_first_kernel, gx_n, gy_n),
        [w3s, w4s, s1, (2, 36, 8, 128), (2, 36, 8, 128), (15, 8, 128), (15, 8, 128),
         (count, 4, 128)],
        [sum3, w3s, w4s, p3, s3, s3, s3, s3, s3, s4, w1s, block, s1, s2] + tmps,
        r3, r3_o, r3.reshape(flat), r3_o.reshape(flat), w1, right, c1, c2,
        hbm_in=(4, 5, 6, 7), hbm_out=(0, 1, 2, 3), sems=8, limit=28,
    )
    x_one, x_two = trade(first, second, "gx")
    r3 = everywhere(slots)
    x_one_o, x_two_o = swap(x_one), swap(x_two)
    r3_o = swap(r3)
    first, second = call(
        functools.partial(sides_kernel, 1), [(38, 8, 128)] * 2, [], own, x_one, x_two
    )
    y_one, y_two = trade(first, second, "gy")
    y_one_o, y_two_o = swap(y_one), swap(y_two)
    flat = (count * 4, 128)
    (c3,) = call(
        functools.partial(coarse_second_kernel, gx_n, gy_n),
        [sum3], [w3s, w4s, s3, s3, s3, s3, s3, s4],
        r3, r3_o, r3.reshape(flat), r3_o.reshape(flat), w3, w4,
        hbm_in=(4, 5), sems=2, limit=12,
    )
    solution_field, residual = call(
        second_kernel, [(16, 16, 128)] * 2,
        [w1s, w2s, s1, (2, 16, 16, 128), (2, 36, 8, 128), s1, s1, s1, s1, s1, s2, s2, s2, s2, s2]
        + tmps,
        own_kept, w1, w2, x1, right,
        x_one, x_two, y_one, y_two, x_one_o, x_two_o, y_one_o, y_two_o, c3,
        hbm_in=(0, 1, 2, 3, 4), hbm_out=(0, 1), sems=7, limit=28,
    )
    return solution_field, residual


def solution(mesh):
    placed = P("gx", "gy", "grp")

    return jax.shard_map(
        on_device, mesh=mesh, in_specs=(placed, placed), out_specs=(placed, placed),
        check_vma=False,
    )
```

```python
import functools

import jax
import jax.numpy as jnp
from jax import lax
from jax.experimental import pallas as pl
from jax.experimental.pallas import tpu as pltpu
from jax.sharding import PartitionSpec as P


FINE_DEGREE = 5
COARSE_DEGREE = 16
LOW_FINE = 0.2
LOW_COARSE = 0.02
HIGH_BOUND = 2.0
DAMPING = 0.5

F32 = jnp.float32
INTERPRET = False
LANES_X = {1: 1, 2: 2, 3: 4}
HELD = {1: (1, 27), 2: (0, 10), 3: (0, 5)}
STEPS = {
    1: ((2, 26), (3, 25), (4, 24), (5, 23)),
    2: ((1, 9), (1, 9), (2, 8), (2, 8)),
    3: ((1, 4),) * 4,
}
CHUNK = {1: 2, 2: 2, 3: 3}
PAD = {1: 0, 2: 1, 3: 1}
UNROLL = 6
SCALE = {1: 1.0, 2: 0.25, 3: 0.0625, 4: 0.015625}


def cheb_steps(degree, low, high):
    theta = (high + low) / 2.0
    delta = (high - low) / 2.0
    sigma = theta / delta
    rho = 1.0 / sigma
    keeps = []
    pushes = []
    for _ in range(degree - 1):
        rho_new = 1.0 / (2.0 * sigma - rho)
        keeps.append(rho_new * rho)
        pushes.append(2.0 * rho_new / delta)
        rho = rho_new
    return (1.0 / theta, keeps, pushes)


def roll(x, shift, axis):
    size = x.shape[axis]
    return pltpu.roll(x, shift % size, axis)


def lane_iota(shape):
    return lax.broadcasted_iota(jnp.int32, shape, len(shape) - 1)


def dot(x, m):
    high = x.astype(jnp.bfloat16)
    rest = x - high.astype(F32)
    mid = rest.astype(jnp.bfloat16)
    low = (rest - mid.astype(F32)).astype(jnp.bfloat16)
    m = m.astype(jnp.bfloat16)
    mul = lambda v: jnp.dot(v, m, preferred_element_type=F32)
    return mul(high) + (mul(mid) + mul(low))


def select_matrix(fn, value):
    row = lax.broadcasted_iota(jnp.int32, (128, 128), 0)
    col = lax.broadcasted_iota(jnp.int32, (128, 128), 1)
    return jnp.where(fn(row, col), value, 0.0).astype(F32)


def neighbours(q, v):
    zz = 128 // q
    mid = v[:, 1:-1]
    lane = lane_iota(mid.shape)
    if q == 1:
        x_up, x_dn = v[:, 2:], v[:, :-2]
        for_up = for_dn = mid
    else:
        ups = roll(v[:, 1:], -zz, 3)
        dns = roll(v[:, :-1], zz, 3)
        x_up = jnp.where(lane < 128 - zz, ups[:, :-1], ups[:, 1:])
        x_dn = jnp.where(lane >= zz, dns[:, 1:], dns[:, :-1])
        for_up, for_dn = dns[:, 1:], ups[:, :-1]
    other = lambda w: jnp.concatenate([w[1:], w[:1]], axis=0)
    inner = lane % zz
    z_up = roll(jnp.where(inner == 0, other(for_up), mid), -1, 3)
    z_dn = roll(jnp.where(inner == zz - 1, other(for_dn), mid), 1, 3)
    return mid, (x_up, x_dn, roll(mid, -1, 2), roll(mid, 1, 2), z_up, z_dn)


def blocks(start, stop, step, body):
    count = (stop - start) // step
    turns = count // UNROLL if count > UNROLL else 0

    def run(n, _):
        for k in range(UNROLL):
            body(start + (n * UNROLL + k) * step)
        return 0

    if turns:
        lax.fori_loop(0, turns, run, 0)
    for k in range(turns * UNROLL, count):
        body(start + k * step)


def faces(level, a, weights, inv, diag_ref):
    q, pad = LANES_X[level], PAD[level]
    zz = 128 // q
    first, last = HELD[level]
    step = 5 if level == 3 else 2

    def body(i):
        mid, near = neighbours(q, a[:, pl.ds(i + pad - 1, step + 2)])
        core = lax.broadcasted_iota(jnp.int32, mid.shape, 0)
        lane = lane_iota(mid.shape) % zz
        top = (core == 1) & (lane == zz - 1)
        bottom = (core == 0) & (lane == 0)
        x_up, x_dn, y_up, y_dn, z_up, z_dn = near
        z_up = jnp.where(top, 0.0, z_up)
        z_dn = jnp.where(bottom, 0.0, z_dn)
        near = (x_up, x_dn, y_up, y_dn, z_up, z_dn)
        total = 3.0 * mid + 0.5 * ((x_up + x_dn) + (y_up + y_dn) + (z_up + z_dn))
        inverse = jnp.where(mid > 0.0, 1.0 / total, 0.0)
        at = pl.ds(i, step)
        inv[:, at] = inverse
        half = 0.5 * inverse
        for k in range(6):
            w = half * (mid + near[k])
            if k == 4:
                w = jnp.where(top, 0.0, w)
            if k == 5:
                w = jnp.where(bottom, 0.0, w)
            weights[k][:, at] = w
        if diag_ref is not None:
            diag_ref[:, at] = total

    blocks(first, last, step, body)


def weighted(q, i, step, v, weights):
    mid, near = neighbours(q, v[:, pl.ds(i - 1, step + 2)])
    at = pl.ds(i, step)
    terms = [weights[k][:, at] * near[k] for k in range(6)]
    return mid, (terms[0] + terms[1]) + (terms[2] + terms[3]) + (terms[4] + terms[5])


def smooth(level, b, weights, inv, e, d, other, x):
    q = LANES_X[level]
    first, keeps, pushes = cheb_steps(FINE_DEGREE, LOW_FINE, HIGH_BOUND)
    step = CHUNK[level]

    def start(i):
        at = pl.ds(i, 5 if level == 3 else 2)
        ev = b[:, at] * inv[:, at] * (1.0 / SCALE[level])
        e[:, at] = ev
        d[:, at] = ev * first
        x[:, at] = ev * first

    blocks(*HELD[level], 5 if level == 3 else 2, start)
    if level > 1:
        for i in (HELD[level][0], HELD[level][1] - 1):
            other[:, i] = jnp.zeros_like(other[:, i])
    for n in range(FINE_DEGREE - 1):
        src, dst = (d, other) if n % 2 == 0 else (other, d)

        def body(i):
            at = pl.ds(i, step)
            mid, near = weighted(q, i, step, src, weights)
            ev = (e[:, at] - mid) + near
            new = keeps[n] * mid + pushes[n] * ev
            x[:, at] = x[:, at] + new
            if n < FINE_DEGREE - 2:
                e[:, at] = ev
                dst[:, at] = new

        blocks(*STEPS[level][n], step, body)


def x_up4(v):
    moved = roll(v, -32, 2)
    after = jnp.concatenate([moved[1:], moved[:1]], axis=0)
    return jnp.where(lane_iota(v.shape) < 96, moved, after)


def x_dn4(v):
    moved = roll(v, 32, 2)
    before = jnp.concatenate([moved[-1:], moved[:-1]], axis=0)
    return jnp.where(lane_iota(v.shape) >= 32, moved, before)


def faces4(a, fx, fy, fz, inv):
    nb, rows, _ = a.shape
    blk = lax.broadcasted_iota(jnp.int32, a.shape, 0)
    row = lax.broadcasted_iota(jnp.int32, a.shape, 1)
    lane = lane_iota(a.shape)
    half = 0.5 * a
    total = jnp.zeros_like(a)
    for up, dn, last, start, out in (
        (x_up4, x_dn4, (blk == nb - 1) & (lane >= 96), (blk == 0) & (lane < 32), fx),
        (lambda v: roll(v, -1, 1), lambda v: roll(v, 1, 1), row == rows - 1, row == 0, fy),
        (lambda v: roll(v, -1, 2), lambda v: roll(v, 1, 2), lane % 32 == 31, lane % 32 == 0, fz),
    ):
        inner = half + 0.5 * up(a)
        off = jnp.where(last, 0.0, inner)
        out[...] = off
        total = total + jnp.where(last, half, inner) + jnp.where(start, half, dn(off))
    inv[...] = 1.0 / total


def smooth4(b, fx, fy, fz, inv):
    first, keeps, pushes = cheb_steps(COARSE_DEGREE, LOW_COARSE, HIGH_BOUND)
    e = b * inv[...] * (1.0 / SCALE[4])
    x = d = e * first
    for keep, push in zip(keeps, pushes):
        gx, gy, gz = fx[...], fy[...], fz[...]
        near = gx * x_up4(d) + x_dn4(gx * d)
        near = near + gy * roll(d, -1, 1) + roll(gy * d, 1, 1)
        near = near + gz * roll(d, -1, 2) + roll(gz * d, 1, 2)
        e = e - d + inv[...] * near
        d = keep * d + push * e
        x = x + d
    return x


def build4(src, stride, offset, core, gx_n, gy_n):
    count = gx_n * gy_n * 2
    gap = stride // 2
    pairs = src[pl.ds(offset, count, stride), :] + src[pl.ds(offset + gap, count, stride), :]
    pairs = pairs.reshape(gx_n // 2, 2, gy_n * 2, 128)
    out = None
    for odd in range(2):
        mat = select_matrix(
            lambda r, c: c == odd * 64 + (r // 64) * 32 + core * 16 + (r % 32) // 2, 0.125
        )
        part = dot(pairs[:, odd].reshape(gx_n * gy_n, 128), mat)
        out = part if out is None else out + part
    return out.reshape(gx_n // 2, gy_n * 2, 128)


def window3(src, dst, field, fields, core, pos, gx_n, gy_n, pad):
    for bx in range(5):
        for by in range(6):
            ix = pos[1] + (bx - 2)
            iy = pos[2] + (by - 2)
            ok = (ix >= 0) & (ix < gx_n) & (iy >= 0) & (iy < gy_n)
            at = jnp.clip(ix, 0, gx_n - 1) * gy_n + jnp.clip(iy, 0, gy_n - 1)
            if fields == 1:
                tile = src[at]
            else:
                tile = src[at, pl.ds(field, 4, fields), :]
            dst[core, bx + pad, by * 4:by * 4 + 4, :] = jnp.where(ok, tile, 0.0)


def restrict_to2(read_pair, out):
    even = jnp.concatenate([read_pair(2 * k) for k in range(4)], axis=0)
    odd = jnp.concatenate([read_pair(2 * k + 1) for k in range(4)], axis=0)
    low = select_matrix(lambda r, c: c == r // 2, 0.125)
    high = select_matrix(lambda r, c: c == 64 + r // 2, 0.125)
    both = dot(even, low) + dot(odd, high)
    for k in range(4):
        out(k, both[k * 8:k * 8 + 8])


def restrict_to3(read_rows):
    total = None
    for k in range(4):
        mat = select_matrix(lambda r, c: c == k * 32 + (r % 64) // 2, 0.125)
        part = dot(read_rows(k), mat)
        total = part if total is None else total + part
    return total


class Copies:
    def __init__(self, sems):
        self.sems, self.made = sems, []

    def start(self, src, dst):
        copy = pltpu.make_async_copy(src, dst, self.sems.at[len(self.made)])
        copy.start()
        self.made.append(copy)
        return copy

    def finish(self):
        for copy in self.made:
            copy.wait()


def position():
    return tuple(lax.axis_index(name) for name in ("grp", "gx", "gy"))


def put_pair(even, first, second, at, up, down):
    first[at] = jnp.where(even, up, down)
    second[at] = jnp.where(even, down, up)


def is_even(index):
    return lax.rem(index, 2) == 0


def prepare_kernel(a_hbm, b_hbm, own, mid_hbm, first, second, slots, a, b, sems):
    even = is_even(position()[1])
    copies = Copies(sems)
    copies.start(a_hbm, a)
    copies.start(b_hbm, b)
    for f, src in enumerate((a, b)):
        copies.made[f].wait()

        def read_pair(k):
            total = None
            for x in (2 * k, 2 * k + 1):
                part = src[x, pl.ds(0, 8, 2), :] + src[x, pl.ds(1, 8, 2), :]
                total = part if total is None else total + part
            return total

        values = []

        def out(k, value):
            own[64 + f * 4 + k] = value
            values.append(value)

        restrict_to2(read_pair, out)
        for k in range(3):
            put_pair(even, first, second, 24 + f * 3 + k, values[k + 1], values[k])
    keep = copies.start(own.at[64:72], mid_hbm)
    for f, src in enumerate((a, b)):
        for t in range(2):
            own[pl.ds(f * 32 + t, 16, 2)] = src[:, t * 8:t * 8 + 8, :]
            put_pair(
                even, first, second, pl.ds(f * 12 + t, 6, 2),
                src[10:16, t * 8:t * 8 + 8, :], src[0:6, t * 8:t * 8 + 8, :],
            )
        slots[0, pl.ds(f, 4, 2), :] = restrict_to3(
            lambda k: own[64 + f * 4 + k, pl.ds(0, 4, 2), :] + own[64 + f * 4 + k, pl.ds(1, 4, 2), :]
        )
    slots[1:] = jnp.broadcast_to(slots[0:1], (slots.shape[0] - 1, 8, 128))
    keep.wait()


def sides_kernel(nf, own, one, two, first, second):
    core, gx, gy = position()
    even_x, even_y = is_even(gx), is_even(gy)
    if nf == 2:
        mine = lambda i: own[i]
    else:
        mine = lambda i: own[core, i]

    def lower(i):
        return jnp.where(even_x, two[i], one[i])

    def upper(i):
        return jnp.where(even_x, one[i], two[i])

    for f in range(nf):
        for i in range(28):
            if i < 6:
                low, high = lower(f * 12 + 2 * i), lower(f * 12 + 2 * i + 1)
            elif i >= 22:
                low, high = upper(f * 12 + 2 * (i - 22)), upper(f * 12 + 2 * (i - 22) + 1)
            else:
                low, high = mine(f * 32 + 2 * (i - 6)), mine(f * 32 + 2 * (i - 6) + 1)
            put_pair(even_y, first, second, f * 28 + i, high, low)
        for i in range(10):
            if i < 3:
                tile = lower(nf * 12 + f * 3 + i)
            elif i >= 7:
                tile = upper(nf * 12 + f * 3 + i - 7)
            else:
                tile = mine(nf * 32 + f * 4 + i - 3)
            first[nf * 28 + f * 10 + i] = tile
            second[nf * 28 + f * 10 + i] = tile


def spread(nf, f, core, even_x, even_y, x_one, x_two, y_one, y_two, fine, mid, pad):
    lower = lambda i: jnp.where(even_x, x_two[i], x_one[i])
    upper = lambda i: jnp.where(even_x, x_one[i], x_two[i])
    below = lambda i: jnp.where(even_y, y_two[i], y_one[i])
    above = lambda i: jnp.where(even_y, y_one[i], y_two[i])
    for i in range(28):
        fine[core, i, 0:8, :] = below(f * 28 + i)
        fine[core, i, 24:32, :] = above(f * 28 + i)
        for t in range(2):
            if i < 6:
                tile = lower(f * 12 + 2 * i + t)
            elif i >= 22:
                tile = upper(f * 12 + 2 * (i - 22) + t)
            else:
                continue
            fine[core, i, 8 + 8 * t:16 + 8 * t, :] = tile
    base = nf * 28 + f * 10
    for i in range(10):
        mid[core, i + pad, 0:8, :] = below(base + i)
        mid[core, i + pad, 16:24, :] = above(base + i)
        if i < 3:
            tile = lower(nf * 12 + f * 3 + i)
        elif i >= 7:
            tile = upper(nf * 12 + f * 3 + i - 7)
        else:
            continue
        mid[core, i + pad, 8:16, :] = tile


def spread_own(nf, f, core, own, fine, mid, pad):
    for i in range(16):
        for t in range(2):
            fine[core, i + 6, 8 + 8 * t:16 + 8 * t, :] = own[f * 32 + 2 * i + t]
    for i in range(4):
        mid[core, i + 3 + pad, 8:16, :] = own[nf * 32 + f * 4 + i]


def add_coarsest(pos, gx_n, gy_n, x4, x3, out):
    gx, gy = pos[1], pos[2]
    yrow = lax.broadcasted_iota(jnp.int32, (24, gy_n * 2), 0)
    ycol = lax.broadcasted_iota(jnp.int32, (24, gy_n * 2), 1)
    rows = jnp.where(ycol == (4 * gy - 8 + yrow + 1024) // 2 - 512, 1.0, 0.0).astype(F32)
    for bx in (1, 2, 3):
        ix = gx + (bx - 2)
        ok = (ix >= 0) & (ix < gx_n)
        at = jnp.clip(ix, 0, gx_n - 1)
        odd = lax.rem(at, 2)
        picked = select_rows(rows, x4[lax.div(at, 2)])
        for c in range(2):
            mat = select_matrix(
                lambda r, k: r == odd * 64 + (k // 64) * 32 + c * 16 + (k % 32) // 2, 1.0
            )
            out[c, bx - 1] = x3[c, bx] + jnp.where(ok, dot(picked, mat), 0.0)


def select_rows(rows, v):
    high = v.astype(jnp.bfloat16)
    rest = v - high.astype(F32)
    mid = rest.astype(jnp.bfloat16)
    low = (rest - mid.astype(F32)).astype(jnp.bfloat16)
    rows = rows.astype(jnp.bfloat16)
    mul = lambda w: jnp.dot(rows, w, preferred_element_type=F32)
    return mul(high) + (mul(mid) + mul(low))


def combine(sum3, c2, x2, tmp3, tmp2):
    for c in range(2):
        for bx in range(3):
            tmp3[c, bx, pl.ds(0, 12, 2), :] = sum3[c, bx, 4:16, :]
            tmp3[c, bx, pl.ds(1, 12, 2), :] = sum3[c, bx, 4:16, :]
    for low in range(4):
        mat = select_matrix(lambda r, k: r == low * 32 + (k % 64) // 2, 1.0)
        for i in [i for i in range(2, 8) if (i + 5) % 4 == low]:
            bx = (i + 5) // 4 - 1
            part = dot(tmp3[:, bx].reshape(48, 128), mat).reshape(2, 24, 128)
            x2[:, i - 2] = c2[:, i] + part
    for low in range(2):
        mat = select_matrix(lambda r, k: r == low * 64 + k // 2, 1.0)
        part = dot(x2[...].reshape(2 * 6 * 24, 128), mat).reshape(2, 6, 24, 128)
        for i in range(6):
            piece = part[:, i, 4:20, :]
            tmp2[:, 2 * i + low, pl.ds(0, 16, 2), :] = piece
            tmp2[:, 2 * i + low, pl.ds(1, 16, 2), :] = piece


def split3(ref):
    return [ref.at[k] for k in range(6)], ref.at[6]


def coarse_first_kernel(
    gx_n, gy_n, r3_a, r3_b, r3f_a, r3f_b, sum3, w3_hbm, w4_hbm,
    w3, w4, a3, b3, e3, d3, o3, c3, x4, sems,
):
    pos = position()
    core = pos[0]
    weights3, inv3 = split3(w3)
    fx4, fy4, fz4, inv4 = (w4.at[k] for k in range(4))
    copies = Copies(sems)
    for c in range(2):
        a3[c, 0] = jnp.zeros((24, 128), F32)
        a3[c, 6] = jnp.zeros((24, 128), F32)
    for c, src in ((core, r3_a), (1 - core, r3_b)):
        window3(src, a3, 0, 2, c, pos, gx_n, gy_n, 1)
        window3(src, b3, 1, 2, c, pos, gx_n, gy_n, 0)
    a4 = build4(r3f_a, 4, 0, core, gx_n, gy_n) + build4(r3f_b, 4, 0, 1 - core, gx_n, gy_n)
    b4 = build4(r3f_a, 4, 1, core, gx_n, gy_n) + build4(r3f_b, 4, 1, 1 - core, gx_n, gy_n)
    faces4(a4, fx4, fy4, fz4, inv4)
    copies.start(w4, w4_hbm)
    faces(3, a3, weights3, inv3, None)
    copies.start(w3, w3_hbm)
    x4[...] = smooth4(b4, fx4, fy4, fz4, inv4)
    smooth(3, b3, weights3, inv3, e3, d3, o3, c3)
    add_coarsest(pos, gx_n, gy_n, x4, c3, sum3)
    copies.finish()


def coarse_second_kernel(
    gx_n, gy_n, r3_a, r3_b, r3f_a, r3f_b, w3_hbm, w4_hbm, sum3,
    w3, w4, b3, e3, d3, o3, c3, x4, sems,
):
    pos = position()
    core = pos[0]
    copies = Copies(sems)
    copies.start(w4_hbm, w4)
    copies.start(w3_hbm, w3)
    weights3, inv3 = split3(w3)
    window3(r3_a, b3, 0, 1, core, pos, gx_n, gy_n, 0)
    window3(r3_b, b3, 0, 1, 1 - core, pos, gx_n, gy_n, 0)
    b4 = build4(r3f_a, 2, 0, core, gx_n, gy_n) + build4(r3f_b, 2, 0, 1 - core, gx_n, gy_n)
    copies.made[0].wait()
    x4[...] = smooth4(b4, *(w4.at[k] for k in range(4)))
    copies.made[1].wait()
    smooth(3, b3, weights3, inv3, e3, d3, o3, c3)
    add_coarsest(pos, gx_n, gy_n, x4, c3, sum3)


def first_kernel(
    a_hbm, b_hbm, mid_hbm,
    x_one_a, x_two_a, y_one_a, y_two_a, own_b, x_one_b, x_two_b, y_one_b, y_two_b, sum3,
    w1_hbm, w2_hbm, x1_hbm, right_hbm, own_hbm, own, first, second, slots,
    w1, w2, x1, a1, b1, e1, d1, o1, a2, b2, e2, d2, o2, c2, s2, tmp3, tmp2, rest, sems,
):
    core, gx, gy = position()
    even_x, even_y = is_even(gx), is_even(gy)
    copies = Copies(sems)
    copies.start(a_hbm, a1.at[core, 6:22, 8:24, :])
    copies.start(b_hbm, b1.at[core, 6:22, 8:24, :])
    copies.start(mid_hbm.at[0:4], a2.at[core, 4:8, 8:16, :])
    copies.start(mid_hbm.at[4:8], b2.at[core, 3:7, 8:16, :])
    halves = (
        (core, (x_one_a, x_two_a, y_one_a, y_two_a)),
        (1 - core, (x_one_b, x_two_b, y_one_b, y_two_b)),
    )
    weights1, inv1 = split3(w1)
    diag1 = w1.at[7]
    weights2, inv2 = split3(w2)
    for c in range(2):
        a2[c, 0] = jnp.zeros((24, 128), F32)
        a2[c, 11] = jnp.zeros((24, 128), F32)
    for c, parts in halves:
        spread(2, 0, c, even_x, even_y, *parts, a1, a2, 1)
        spread(2, 1, c, even_x, even_y, *parts, b1, b2, 0)
    spread_own(2, 0, 1 - core, own_b, a1, a2, 1)
    spread_own(2, 1, 1 - core, own_b, b1, b2, 0)
    copies.finish()
    out = Copies(sems.at[pl.ds(4, 5)])
    out.start(b1.at[:, 6:22, 8:24, :], right_hbm)
    faces(2, a2, weights2, inv2, None)
    out.start(w2, w2_hbm)
    faces(1, a1, weights1, inv1, diag1)
    out.start(w1, w1_hbm)
    smooth(2, b2, weights2, inv2, e2, d2, o2, c2)
    smooth(1, b1, weights1, inv1, e1, d1, o1, x1)
    combine(sum3, c2, s2, tmp3, tmp2)

    def finish(i):
        x1[:, i] = DAMPING * (x1[:, i] + tmp2[:, i // 2 - 1])

    blocks(5, 23, 1, finish)
    out.start(x1, x1_hbm)

    def residual(i):
        mid, near = weighted(1, i, 2, x1, weights1)
        at = pl.ds(i, 2)
        res = b1[:, at] - diag1[:, at] * (mid - near)
        rest[:, pl.ds(i - 6, 2)] = res[:, :, 8:24, :]

    blocks(6, 22, 2, residual)
    for c in range(2):
        for t in range(2):
            own[c, pl.ds(t, 16, 2)] = rest[c, :, t * 8:t * 8 + 8, :]

        def read_pair(k):
            total = None
            for x in (2 * k, 2 * k + 1):
                part = rest[c, x, pl.ds(0, 8, 2), :] + rest[c, x, pl.ds(1, 8, 2), :]
                total = part if total is None else total + part
            return total

        def put(k, value):
            own[c, 32 + k] = value

        restrict_to2(read_pair, put)
    out.start(own, own_hbm)
    for i in range(12):
        put_pair(even_x, first, second, i, own[core, 20 + i], own[core, i])
    for i in range(3):
        put_pair(even_x, first, second, 12 + i, own[core, 33 + i], own[core, 32 + i])
    slots[0] = restrict_to3(
        lambda k: own[core, 32 + k, pl.ds(0, 4, 2), :] + own[core, 32 + k, pl.ds(1, 4, 2), :]
    )
    slots[1:] = jnp.broadcast_to(slots[0:1], (slots.shape[0] - 1, 4, 128))
    out.finish()


def second_kernel(
    own_hbm, w1_hbm, w2_hbm, x1_hbm, right_hbm,
    x_one_a, x_two_a, y_one_a, y_two_a, x_one_b, x_two_b, y_one_b, y_two_b, sum3,
    out_x, out_r,
    w1, w2, x1, right, own, b1, e1, d1, o1, c1, b2, e2, d2, o2, c2, s2, tmp3, tmp2, rest, sems,
):
    core, gx, gy = position()
    even_x, even_y = is_even(gx), is_even(gy)
    copies = Copies(sems)
    for src, dst in (
        (own_hbm, own), (w2_hbm, w2), (w1_hbm, w1), (x1_hbm, x1), (right_hbm, right)
    ):
        copies.start(src, dst)
    weights1, inv1 = split3(w1)
    diag1 = w1.at[7]
    weights2, inv2 = split3(w2)
    spread(1, 0, core, even_x, even_y, x_one_a, x_two_a, y_one_a, y_two_a, b1, b2, 0)
    spread(1, 0, 1 - core, even_x, even_y, x_one_b, x_two_b, y_one_b, y_two_b, b1, b2, 0)
    copies.made[0].wait()
    for c in range(2):
        spread_own(1, 0, c, own.at[c], b1, b2, 0)
    copies.made[1].wait()
    smooth(2, b2, weights2, inv2, e2, d2, o2, c2)
    copies.made[2].wait()
    smooth(1, b1, weights1, inv1, e1, d1, o1, c1)
    copies.made[3].wait()
    copies.made[4].wait()
    combine(sum3, c2, s2, tmp3, tmp2)

    def finish(i):
        c1[:, i] = x1[:, i] + DAMPING * (c1[:, i] + tmp2[:, i // 2 - 1])

    blocks(5, 23, 1, finish)
    field = copies.start(c1.at[core, 6:22, 8:24, :], out_x)

    def residual(i):
        mid, near = weighted(1, i, 2, c1, weights1)
        res = diag1[:, pl.ds(i, 2)] * (mid - near)
        at = pl.ds(i - 6, 2)
        rest[:, at] = right[:, at] - res[:, :, 8:24, :]

    blocks(6, 22, 2, residual)
    done = copies.start(rest.at[core], out_r)
    field.wait()
    done.wait()


def call(kernel, outs, scratch, *args, hbm_in=(), hbm_out=(), sems=0, limit=8):
    vmem = pl.BlockSpec(memory_space=pltpu.VMEM)
    hbm = pl.BlockSpec(memory_space=pltpu.HBM)
    specs = [vmem for _ in args]
    args = list(args)
    for i in hbm_in:
        specs[i] = hbm
        args[i] = pltpu.with_memory_space_constraint(args[i], pltpu.HBM)
    scratch = [pltpu.VMEM(s, F32) for s in scratch]
    if sems:
        scratch.append(pltpu.SemaphoreType.DMA((sems,)))
    return pl.pallas_call(
        kernel,
        out_shape=[
            pltpu.HBM(s, F32) if i in hbm_out else jax.ShapeDtypeStruct(s, F32)
            for i, s in enumerate(outs)
        ],
        in_specs=specs,
        out_specs=[hbm if i in hbm_out else vmem for i in range(len(outs))],
        scratch_shapes=scratch,
        compiler_params=pltpu.CompilerParams(vmem_limit_bytes=limit * 1024 * 1024),
        interpret=INTERPRET,
    )(*args)


def trade(first, second, axis):
    size = lax.axis_size(axis)
    pairs = [(i, i ^ 1) for i in range(size)]
    others = [(i, i - 1 if i % 2 == 0 else i + 1) for i in range(1, size - 1)]
    one = lax.ppermute(first, axis, pairs)
    two = lax.ppermute(second, axis, others)
    return one, two


def swap(x):
    return lax.ppermute(x, "grp", [(0, 1), (1, 0)])


def everywhere(slots):
    return lax.all_to_all(slots, ("gx", "gy"), 0, 0, tiled=True)


def on_device(right_side, coefficient):
    gx_n, gy_n = lax.axis_size("gx"), lax.axis_size("gy")
    count = gx_n * gy_n
    s1, s2, s3 = (2, 28, 32, 128), (2, 10, 24, 128), (2, 5, 24, 128)
    p2, p3 = (2, 12, 24, 128), (2, 7, 24, 128)
    s4 = (gx_n // 2, gy_n * 2, 128)
    sum3 = (2, 3, 24, 128)
    tmps = [(2, 6, 24, 128), sum3, (2, 12, 32, 128), (2, 16, 16, 128)]

    own, middle, first, second, slots = call(
        prepare_kernel,
        [(72, 8, 128), (8, 8, 128), (30, 8, 128), (30, 8, 128), (count, 8, 128)],
        [(16, 16, 128)] * 2, coefficient, right_side, hbm_in=(0, 1), hbm_out=(1,), sems=3,
    )
    own_o = swap(own)
    x_one, x_two = trade(first, second, "gx")
    r3 = everywhere(slots)
    x_one_o, x_two_o = swap(x_one), swap(x_two)
    r3_o = swap(r3)
    first, second = call(
        functools.partial(sides_kernel, 2), [(76, 8, 128)] * 2, [], own, x_one, x_two
    )
    y_one, y_two = trade(first, second, "gy")
    y_one_o, y_two_o = swap(y_one), swap(y_two)
    flat = (count * 8, 128)
    w1s, w2s, w3s, w4s = (8,) + s1, (7,) + s2, (7,) + s3, (4,) + s4
    c3, w3, w4 = call(
        functools.partial(coarse_first_kernel, gx_n, gy_n), [sum3, w3s, w4s],
        [w3s, w4s, p3, s3, s3, s3, s3, s3, s4],
        r3, r3_o, r3.reshape(flat), r3_o.reshape(flat), hbm_out=(1, 2), sems=2, limit=12,
    )
    w1, w2, x1, right, own_kept, own, first, second, slots = call(
        first_kernel,
        [w1s, w2s, s1, (2, 16, 16, 128), (2, 36, 8, 128), (2, 36, 8, 128), (15, 8, 128),
         (15, 8, 128), (count, 4, 128)],
        [w1s, w2s, s1, s1, s1, s1, s1, s1, p2, s2, s2, s2, s2, s2] + tmps,
        coefficient, right_side, middle,
        x_one, x_two, y_one, y_two, own_o, x_one_o, x_two_o, y_one_o, y_two_o, c3,
        hbm_in=(0, 1, 2), hbm_out=(0, 1, 2, 3, 4), sems=9, limit=28,
    )
    x_one, x_two = trade(first, second, "gx")
    r3 = everywhere(slots)
    x_one_o, x_two_o = swap(x_one), swap(x_two)
    r3_o = swap(r3)
    first, second = call(
        functools.partial(sides_kernel, 1), [(38, 8, 128)] * 2, [], own, x_one, x_two
    )
    y_one, y_two = trade(first, second, "gy")
    y_one_o, y_two_o = swap(y_one), swap(y_two)
    flat = (count * 4, 128)
    (c3,) = call(
        functools.partial(coarse_second_kernel, gx_n, gy_n),
        [sum3], [w3s, w4s, s3, s3, s3, s3, s3, s4],
        r3, r3_o, r3.reshape(flat), r3_o.reshape(flat), w3, w4,
        hbm_in=(4, 5), sems=2, limit=12,
    )
    solution_field, residual = call(
        second_kernel, [(16, 16, 128)] * 2,
        [w1s, w2s, s1, (2, 16, 16, 128), (2, 36, 8, 128), s1, s1, s1, s1, s1, s2, s2, s2, s2, s2]
        + tmps,
        own_kept, w1, w2, x1, right,
        x_one, x_two, y_one, y_two, x_one_o, x_two_o, y_one_o, y_two_o, c3,
        hbm_in=(0, 1, 2, 3, 4), hbm_out=(0, 1), sems=7, limit=28,
    )
    return solution_field, residual


def solution(mesh):
    placed = P("gx", "gy", "grp")

    return jax.shard_map(
        on_device, mesh=mesh, in_specs=(placed, placed), out_specs=(placed, placed),
        check_vma=False,
    )
```
